128 devices in a mesh: shard: 32 (over y, z, core), tensor: 4 (over x).
Axes of the slice: x: 4, y: 4, z: 4, core: 2. Of those that a mesh axis runs over, the one named last changes fastest.
Arguments:
- gradient: float32 [384, 4, 20736], P('shard', 'tensor'), may hold values from -6 to 6
- weight: float32 [384, 4, 20736], P('shard', 'tensor'), may hold values from -0.3125 to 0.3125
- first_moment: float32 [384, 4, 20736], P('shard', 'tensor'), may hold values from -6 to 6
- second_moment: float32 [384, 4, 20736], P('shard', 'tensor'), may hold values from 0.3 to 3
- left_basis: float32 [384, 4, 5760], P('shard', 'tensor')
- left_gram: float32 [384, 4, 5760], P('shard', 'tensor'), as said below
- owner_table: int32 [12, 5], replicated, may hold values from 0 to 31, as said below
- bias_gradient: float32 [69120], P(('shard', 'tensor')), may hold values from -6 to 6
- bias_weight: float32 [69120], P(('shard', 'tensor')), may hold values from -3 to 3
- bias_first: float32 [69120], P(('shard', 'tensor')), may hold values from -6 to 6
- bias_second: float32 [69120], P(('shard', 'tensor')), may hold values from 0.3 to 3
Outputs:
- new_weight: float32 [384, 4, 20736], P('shard', 'tensor')
- new_first: float32 [384, 4, 20736], P('shard', 'tensor')
- new_second: float32 [384, 4, 20736], P('shard', 'tensor')
- owned_basis: float32 [32, 2, 384, 384], P('shard', None, None, 'tensor')
- owned_gram: float32 [32, 2, 384, 384], P('shard', None, None, 'tensor')
- bias_updated: float32 [69120], P(('shard', 'tensor'))
- bias_first_new: float32 [69120], P(('shard', 'tensor'))
- bias_second_new: float32 [69120], P(('shard', 'tensor'))
The draws below stay inside these ranges and needn't reach their ends.
Inputs may be any that keep to these rules, and one draw needn't show every extreme that they name: `owner_table`: every owner group that owns a matrix owns exactly 2, with at most 8 column tiles together, and some group has exactly 8; group 0 and the last group own matrices. `left_gram`: each matrix is symmetric.
All inputs are finite; a program needn't handle non-finite values.
Results may differ from the reference program's by a relative error of at most 0.0001.
Values sent between devices are 32-bit elements; how exact they have to be, the bound alone decides.
A program may use at most 128 MiB of HBM per device.

```python
import math
import jax
import jax.numpy as jnp
from jax import lax

D = 384
LAYERS = 12
TILES = 216
MATS = 60
BIAS = 5760
MCAP = 2
STEP = 10
NS_STEPS = 5
N_SHARD = 32
N_TENSOR = 4


def relay_draw(tiles):
    count = tiles.shape[0]
    return tiles.reshape(count, D, N_TENSOR, D // N_TENSOR).transpose(1, 2, 0, 3).reshape(D, N_TENSOR, count * (D // N_TENSOR))


def draw_left_basis(key, part):
    noise = jax.random.normal(key, (MATS, D, D), jnp.float32)
    ident = (jnp.arange(D)[:, None] == jnp.arange(D)[None, :]).astype(jnp.float32)
    return relay_draw(ident[None] + 0.4 / math.sqrt(D) * noise)


def draw_left_gram(key, part):
    key_diag, key_off = jax.random.split(key)
    diag_vals = jnp.exp(jax.random.uniform(key_diag, (MATS, D), jnp.float32, math.log(100.0), math.log(3000.0)))
    off_vals = 30.0 * jax.random.normal(key_off, (MATS, D, D), jnp.float32)
    ident = (jnp.arange(D)[:, None] == jnp.arange(D)[None, :]).astype(jnp.float32)
    symmetric = 0.5 * (off_vals + off_vals.transpose(0, 2, 1))
    return relay_draw(symmetric * (1.0 - ident)[None] + diag_vals[:, :, None] * ident[None])


def draw_owner_table(key, part):
    used = 5 * LAYERS // 2
    key_pick, key_mix = jax.random.split(key)
    middle = jax.random.permutation(key_pick, jnp.arange(1, N_SHARD - 1, dtype=jnp.int32))[:used - 2]
    picked = jnp.concatenate([jnp.array([0, N_SHARD - 1], jnp.int32), middle])
    groups = jax.random.permutation(key_mix, picked).reshape(LAYERS // 2, 5)
    even_rows = jnp.stack([groups[:, 4], groups[:, 0], groups[:, 2], groups[:, 2], groups[:, 0]], axis=1)
    odd_rows = jnp.stack([groups[:, 4], groups[:, 1], groups[:, 3], groups[:, 3], groups[:, 1]], axis=1)
    return jnp.stack([even_rows, odd_rows], axis=1).reshape(LAYERS, 5).astype(jnp.int32)


def level_of(rng, extent, pieces, smallest, top_value):
    level, own = 1.0, jax.random.fold_in(rng, 6)
    for axis_at, shards_of in pieces:
        heights = jnp.exp(jax.random.uniform(jax.random.fold_in(own, axis_at), (shards_of,), jnp.float32, smallest / len(pieces), top_value / len(pieces)))
        level = level * jnp.repeat(heights, extent[axis_at] // shards_of).reshape([-1 if axis == axis_at else 1 for axis in range(len(extent))])
    return level


def normal_values(key, dims, width, reach, cuts=(), held_as=jnp.bfloat16):
    factor_of = level_of(key, dims, cuts, -0.22, 0.18) if cuts else 1.0
    values = jax.random.normal(key, dims, jnp.float32) * width * factor_of
    return jnp.minimum(jnp.maximum(values, -reach), reach).astype(held_as)


def setup_inputs(seed: int = 0) -> dict:
    splits = jax.random.split(jax.random.key(seed), 12)
    return {
        "gradient": normal_values(splits[0], (D, N_TENSOR, TILES * (D // N_TENSOR)), 1.0, 6.0, ((0, 32), (1, 4)), jnp.float32),
        "weight": normal_values(splits[1], (D, N_TENSOR, TILES * (D // N_TENSOR)), D ** -0.5, 0.3125, ((0, 32), (1, 4)), jnp.float32),
        "first_moment": normal_values(splits[2], (D, N_TENSOR, TILES * (D // N_TENSOR)), 1.0, 6.0, ((0, 32), (1, 4)), jnp.float32),
        "second_moment": jnp.clip(jnp.exp(math.log(3.0) - 2.3025851 * jax.random.uniform(splits[3], (D, N_TENSOR, TILES * (D // N_TENSOR)), jnp.float32) ** level_of(splits[3], (D, N_TENSOR, TILES * (D // N_TENSOR)), ((0, 32), (1, 4)), -0.2, 0.2)), 0.3, 3.0),
        "left_basis": draw_left_basis(jax.random.fold_in(splits[11], 71), 0),
        "left_gram": draw_left_gram(jax.random.fold_in(splits[11], 71), 0),
        "owner_table": draw_owner_table(jax.random.fold_in(splits[11], 71), 0),
        "bias_gradient": normal_values(splits[7], (LAYERS * BIAS,), 1.0, 6.0, ((0, 128),), jnp.float32),
        "bias_weight": normal_values(splits[8], (LAYERS * BIAS,), 0.5, 3.0, ((0, 128),), jnp.float32),
        "bias_first": normal_values(splits[9], (LAYERS * BIAS,), 1.0, 6.0, ((0, 128),), jnp.float32),
        "bias_second": jnp.clip(jnp.exp(math.log(3.0) - 2.3025851 * jax.random.uniform(splits[10], (LAYERS * BIAS,), jnp.float32) ** level_of(splits[10], (LAYERS * BIAS,), ((0, 128),), -0.2, 0.2)), 0.3, 3.0),
    }


TYPE_TILES = (3, 1, 4, 4, 6)
TYPE_START = (0, 3, 4, 8, 12)
HIGH = lax.Precision.HIGHEST

def adam_direction(moment_hat, second_new):
    corr_one = 1.0 - 0.9 ** STEP
    corr_two = 1.0 - 0.95 ** STEP
    return moment_hat / corr_one / (jnp.sqrt(second_new / corr_two) + 1e-08)

def unlay(packed):
    count = packed.shape[2] // (D // N_TENSOR)
    return packed.reshape(D, N_TENSOR, count, D // N_TENSOR).transpose(2, 0, 1, 3).reshape(count, D, D)

def relay(tiles):
    count = tiles.shape[0]
    return tiles.reshape(count, D, N_TENSOR, D // N_TENSOR).transpose(1, 2, 0, 3).reshape(D, N_TENSOR, count * (D // N_TENSOR))

def join_tiles(tiles):
    return tiles.transpose(1, 0, 2).reshape(tiles.shape[1], tiles.shape[0] * tiles.shape[2])

def split_tiles(matrix, tile_count):
    return matrix.reshape(matrix.shape[0], tile_count, matrix.shape[0]).transpose(1, 0, 2)

def refresh_basis(gram_new, basis):
    power = jnp.dot(gram_new, basis, precision=HIGH, preferred_element_type=jnp.float32)
    frame = power / jnp.sqrt(jnp.sum(power * power) + 1e-06)
    for sweep in range(NS_STEPS):
        square = jnp.dot(frame, frame.T, precision=HIGH, preferred_element_type=jnp.float32)
        frame = 1.5 * frame - 0.5 * jnp.dot(square, frame, precision=HIGH, preferred_element_type=jnp.float32)
    return frame

def slot_ranks(owner_table):
    owners = owner_table.reshape(-1).astype(jnp.int32)
    matrix_ids = jnp.arange(owners.shape[0], dtype=jnp.int32)
    earlier = (owners[:, None] == owners[None, :]) & (matrix_ids[None, :] < matrix_ids[:, None])
    return (owners, lax.optimization_barrier(jnp.sum(earlier.astype(jnp.int32), axis=1)).astype(jnp.int32))

def reference(gradient, weight, first_moment, second_moment, left_basis, left_gram, owner_table, bias_gradient, bias_weight, bias_first, bias_second):
    gradient = unlay(gradient)
    weight = unlay(weight)
    first_moment = unlay(first_moment)
    second_moment = unlay(second_moment)
    left_basis = unlay(left_basis)
    left_gram = unlay(left_gram)
    weight_list, first_list, second_list, basis_list, gram_list = ([], [], [], [], [])
    for layer_id in range(LAYERS):
        for kind_id in range(5):
            tile_count = TYPE_TILES[kind_id]
            first_tile = 18 * layer_id + TYPE_START[kind_id]
            matrix_id = 5 * layer_id + kind_id
            grad_mat = join_tiles(gradient[first_tile:first_tile + tile_count])
            weight_mat = join_tiles(weight[first_tile:first_tile + tile_count])
            first_mat = join_tiles(first_moment[first_tile:first_tile + tile_count])
            second_mat = join_tiles(second_moment[first_tile:first_tile + tile_count])
            basis = left_basis[matrix_id]
            gram = left_gram[matrix_id]
            moment_new = 0.9 * first_mat + 0.1 * grad_mat
            grad_hat = jnp.dot(basis.T, grad_mat, precision=HIGH, preferred_element_type=jnp.float32)
            moment_hat = jnp.dot(basis.T, moment_new, precision=HIGH, preferred_element_type=jnp.float32)
            second_new = 0.95 * second_mat + 0.05 * grad_hat * grad_hat
            direction = jnp.dot(basis, adam_direction(moment_hat, second_new), precision=HIGH, preferred_element_type=jnp.float32)
            weight_new = weight_mat - 0.01 * (direction + 0.1 * weight_mat)
            gram_new = 0.95 * gram + 0.05 * jnp.dot(grad_mat, grad_mat.T, precision=HIGH, preferred_element_type=jnp.float32)
            weight_list.append(split_tiles(weight_new, tile_count))
            first_list.append(split_tiles(moment_new, tile_count))
            second_list.append(split_tiles(second_new, tile_count))
            basis_list.append(refresh_basis(gram_new, basis))
            gram_list.append(gram_new)
    owners, ranks = slot_ranks(owner_table)
    owned_basis = jnp.zeros((N_SHARD, MCAP, D, D), jnp.float32).at[owners, ranks].set(jnp.stack(basis_list))
    owned_gram = jnp.zeros((N_SHARD, MCAP, D, D), jnp.float32).at[owners, ranks].set(jnp.stack(gram_list))
    bias_first_new = 0.9 * bias_first + 0.1 * bias_gradient
    bias_second_new = 0.95 * bias_second + 0.05 * bias_gradient * bias_gradient
    bias_updated = bias_weight - 0.01 * adam_direction(bias_first_new, bias_second_new)
    return (relay(jnp.concatenate(weight_list, axis=0)), relay(jnp.concatenate(first_list, axis=0)), relay(jnp.concatenate(second_list, axis=0)), owned_basis, owned_gram, bias_updated, bias_first_new, bias_second_new)
```

```python
import functools

import jax
import jax.numpy as jnp
from jax import lax
from jax.experimental import pallas as pl
from jax.experimental.pallas import tpu as pltpu
from jax.sharding import PartitionSpec as P

MESH = pl.DeviceIdType.MESH
STEP = 10
NS_STEPS = 5
N_SHARD = 32
N_TENSOR = 4
D = 384
ROWS = 12
PAIRS = 6
TYPE_TILES = (3, 1, 4, 4, 6)
TYPE_START = (0, 3, 4, 8, 12)
TYPE_CHUNKS = (3, 1, 3, 3, 5)
CHUNK_START = (0, 3, 4, 7, 10)
CAP = 6
MSG = ROWS * CAP
QMSG = ROWS * 2
LINE = 162
QLINE = 45
ZERO_CHUNK = 180
ZERO_MAT = 60
CORR_ONE = 1.0 - 0.9**STEP
CORR_TWO = 1.0 - 0.95**STEP
TAB_M = 256
TAB_LOC = 320
TAB_C0 = 384
TAB_SIZE = 512
F32 = jnp.float32
BF16 = jnp.bfloat16


def table_kernel(owner_ref, tab_ref):
    @pl.loop(0, 256)
    def _(i):
        tab_ref[i] = ZERO_CHUNK

    @pl.loop(0, 64)
    def _(i):
        tab_ref[TAB_M + i] = ZERO_MAT

    @pl.loop(0, 32)
    def _(i):
        tab_ref[TAB_C0 + i] = 0

    @pl.loop(0, 12)
    def _(layer):
        for kind in range(5):
            mat = layer * 5 + kind
            owner = owner_ref[layer, kind]
            first = tab_ref[TAB_M + 2 * owner] == ZERO_MAT
            chunks = TYPE_CHUNKS[kind]
            held = tab_ref[TAB_C0 + owner]
            base = jnp.where(first, 0, held)
            tab_ref[TAB_M + 2 * owner + jnp.where(first, 0, 1)] = mat
            tab_ref[TAB_C0 + owner] = jnp.where(first, chunks, held)
            tab_ref[TAB_LOC + mat] = MSG * owner + base
            for j in range(chunks):
                tab_ref[owner * 8 + base + j] = layer * 15 + CHUNK_START[kind] + j


def align_rows(src, dst):
    lane = lax.broadcasted_iota(jnp.int32, (ROWS, 128), 1)

    @pl.loop(0, PAIRS)
    def _(pair):
        for half in range(2):
            for kind in range(5):
                for j in range(TYPE_CHUNKS[kind]):
                    col = 1728 * half + 96 * TYPE_START[kind] + 128 * j
                    at, shift = divmod(col, 128)
                    valid = min(128, 96 * TYPE_TILES[kind] - 128 * j)
                    val = src[pl.ds(27 * pair + at, ROWS, stride=LINE), :]
                    if shift:
                        val = pltpu.roll(val, 128 - shift, 1)
                        if valid > 128 - shift:
                            nxt = src[pl.ds(27 * pair + at + 1, ROWS, stride=LINE), :]
                            nxt = pltpu.roll(nxt, 128 - shift, 1)
                            val = jnp.where(lane < 128 - shift, val, nxt)
                    if valid < 128:
                        val = jnp.where(lane < valid, val, 0.0)
                    dst[30 * pair + 15 * half + CHUNK_START[kind] + j] = val


def align_mats(src, dst):
    lane = lax.broadcasted_iota(jnp.int32, (ROWS, 128), 1)

    @pl.loop(0, 15)
    def _(quad):
        for part in range(4):
            at, shift = divmod(96 * part, 128)
            val = src[pl.ds(3 * quad + at, ROWS, stride=QLINE), :]
            if shift:
                val = pltpu.roll(val, 128 - shift, 1)
                if 96 > 128 - shift:
                    nxt = src[pl.ds(3 * quad + at + 1, ROWS, stride=QLINE), :]
                    nxt = pltpu.roll(nxt, 128 - shift, 1)
                    val = jnp.where(lane < 128 - shift, val, nxt)
            dst[4 * quad + part] = jnp.where(lane < 96, val, 0.0)


def split(x):
    high = x.astype(BF16)
    return high, (x - high.astype(F32)).astype(BF16)


def dot3(a, b, dims):
    ah, al = a
    bh, bl = b
    dot = functools.partial(
        lax.dot_general, dimension_numbers=(dims, ((), ())), preferred_element_type=F32
    )
    return dot(ah, bh) + (dot(ah, bl) + dot(al, bh))


NN = ((1,), (0,))
NT = ((1,), (1,))


def main_kernel(
    tab,
    g_hbm,
    m_hbm,
    v_hbm,
    q_hbm,
    s_hbm,
    back_d,
    back_n,
    basis_out,
    gram_out,
    g2,
    m2,
    v2,
    q2,
    s2,
    lined,
    lined_q,
    send_g,
    send_m,
    send_v,
    send_q,
    send_s,
    recv_g,
    recv_m,
    recv_v,
    recv_s,
    qx,
    ret_d,
    ret_n,
    gram,
    xg,
    power,
    q_hi,
    q_lo,
    qt_hi,
    qt_lo,
    g_hat,
    m_hat,
    in_sem,
    send_sem,
    recv_sem,
    own_sem,
):
    me = lax.axis_index("shard")
    rank = lax.axis_index("tensor")
    my_y, my_z, my_c = me // 8, (me // 2) % 4, me % 2

    loads = []
    for n, (src, dst) in enumerate(
        ((q_hbm, q2), (g_hbm, g2), (s_hbm, s2), (m_hbm, m2), (v_hbm, v2))
    ):
        load = pltpu.make_async_copy(src, dst, in_sem.at[n])
        load.start()
        loads.append(load)

    def peer(t):
        o = (11 * t) % 32
        return (
            ((my_y + o // 8) % 4) * 8 + ((my_z + (o // 2) % 4) % 4) * 2 + (my_c + o % 2) % 2
        )

    barrier = pltpu.get_barrier_semaphore()

    @pl.loop(1, N_SHARD)
    def _(t):
        pl.semaphore_signal(barrier, inc=1, device_id=(peer(t), rank), device_id_type=MESH)

    for dx in range(1, N_TENSOR):
        pl.semaphore_signal(
            barrier, inc=1, device_id=(me, (rank + dx) % N_TENSOR), device_id_type=MESH
        )

    lined[ZERO_CHUNK] = jnp.zeros((ROWS, 128), F32)
    lined_q[ZERO_MAT] = jnp.zeros((ROWS, 128), F32)

    def exchange(send, recv, rows, n):
        def one(t):
            dst = peer(t)
            return pltpu.make_async_remote_copy(
                src_ref=send.at[pl.ds(pl.multiple_of(dst * rows, 8), rows)],
                dst_ref=recv.at[pl.ds(pl.multiple_of(me * rows, 8), rows)],
                send_sem=send_sem.at[n],
                recv_sem=recv_sem.at[n],
                device_id=(dst, rank),
                device_id_type=MESH,
            )

        @pl.loop(1, N_SHARD)
        def _(t):
            one(t).start()

        own = pl.ds(pl.multiple_of(me * rows, 8), rows)
        pltpu.make_async_copy(send.at[own], recv.at[own], own_sem.at[n]).start()

    def exchange_done(send, recv, rows, n):
        whole = pl.ds(0, (N_SHARD - 1) * rows)
        every = pltpu.make_async_remote_copy(
            src_ref=send.at[whole],
            dst_ref=recv.at[whole],
            send_sem=send_sem.at[n],
            recv_sem=recv_sem.at[n],
            device_id=((me + 1) % N_SHARD, rank),
            device_id_type=MESH,
        )
        own = pl.ds(pl.multiple_of(me * rows, 8), rows)
        pltpu.make_async_copy(send.at[own], recv.at[own], own_sem.at[n]).wait()
        every.wait_send()
        every.wait_recv()

    def pack(lines, send):
        @pl.loop(0, N_SHARD)
        def _(d):
            for k in range(CAP):
                send[pl.ds(MSG * d + k, ROWS, stride=CAP), :] = lines[tab[d * 8 + k]]

    def pack_mats(lines, send):
        @pl.loop(0, N_SHARD)
        def _(d):
            for j in range(2):
                send[pl.ds(QMSG * d + j, ROWS, stride=2), :] = lines[tab[TAB_M + 2 * d + j]]

    loads[0].wait()
    align_mats(q2, lined_q)
    pack_mats(lined_q, send_q)
    pl.semaphore_wait(barrier, N_SHARD - 1 + N_TENSOR - 1)
    exchange(send_q, qx.at[rank], QMSG, 0)

    loads[1].wait()
    align_rows(g2, lined)
    pack(lined, send_g)
    exchange(send_g, recv_g, MSG, 1)

    loads[2].wait()
    align_mats(s2, lined_q)
    pack_mats(lined_q, send_s)
    exchange(send_s, recv_s, QMSG, 2)

    loads[3].wait()
    m2[...] = 0.9 * m2[...] + 0.1 * g2[...]
    align_rows(m2, lined)
    pack(lined, send_m)
    exchange(send_m, recv_m, MSG, 3)

    loads[4].wait()
    align_rows(v2, lined)
    pack(lined, send_v)
    exchange(send_v, recv_v, MSG, 4)

    def spread(src_of, dst_of, n):
        for dx in range(1, N_TENSOR):
            other = (rank + dx) % N_TENSOR
            pltpu.make_async_remote_copy(
                src_ref=src_of(other),
                dst_ref=dst_of(rank),
                send_sem=send_sem.at[n],
                recv_sem=recv_sem.at[n],
                device_id=(me, other),
                device_id_type=MESH,
            ).start()

    def spread_done(three, n):
        every = pltpu.make_async_remote_copy(
            src_ref=three,
            dst_ref=three,
            send_sem=send_sem.at[n],
            recv_sem=recv_sem.at[n],
            device_id=(me, (rank + 1) % N_TENSOR),
            device_id_type=MESH,
        )
        every.wait_send()
        every.wait_recv()

    exchange_done(send_q, qx.at[rank], QMSG, 0)
    q_part = (lambda other: qx.at[rank]), (lambda other: qx.at[other])
    spread(*q_part, 5)

    exchange_done(send_g, recv_g, MSG, 1)
    c0 = tab[TAB_C0 + me]
    for j in range(2):
        left_h, left_l, right_h, right_l = [], [], [], []
        for k in range(CAP):
            chunk = recv_g[pl.ds(k, D, stride=CAP), :]
            mine = (k < c0) if j == 0 else (k >= c0)
            high, low = split(chunk)
            right_h.append(high)
            right_l.append(low)
            high, low = split(jnp.where(mine, chunk, 0.0))
            left_h.append(high)
            left_l.append(low)
        cat = functools.partial(jnp.concatenate, axis=1)
        gram[j] = dot3((cat(left_h), cat(left_l)), (cat(right_h), cat(right_l)), NT)

    def strip(x):
        return pl.ds(pl.multiple_of(96 * x, 8), 96)

    g_part = (lambda other: gram.at[:, strip(other), :]), (lambda other: xg.at[other])
    spread(*g_part, 6)

    spread_done(qx.at[pl.ds(0, 3)], 5)
    lane = lax.broadcasted_iota(jnp.int32, (D, 128), 1)
    for j in range(2):
        parts = [qx[x, pl.ds(j, D, stride=2), :] for x in range(4)]
        full = jnp.concatenate(
            [
                jnp.where(lane < 96, parts[0], pltpu.roll(parts[1], 96, 1)),
                jnp.where(lane < 64, pltpu.roll(parts[1], 96, 1), pltpu.roll(parts[2], 64, 1)),
                jnp.where(lane < 32, pltpu.roll(parts[2], 64, 1), pltpu.roll(parts[3], 32, 1)),
            ],
            axis=1,
        )
        q_hi[j], q_lo[j] = split(full)
        qt_hi[j], qt_lo[j] = split(full.T)

    exchange_done(send_s, recv_s, QMSG, 2)
    exchange_done(send_m, recv_m, MSG, 3)

    @pl.loop(0, CAP)
    def _(k):
        sel = jnp.where(k >= c0, 1, 0)
        both = jnp.concatenate(
            [recv_g[pl.ds(k, D, stride=CAP), :], recv_m[pl.ds(k, D, stride=CAP), :]], axis=1
        )
        hat = dot3((qt_hi[sel], qt_lo[sel]), split(both), NN)
        g_hat[k] = hat[:, :128]
        m_hat[k] = hat[:, 128:]

    spread_done(xg.at[pl.ds(0, 3)], 6)
    for j in range(2):
        total = gram[j, strip(rank), :]
        for dx in range(1, N_TENSOR):
            total = total + xg[(rank + dx) % N_TENSOR, j]
        held = recv_s[pl.ds(j, D, stride=2), :].T[:96]
        fresh = 0.95 * held + 0.05 * total
        gram_out[j] = fresh.T
        power[j, strip(rank), :] = dot3(split(fresh), (q_hi[j], q_lo[j]), NN)
    p_part = (
        (lambda other: power.at[:, strip(rank), :]),
        (lambda other: power.at[:, strip(other), :]),
    )
    spread(*p_part, 7)

    exchange_done(send_v, recv_v, MSG, 4)

    @pl.loop(0, CAP)
    def _(k):
        rot = g_hat[k]
        second = 0.95 * recv_v[pl.ds(k, D, stride=CAP), :] + 0.05 * rot * rot
        ret_n[pl.ds(k, D, stride=CAP), :] = second
        m_hat[k] = m_hat[k] / CORR_ONE / (jnp.sqrt(second / CORR_TWO) + 1e-08)

    exchange(ret_n, back_n, MSG, 8)

    @pl.loop(0, CAP)
    def _(k):
        sel = jnp.where(k >= c0, 1, 0)
        ret_d[pl.ds(k, D, stride=CAP), :] = dot3((q_hi[sel], q_lo[sel]), split(m_hat[k]), NN)

    exchange(ret_d, back_d, MSG, 9)

    spread_done(power.at[:, pl.ds(0, 288), :], 7)
    for j in range(2):
        full = power[j]
        norm = jnp.sqrt(jnp.sum(full * full, keepdims=True) + 1e-06)
        power[j] = full / norm

    @pl.loop(0, NS_STEPS)
    def _(sweep):
        for j in range(2):
            frame = power[j]
            pieces = split(frame)
            square = dot3(pieces, pieces, NT)
            power[j] = 1.5 * frame - 0.5 * dot3(split(square), pieces, NN)

    for x in range(N_TENSOR):

        @pl.when(rank == x)
        def _():
            basis_out[...] = power[:, :, 96 * x : 96 * x + 96]

    exchange_done(ret_n, back_n, MSG, 8)
    exchange_done(ret_d, back_d, MSG, 9)


def out_pieces():
    owner_of = []
    for half in range(2):
        for kind in range(5):
            start = 1728 * half + 96 * TYPE_START[kind]
            for c in range(96 * TYPE_TILES[kind]):
                owner_of.append((5 * half + kind, start))
    table = []
    for chunk in range(27):
        pieces = []
        for lane in range(128):
            col = 128 * chunk + lane
            mat, start = owner_of[col]
            j, src = divmod(col - start, 128)
            key = (mat, j, (lane - src) % 128)
            if pieces and pieces[-1][0] == key:
                pieces[-1][2] = lane + 1
            else:
                pieces.append([key, lane, lane + 1])
        table.append(pieces)
    return table


def unpack_kernel(tab, back_d, back_n, w2, g2, m2, weight_out, first_out, second_out):
    lane = lax.broadcasted_iota(jnp.int32, (ROWS, 128), 1)
    table = out_pieces()

    @pl.loop(0, PAIRS)
    def _(pair):
        for chunk in range(27):
            vals = [None, None]
            for (mat, j, turn), _lo, hi in reversed(table[chunk]):
                at = tab[TAB_LOC + 10 * pair + mat] + j
                for n, back in enumerate((back_d, back_n)):
                    val = back[pl.ds(at, ROWS, stride=CAP), :]
                    if turn:
                        val = pltpu.roll(val, turn, 1)
                    vals[n] = val if vals[n] is None else jnp.where(lane < hi, val, vals[n])
            here = pl.ds(27 * pair + chunk, ROWS, stride=LINE)
            w = w2[here, :]
            weight_out[here, :] = w - 0.01 * (vals[0] + 0.1 * w)
            second_out[here, :] = vals[1]

    first_out[...] = 0.9 * m2[...] + 0.1 * g2[...]


def adam_direction(moment_hat, second_new):
    return moment_hat / CORR_ONE / (jnp.sqrt(second_new / CORR_TWO) + 1e-08)


def body(
    gradient,
    weight,
    first_moment,
    second_moment,
    left_basis,
    left_gram,
    owner_table,
    bias_gradient,
    bias_weight,
    bias_first,
    bias_second,
):
    smem = pl.BlockSpec(memory_space=pltpu.SMEM)
    vmem = pl.BlockSpec(memory_space=pltpu.VMEM)
    anyw = pl.BlockSpec(memory_space=pl.ANY)
    tab = pl.pallas_call(
        table_kernel,
        out_shape=jax.ShapeDtypeStruct((TAB_SIZE,), jnp.int32),
        in_specs=[smem],
        out_specs=smem,
        name="tables",
    )(owner_table)
    flat = (ROWS * LINE, 128)
    flat_q = (ROWS * QLINE, 128)
    g, w, m, v = (a.reshape(flat) for a in (gradient, weight, first_moment, second_moment))
    q, s = left_basis.reshape(flat_q), left_gram.reshape(flat_q)
    wide = pltpu.VMEM((N_SHARD * MSG, 128), F32)
    mats = pltpu.VMEM((N_SHARD * QMSG, 128), F32)
    full = pltpu.VMEM((2, D, D), F32)
    half = pltpu.VMEM((2, D, D), BF16)
    hats = pltpu.VMEM((CAP, D, 128), F32)
    back_d, back_n, basis, gram = pl.pallas_call(
        main_kernel,
        out_shape=(
            jax.ShapeDtypeStruct((N_SHARD * MSG, 128), F32),
            jax.ShapeDtypeStruct((N_SHARD * MSG, 128), F32),
            jax.ShapeDtypeStruct((2, D, 96), F32),
            jax.ShapeDtypeStruct((2, D, 96), F32),
        ),
        in_specs=[smem] + [anyw] * 5,
        out_specs=(vmem,) * 4,
        scratch_shapes=[pltpu.VMEM(flat, F32)] * 3
        + [pltpu.VMEM(flat_q, F32)] * 2
        + [pltpu.VMEM((ZERO_CHUNK + 1, ROWS, 128), F32), pltpu.VMEM((ZERO_MAT + 1, ROWS, 128), F32)]
        + [wide] * 3
        + [mats] * 2
        + [wide] * 3
        + [mats]
        + [pltpu.VMEM((N_TENSOR, N_SHARD * QMSG, 128), F32)]
        + [wide] * 2
        + [full, pltpu.VMEM((N_TENSOR, 2, 96, D), F32), full]
        + [half] * 4
        + [hats] * 2
        + [
            pltpu.SemaphoreType.DMA((5,)),
            pltpu.SemaphoreType.DMA((10,)),
            pltpu.SemaphoreType.DMA((10,)),
            pltpu.SemaphoreType.DMA((10,)),
        ],
        compiler_params=pltpu.CompilerParams(
            collective_id=0, has_side_effects=True, vmem_limit_bytes=48 << 20
        ),
        name="exchange_and_rotate",
    )(tab, g, m, v, q, s)
    weight_new, first_new, second_new = pl.pallas_call(
        unpack_kernel,
        out_shape=(jax.ShapeDtypeStruct(flat, F32),) * 3,
        in_specs=[smem] + [vmem] * 5,
        out_specs=(vmem,) * 3,
        name="unpack",
    )(tab, back_d, back_n, w, g, m)
    bias_first_new = 0.9 * bias_first + 0.1 * bias_gradient
    bias_second_new = 0.95 * bias_second + 0.05 * bias_gradient * bias_gradient
    bias_updated = bias_weight - 0.01 * adam_direction(bias_first_new, bias_second_new)
    return (
        weight_new.reshape(weight.shape),
        first_new.reshape(weight.shape),
        second_new.reshape(weight.shape),
        basis[None],
        gram[None],
        bias_updated,
        bias_first_new,
        bias_second_new,
    )


def solution(mesh):
    rows = P("shard", "tensor", None)
    flat = P(("shard", "tensor"))
    owned = P("shard", None, None, "tensor")
    return jax.shard_map(
        body,
        mesh=mesh,
        in_specs=(rows,) * 6 + (P(),) + (flat,) * 4,
        out_specs=(rows,) * 3 + (owned,) * 2 + (flat,) * 3,
        check_vma=False,
    )
```

```python
import functools

import jax
import jax.numpy as jnp
from jax import lax
from jax.experimental import pallas as pl
from jax.experimental.pallas import tpu as pltpu
from jax.sharding import PartitionSpec as P

MESH = pl.DeviceIdType.MESH
STEP = 10
NS_STEPS = 5
N_SHARD = 32
N_TENSOR = 4
D = 384
ROWS = 12
PAIRS = 6
TYPE_TILES = (3, 1, 4, 4, 6)
TYPE_START = (0, 3, 4, 8, 12)
TYPE_CHUNKS = (3, 1, 3, 3, 5)
CHUNK_START = (0, 3, 4, 7, 10)
CAP = 6
MSG = ROWS * CAP
QMSG = ROWS * 2
LINE = 162
QLINE = 45
ZERO_CHUNK = 180
ZERO_MAT = 60
CORR_ONE = 1.0 - 0.9**STEP
CORR_TWO = 1.0 - 0.95**STEP
NO_CODE = ZERO_MAT + (ZERO_CHUNK << 8)
HEAD = 48
TAIL = 24
VMEM_ALL = 67043328
F32 = jnp.float32
BF16 = jnp.bfloat16


def code_of(mat):
    layer, kind = divmod(mat, 5)
    return mat + ((layer * 15 + CHUNK_START[kind]) << 8) + (TYPE_CHUNKS[kind] << 16)


def fill_tables(owner, chunk_tab, mat_tab, first_tab):
    @pl.loop(0, N_SHARD)
    def _(d):
        first = jnp.int32(NO_CODE)
        second = jnp.int32(NO_CODE)
        for mat in range(60):
            back = 59 - mat
            first = jnp.where(owner[back % 5, back // 5] == d, code_of(back), first)
            second = jnp.where(owner[mat % 5, mat // 5] == d, code_of(mat), second)
        second = jnp.where(second == first, NO_CODE, second)
        c0, c1 = first >> 16, second >> 16
        at0, at1 = (first >> 8) & 255, (second >> 8) & 255
        mat_tab[2 * d] = first & 255
        mat_tab[2 * d + 1] = second & 255
        first_tab[d] = c0
        for k in range(CAP):
            rest = jnp.where(k - c0 < c1, at1 + k - c0, ZERO_CHUNK)
            chunk_tab[8 * d + k] = jnp.where(k < c0, at0 + k, rest)


def align_rows(src, dst):
    lane = lax.broadcasted_iota(jnp.int32, (ROWS, 128), 1)

    @pl.loop(0, PAIRS)
    def _(pair):
        for half in range(2):
            for kind in range(5):
                for j in range(TYPE_CHUNKS[kind]):
                    col = 1728 * half + 96 * TYPE_START[kind] + 128 * j
                    at, shift = divmod(col, 128)
                    valid = min(128, 96 * TYPE_TILES[kind] - 128 * j)
                    val = src[pl.ds(27 * pair + at, ROWS, stride=LINE), :]
                    if shift:
                        val = pltpu.roll(val, 128 - shift, 1)
                        if valid > 128 - shift:
                            nxt = src[pl.ds(27 * pair + at + 1, ROWS, stride=LINE), :]
                            nxt = pltpu.roll(nxt, 128 - shift, 1)
                            val = jnp.where(lane < 128 - shift, val, nxt)
                    if valid < 128:
                        val = jnp.where(lane < valid, val, 0.0)
                    dst[30 * pair + 15 * half + CHUNK_START[kind] + j] = val


def align_mats(src, dst):
    lane = lax.broadcasted_iota(jnp.int32, (ROWS, 128), 1)

    @pl.loop(0, 15)
    def _(quad):
        for part in range(4):
            at, shift = divmod(96 * part, 128)
            val = src[3 * quad + at]
            if shift:
                val = pltpu.roll(val, 128 - shift, 1)
                if 96 > 128 - shift:
                    nxt = src[3 * quad + at + 1]
                    nxt = pltpu.roll(nxt, 128 - shift, 1)
                    val = jnp.where(lane < 128 - shift, val, nxt)
            dst[4 * quad + part] = jnp.where(lane < 96, val, 0.0)


def split(x):
    high = x.astype(BF16)
    return high, (x - high.astype(F32)).astype(BF16)


def dot3(a, b, dims):
    ah, al = a
    bh, bl = b
    dot = functools.partial(
        lax.dot_general, dimension_numbers=(dims, ((), ())), preferred_element_type=F32
    )
    return dot(ah, bh) + (dot(ah, bl) + dot(al, bh))


NN = ((1,), (0,))
NT = ((1,), (1,))


def main_kernel(
    owner,
    g_hbm,
    m_hbm,
    v_hbm,
    q_hbm,
    s_hbm,
    back_d,
    back_n,
    first_out,
    basis_out,
    gram_out,
    loc_out,
    g2,
    m2,
    v2,
    q2,
    s2,
    lined,
    lined_q,
    send_g,
    send_m,
    send_v,
    send_q,
    send_s,
    recv_g,
    recv_m,
    recv_v,
    recv_s,
    qx,
    ret_d,
    ret_n,
    gram,
    xg,
    power,
    q_hi,
    q_lo,
    qt_hi,
    qt_lo,
    g_hat,
    m_hat,
    gram_strip,
    basis_strip,
    chunk_tab,
    mat_tab,
    first_tab,
    in_sem,
    q_sem,
    s_sem,
    send_sem,
    recv_sem,
    own_sem,
):
    me = lax.axis_index("shard")
    rank = lax.axis_index("tensor")
    my_y, my_z, my_c = me // 8, (me // 2) % 4, me % 2

    def chunk_load(src, dst, sem, c):
        lanes = pl.ds(pl.multiple_of(128 * c, 128), 128)
        return pltpu.make_async_copy(src.at[:, 0, lanes], dst.at[c], sem.at[c])

    @pl.loop(0, QLINE)
    def _(c):
        chunk_load(q_hbm, q2, q_sem, c).start()

    loads = []
    for n, (src, dst) in enumerate(((g_hbm, g2), (m_hbm, m2), (v_hbm, v2))):
        load = pltpu.make_async_copy(src, dst, in_sem.at[n])
        load.start()
        loads.append(load)

    @pl.loop(0, QLINE)
    def _(c):
        chunk_load(s_hbm, s2, s_sem, c).start()

    def peer(t):
        o = (11 * t) % 32
        return (
            ((my_y + o // 8) % 4) * 8 + ((my_z + (o // 2) % 4) % 4) * 2 + (my_c + o % 2) % 2
        )

    barrier = pltpu.get_barrier_semaphore()

    @pl.loop(1, N_SHARD)
    def _(t):
        pl.semaphore_signal(barrier, inc=1, device_id=(peer(t), rank), device_id_type=MESH)

    for dx in range(1, N_TENSOR):
        pl.semaphore_signal(
            barrier, inc=1, device_id=(me, (rank + dx) % N_TENSOR), device_id_type=MESH
        )

    lined[ZERO_CHUNK] = jnp.zeros((ROWS, 128), F32)
    lined_q[ZERO_MAT] = jnp.zeros((ROWS, 128), F32)
    fill_tables(owner, chunk_tab, mat_tab, first_tab)

    def own_copy(send, recv, unit, off, rows, n):
        own = pl.ds(pl.multiple_of(me * unit + off, 8), rows)
        return pltpu.make_async_copy(send.at[own], recv.at[own], own_sem.at[n])

    def exchange(send, recv, unit, n, off=0, rows=None):
        rows = unit if rows is None else rows

        @pl.loop(1, N_SHARD)
        def _(t):
            dst = peer(t)
            pltpu.make_async_remote_copy(
                src_ref=send.at[pl.ds(pl.multiple_of(dst * unit + off, 8), rows)],
                dst_ref=recv.at[pl.ds(pl.multiple_of(me * unit + off, 8), rows)],
                send_sem=send_sem.at[n],
                recv_sem=recv_sem.at[n],
                device_id=(dst, rank),
                device_id_type=MESH,
            ).start()

        own_copy(send, recv, unit, off, rows, n).start()

    def exchange_done(send, recv, unit, n, off=0, rows=None):
        rows = unit if rows is None else rows
        whole = pl.ds(0, (N_SHARD - 1) * rows)
        every = pltpu.make_async_remote_copy(
            src_ref=send.at[whole],
            dst_ref=recv.at[whole],
            send_sem=send_sem.at[n],
            recv_sem=recv_sem.at[n],
            device_id=((me + 1) % N_SHARD, rank),
            device_id_type=MESH,
        )
        own_copy(send, recv, unit, off, rows, n).wait()
        every.wait_send()
        every.wait_recv()

    def pack(lines, send):
        @pl.loop(0, N_SHARD)
        def _(d):
            for k in range(CAP):
                send[pl.ds(MSG * d + k, ROWS, stride=CAP), :] = lines[chunk_tab[d * 8 + k]]

    def pack_mats(lines, send):
        @pl.loop(0, N_SHARD)
        def _(d):
            for j in range(2):
                send[pl.ds(QMSG * d + j, ROWS, stride=2), :] = lines[mat_tab[2 * d + j]]

    @pl.loop(0, QLINE)
    def _(c):
        chunk_load(q_hbm, q2, q_sem, c).wait()

    align_mats(q2, lined_q)
    pack_mats(lined_q, send_q)
    pl.semaphore_wait(barrier, N_SHARD - 1 + N_TENSOR - 1)
    exchange(send_q, qx.at[rank], QMSG, 0)

    loads[0].wait()
    align_rows(g2, lined)
    pack(lined, send_g)
    exchange(send_g, recv_g, MSG, 1)

    @pl.loop(0, QLINE)
    def _(c):
        chunk_load(s_hbm, s2, s_sem, c).wait()

    align_mats(s2, lined_q)
    pack_mats(lined_q, send_s)
    exchange(send_s, recv_s, QMSG, 2)

    loads[1].wait()
    m2[...] = 0.9 * m2[...] + 0.1 * g2[...]
    save_first = pltpu.make_async_copy(m2, first_out, in_sem.at[3])
    save_first.start()
    align_rows(m2, lined)
    pack(lined, send_m)
    exchange(send_m, recv_m, MSG, 3)

    loads[2].wait()
    align_rows(v2, lined)
    pack(lined, send_v)
    exchange(send_v, recv_v, MSG, 4, 0, HEAD)
    exchange(send_v, recv_v, MSG, 10, HEAD, TAIL)

    @pl.loop(0, 12)
    def _(layer):
        for kind in range(5):
            mat = 5 * layer + kind
            group = owner[kind, layer]
            base = jnp.where(mat_tab[2 * group] == mat, 0, first_tab[group])
            loc_out[mat] = MSG * group + base

    def spread(src_of, dst_of, n):
        for dx in range(1, N_TENSOR):
            other = (rank + dx) % N_TENSOR
            pltpu.make_async_remote_copy(
                src_ref=src_of(other),
                dst_ref=dst_of(rank),
                send_sem=send_sem.at[n],
                recv_sem=recv_sem.at[n],
                device_id=(me, other),
                device_id_type=MESH,
            ).start()

    def spread_done(three, n):
        every = pltpu.make_async_remote_copy(
            src_ref=three,
            dst_ref=three,
            send_sem=send_sem.at[n],
            recv_sem=recv_sem.at[n],
            device_id=(me, (rank + 1) % N_TENSOR),
            device_id_type=MESH,
        )
        every.wait_send()
        every.wait_recv()

    exchange_done(send_q, qx.at[rank], QMSG, 0)
    q_part = (lambda other: qx.at[rank]), (lambda other: qx.at[other])
    spread(*q_part, 5)

    exchange_done(send_g, recv_g, MSG, 1)
    c0 = first_tab[me]
    for j in range(2):
        left_h, left_l, right_h, right_l = [], [], [], []
        for k in range(CAP):
            chunk = recv_g[pl.ds(k, D, stride=CAP), :]
            mine = (k < c0) if j == 0 else (k >= c0)
            high, low = split(chunk)
            right_h.append(high)
            right_l.append(low)
            high, low = split(jnp.where(mine, chunk, 0.0))
            left_h.append(high)
            left_l.append(low)
        cat = functools.partial(jnp.concatenate, axis=1)
        gram[j] = dot3((cat(left_h), cat(left_l)), (cat(right_h), cat(right_l)), NT)

    def strip(x):
        return pl.ds(pl.multiple_of(96 * x, 8), 96)

    g_part = (lambda other: gram.at[:, strip(other), :]), (lambda other: xg.at[other])
    spread(*g_part, 6)

    spread_done(qx.at[pl.ds(0, 3)], 5)
    lane = lax.broadcasted_iota(jnp.int32, (D, 128), 1)
    for j in range(2):
        parts = [qx[x, pl.ds(j, D, stride=2), :] for x in range(4)]
        full = jnp.concatenate(
            [
                jnp.where(lane < 96, parts[0], pltpu.roll(parts[1], 96, 1)),
                jnp.where(lane < 64, pltpu.roll(parts[1], 96, 1), pltpu.roll(parts[2], 64, 1)),
                jnp.where(lane < 32, pltpu.roll(parts[2], 64, 1), pltpu.roll(parts[3], 32, 1)),
            ],
            axis=1,
        )
        q_hi[j], q_lo[j] = split(full)
        qt_hi[j], qt_lo[j] = split(full.T)

    exchange_done(send_s, recv_s, QMSG, 2)
    exchange_done(send_m, recv_m, MSG, 3)

    @pl.loop(0, CAP)
    def _(k):
        sel = jnp.where(k >= c0, 1, 0)
        both = jnp.concatenate(
            [recv_g[pl.ds(k, D, stride=CAP), :], recv_m[pl.ds(k, D, stride=CAP), :]], axis=1
        )
        hat = dot3((qt_hi[sel], qt_lo[sel]), split(both), NN)
        g_hat[pl.ds(k, D, stride=CAP), :] = hat[:, :128]
        m_hat[pl.ds(k, D, stride=CAP), :] = hat[:, 128:]

    spread_done(xg.at[pl.ds(0, 3)], 6)
    for j in range(2):
        total = gram[j, strip(rank), :]
        for dx in range(1, N_TENSOR):
            total = total + xg[(rank + dx) % N_TENSOR, j]
        held = recv_s[pl.ds(j, D, stride=2), :].T[:96]
        fresh = 0.95 * held + 0.05 * total
        gram_strip[j] = fresh
        power[j, strip(rank), :] = dot3(split(fresh), (q_hi[j], q_lo[j]), NN)
    p_part = (
        (lambda other: power.at[:, strip(rank), :]),
        (lambda other: power.at[:, strip(other), :]),
    )
    spread(*p_part, 7)

    for n, off, rows in ((4, 0, HEAD), (10, HEAD, TAIL)):
        exchange_done(send_v, recv_v, MSG, n, off, rows)

        @pl.loop(0, N_SHARD)
        def _(s):
            here = pl.ds(pl.multiple_of(MSG * s + off, 8), rows)
            rot = g_hat[here, :]
            ret_n[here, :] = 0.95 * recv_v[here, :] + 0.05 * rot * rot

        exchange(ret_n, back_n, MSG, 8 if off == 0 else 11, off, rows)

    @pl.loop(0, N_SHARD)
    def _(s):
        here = pl.ds(pl.multiple_of(MSG * s, 8), MSG)
        m_hat[here, :] = m_hat[here, :] / CORR_ONE / (jnp.sqrt(ret_n[here, :] / CORR_TWO) + 1e-08)

    @pl.loop(0, CAP)
    def _(k):
        sel = jnp.where(k >= c0, 1, 0)
        ret_d[pl.ds(k, D, stride=CAP), :] = dot3((q_hi[sel], q_lo[sel]), split(m_hat[pl.ds(k, D, stride=CAP), :]), NN)

    exchange(ret_d, back_d, MSG, 9)

    spread_done(power.at[:, pl.ds(0, 288), :], 7)
    for j in range(2):
        full = power[j]
        norm = jnp.sqrt(jnp.sum(full * full, keepdims=True) + 1e-06)
        power[j] = full / norm

    @pl.loop(0, NS_STEPS)
    def _(sweep):
        for j in range(2):
            frame = power[j]
            pieces = split(frame)
            square = dot3(pieces, pieces, NT)
            power[j] = 1.5 * frame - 0.5 * dot3(split(square), pieces, NN)

    for x in range(N_TENSOR):

        @pl.when(rank == x)
        def _():
            for j in range(2):
                basis_strip[j] = power[j, :, 96 * x : 96 * x + 96].T

    save_basis = pltpu.make_async_copy(basis_strip, basis_out, in_sem.at[4])
    save_basis.start()
    save_gram = pltpu.make_async_copy(gram_strip, gram_out, in_sem.at[5])
    save_gram.start()
    exchange_done(ret_n, back_n, MSG, 8, 0, HEAD)
    exchange_done(ret_n, back_n, MSG, 11, HEAD, TAIL)
    exchange_done(ret_d, back_d, MSG, 9)
    save_first.wait()
    save_basis.wait()
    save_gram.wait()


def out_pieces():
    owner_of = []
    for half in range(2):
        for kind in range(5):
            start = 1728 * half + 96 * TYPE_START[kind]
            for c in range(96 * TYPE_TILES[kind]):
                owner_of.append((5 * half + kind, start))
    table = []
    for chunk in range(27):
        pieces = []
        for lane in range(128):
            col = 128 * chunk + lane
            mat, start = owner_of[col]
            j, src = divmod(col - start, 128)
            key = (mat, j, (lane - src) % 128)
            if pieces and pieces[-1][0] == key:
                pieces[-1][2] = lane + 1
            else:
                pieces.append([key, lane, lane + 1])
        table.append(pieces)
    return table


def unpack_kernel(
    loc,
    back_d,
    back_n,
    w_hbm,
    first,
    basis,
    gram,
    bias_g,
    bias_w,
    bias_m,
    bias_v,
    weight_out,
    first_out,
    second_out,
    basis_out,
    gram_out,
    bias_w_out,
    bias_m_out,
    bias_v_out,
    dv,
    nv,
    w2,
    f2,
    b2,
    s2,
    second2,
    sem,
    sem_out,
):
    def copy(src, dst, n, sems=sem):
        made = pltpu.make_async_copy(src, dst, sems.at[n])
        made.start()
        return made

    load_n = copy(back_n, nv, 0)
    load_d = copy(back_d, dv, 1)
    load_w = copy(w_hbm, w2, 2)
    load_f = copy(first, f2, 3)
    load_b = copy(basis, b2, 4)
    load_s = copy(gram, s2, 5)

    moment = 0.9 * bias_m[...] + 0.1 * bias_g[...]
    second = 0.95 * bias_v[...] + 0.05 * bias_g[...] * bias_g[...]
    bias_m_out[...] = moment
    bias_v_out[...] = second
    bias_w_out[...] = bias_w[...] - 0.01 * (
        moment / CORR_ONE / (jnp.sqrt(second / CORR_TWO) + 1e-08)
    )
    lane = lax.broadcasted_iota(jnp.int32, (ROWS, 128), 1)
    table = out_pieces()

    def unpack(back, write):
        @pl.loop(0, PAIRS)
        def _(pair):
            for chunk in range(27):
                out = None
                for (mat, j, turn), _lo, hi in reversed(table[chunk]):
                    at = loc[10 * pair + mat] + j
                    val = back[pl.ds(at, ROWS, stride=CAP), :]
                    if turn:
                        val = pltpu.roll(val, turn, 1)
                    out = val if out is None else jnp.where(lane < hi, val, out)
                write(pl.ds(27 * pair + chunk, ROWS, stride=LINE), out)

    def write_second(here, val):
        second2[here, :] = val

    def write_weight(here, val):
        w = w2[here, :]
        w2[here, :] = w - 0.01 * (val + 0.1 * w)

    load_n.wait()
    unpack(nv, write_second)
    saves = [copy(second2, second_out, 0, sem_out)]
    load_f.wait()
    saves.append(copy(f2, first_out, 1, sem_out))
    load_b.wait()
    saves.append(copy(b2, basis_out, 2, sem_out))
    load_s.wait()
    saves.append(copy(s2, gram_out, 3, sem_out))
    load_d.wait()
    load_w.wait()
    unpack(dv, write_weight)
    saves.append(copy(w2, weight_out, 4, sem_out))
    for save in saves:
        save.wait()


def body(
    gradient,
    weight,
    first_moment,
    second_moment,
    left_basis,
    left_gram,
    owner_table,
    bias_gradient,
    bias_weight,
    bias_first,
    bias_second,
):
    smem = pl.BlockSpec(memory_space=pltpu.SMEM)
    vmem = pl.BlockSpec(memory_space=pltpu.VMEM)
    hbm = pl.BlockSpec(memory_space=pltpu.HBM)
    flat = (ROWS * LINE, 128)
    g, w, m, v = (a.reshape(flat) for a in (gradient, weight, first_moment, second_moment))
    wide = pltpu.VMEM((N_SHARD * MSG, 128), F32)
    mats = pltpu.VMEM((N_SHARD * QMSG, 128), F32)
    full = pltpu.VMEM((2, D, D), F32)
    half = pltpu.VMEM((2, D, D), BF16)
    strips = pltpu.VMEM((2, 96, D), F32)
    rows = pltpu.VMEM(flat, F32)
    lines_q = pltpu.VMEM((QLINE, ROWS, 128), F32)
    wide_out = jax.ShapeDtypeStruct((N_SHARD * MSG, 128), F32)
    flat_out = jax.ShapeDtypeStruct(flat, F32)
    strip_out = jax.ShapeDtypeStruct((2, 96, D), F32)
    back_d, back_n, first, basis, gram, loc = pl.pallas_call(
        main_kernel,
        out_shape=(
            wide_out,
            wide_out,
            flat_out,
            strip_out,
            strip_out,
            jax.ShapeDtypeStruct((64,), jnp.int32),
        ),
        in_specs=[smem] + [hbm] * 5,
        out_specs=(hbm,) * 5 + (smem,),
        scratch_shapes=[rows] * 3
        + [lines_q] * 2
        + [pltpu.VMEM((ZERO_CHUNK + 1, ROWS, 128), F32), pltpu.VMEM((ZERO_MAT + 1, ROWS, 128), F32)]
        + [wide] * 3
        + [mats] * 2
        + [wide] * 3
        + [mats]
        + [pltpu.VMEM((N_TENSOR, N_SHARD * QMSG, 128), F32)]
        + [wide] * 2
        + [full, pltpu.VMEM((N_TENSOR, 2, 96, D), F32), full]
        + [half] * 4
        + [wide] * 2
        + [strips] * 2
        + [
            pltpu.SMEM((256,), jnp.int32),
            pltpu.SMEM((64,), jnp.int32),
            pltpu.SMEM((32,), jnp.int32),
            pltpu.SemaphoreType.DMA((6,)),
            pltpu.SemaphoreType.DMA((QLINE,)),
            pltpu.SemaphoreType.DMA((QLINE,)),
            pltpu.SemaphoreType.DMA((12,)),
            pltpu.SemaphoreType.DMA((12,)),
            pltpu.SemaphoreType.DMA((12,)),
        ],
        compiler_params=pltpu.CompilerParams(
            collective_id=0, has_side_effects=True, vmem_limit_bytes=VMEM_ALL
        ),
        name="exchange_and_rotate",
    )(owner_table.T, g, m, v, left_basis, left_gram)
    bias_out = jax.ShapeDtypeStruct(bias_gradient.shape, F32)
    outs = pl.pallas_call(
        unpack_kernel,
        out_shape=(flat_out,) * 3 + (strip_out,) * 2 + (bias_out,) * 3,
        in_specs=[smem] + [hbm] * 6 + [vmem] * 4,
        out_specs=(hbm,) * 5 + (vmem,) * 3,
        scratch_shapes=[wide] * 2
        + [rows] * 2
        + [strips] * 2
        + [rows]
        + [pltpu.SemaphoreType.DMA((6,)), pltpu.SemaphoreType.DMA((5,))],
        compiler_params=pltpu.CompilerParams(vmem_limit_bytes=VMEM_ALL),
        name="unpack",
    )(
        loc,
        back_d,
        back_n,
        w,
        first,
        basis,
        gram,
        bias_gradient,
        bias_weight,
        bias_first,
        bias_second,
    )
    weight_new, first_new, second_new, basis_new, gram_new = outs[:5]
    return (
        weight_new.reshape(weight.shape),
        first_new.reshape(weight.shape),
        second_new.reshape(weight.shape),
        basis_new.transpose(0, 2, 1)[None],
        gram_new.transpose(0, 2, 1)[None],
        *outs[5:],
    )


def solution(mesh):
    rows = P("shard", "tensor", None)
    flat = P(("shard", "tensor"))
    owned = P("shard", None, None, "tensor")
    return jax.shard_map(
        body,
        mesh=mesh,
        in_specs=(rows,) * 6 + (P(),) + (flat,) * 4,
        out_specs=(rows,) * 3 + (owned,) * 2 + (flat,) * 3,
        check_vma=False,
    )
```

```python
import functools

import jax
import jax.numpy as jnp
from jax import lax
from jax.experimental import pallas as pl
from jax.experimental.pallas import tpu as pltpu
from jax.sharding import PartitionSpec as P

MESH = pl.DeviceIdType.MESH
STEP = 10
NS_STEPS = 5
N_SHARD = 32
N_TENSOR = 4
D = 384
ROWS = 12
PAIRS = 6
TYPE_TILES = (3, 1, 4, 4, 6)
TYPE_START = (0, 3, 4, 8, 12)
TYPE_CHUNKS = (3, 1, 3, 3, 5)
CHUNK_START = (0, 3, 4, 7, 10)
CAP = 6
MSG = ROWS * CAP
QMSG = ROWS * 2
LINE = 162
QLINE = 45
ZERO_CHUNK = 180
ZERO_MAT = 60
CORR_ONE = 1.0 - 0.9**STEP
CORR_TWO = 1.0 - 0.95**STEP
NO_CODE = (ZERO_MAT << 16) + (ZERO_CHUNK << 8)
HEAD = 48
TAIL = 24
VMEM_ALL = 67043328
F32 = jnp.float32
BF16 = jnp.bfloat16


def table_of(owners):
    group = lax.broadcasted_iota(jnp.int32, (N_SHARD, 12), 0)
    layer = lax.broadcasted_iota(jnp.int32, (N_SHARD, 12), 1)
    low = jnp.full((N_SHARD, 12), NO_CODE, jnp.int32)
    high = jnp.full((N_SHARD, 12), -1, jnp.int32)
    for kind in range(5):
        code = ((5 * layer + kind) << 16) + ((15 * layer + CHUNK_START[kind]) << 8)
        code = code + TYPE_CHUNKS[kind]
        hit = owners[kind : kind + 1, :] == group
        low = jnp.minimum(low, jnp.where(hit, code, NO_CODE))
        high = jnp.maximum(high, jnp.where(hit, code, -1))
    first = jnp.min(low, axis=1, keepdims=True)
    second = jnp.max(high, axis=1, keepdims=True)
    second = jnp.where((second < 0) | (second == first), NO_CODE, second)
    c0, c1 = first & 255, second & 255
    at0, at1 = (first >> 8) & 255, (second >> 8) & 255
    k = lax.broadcasted_iota(jnp.int32, (N_SHARD, 128), 1)
    rest = jnp.where(k - c0 < c1, at1 + k - c0, ZERO_CHUNK)
    table = jnp.where(k < c0, at0 + k, rest)
    table = jnp.where(k == 8, first >> 16, table)
    table = jnp.where(k == 9, second >> 16, table)
    return jnp.where(k == 10, c0, table)


def place_of(owner, tab, pair, mat):
    group = owner[mat % 5, 2 * pair + mat // 5]
    base = jnp.where(tab[group, 8] == 10 * pair + mat, 0, tab[group, 10])
    return MSG * group + base


def align_rows(src, dst):
    lane = lax.broadcasted_iota(jnp.int32, (ROWS, 128), 1)

    @pl.loop(0, PAIRS)
    def _(pair):
        for half in range(2):
            for kind in range(5):
                for j in range(TYPE_CHUNKS[kind]):
                    col = 1728 * half + 96 * TYPE_START[kind] + 128 * j
                    at, shift = divmod(col, 128)
                    valid = min(128, 96 * TYPE_TILES[kind] - 128 * j)
                    val = src[pl.ds(27 * pair + at, ROWS, stride=LINE), :]
                    if shift:
                        val = pltpu.roll(val, 128 - shift, 1)
                        if valid > 128 - shift:
                            nxt = src[pl.ds(27 * pair + at + 1, ROWS, stride=LINE), :]
                            nxt = pltpu.roll(nxt, 128 - shift, 1)
                            val = jnp.where(lane < 128 - shift, val, nxt)
                    if valid < 128:
                        val = jnp.where(lane < valid, val, 0.0)
                    dst[30 * pair + 15 * half + CHUNK_START[kind] + j] = val


def align_mats(src, dst):
    lane = lax.broadcasted_iota(jnp.int32, (ROWS, 128), 1)

    @pl.loop(0, 15)
    def _(quad):
        for part in range(4):
            at, shift = divmod(96 * part, 128)
            val = src[pl.ds(3 * quad + at, ROWS, stride=QLINE), :]
            if shift:
                val = pltpu.roll(val, 128 - shift, 1)
                if 96 > 128 - shift:
                    nxt = src[pl.ds(3 * quad + at + 1, ROWS, stride=QLINE), :]
                    nxt = pltpu.roll(nxt, 128 - shift, 1)
                    val = jnp.where(lane < 128 - shift, val, nxt)
            dst[4 * quad + part] = jnp.where(lane < 96, val, 0.0)


def split(x):
    high = x.astype(BF16)
    return high, (x - high.astype(F32)).astype(BF16)


def dot3(a, b, dims):
    ah, al = a
    bh, bl = b
    dot = functools.partial(
        lax.dot_general, dimension_numbers=(dims, ((), ())), preferred_element_type=F32
    )
    return dot(ah, bh) + (dot(ah, bl) + dot(al, bh))


NN = ((1,), (0,))
NT = ((1,), (1,))


def out_pieces():
    owner_of = []
    for half in range(2):
        for kind in range(5):
            start = 1728 * half + 96 * TYPE_START[kind]
            for c in range(96 * TYPE_TILES[kind]):
                owner_of.append((5 * half + kind, start))
    table = []
    for chunk in range(27):
        pieces = []
        for lane in range(128):
            col = 128 * chunk + lane
            mat, start = owner_of[col]
            j, src = divmod(col - start, 128)
            key = (mat, j, (lane - src) % 128)
            if pieces and pieces[-1][0] == key:
                pieces[-1][2] = lane + 1
            else:
                pieces.append([key, lane, lane + 1])
        table.append(pieces)
    return table


def unpack(back, owner, tab, write):
    lane = lax.broadcasted_iota(jnp.int32, (ROWS, 128), 1)
    table = out_pieces()

    @pl.loop(0, PAIRS)
    def _(pair):
        places = [place_of(owner, tab, pair, mat) for mat in range(10)]
        for chunk in range(27):
            out = None
            for (mat, j, turn), _lo, hi in reversed(table[chunk]):
                val = back[pl.ds(places[mat] + j, ROWS, stride=CAP), :]
                if turn:
                    val = pltpu.roll(val, turn, 1)
                out = val if out is None else jnp.where(lane < hi, val, out)
            write(pl.ds(27 * pair + chunk, ROWS, stride=LINE), out)


def main_kernel(
    owner,
    owners,
    g_hbm,
    m_hbm,
    v_hbm,
    q_hbm,
    s_hbm,
    back_d,
    second_out,
    first_out,
    basis_out,
    gram_out,
    tab_out,
    g2,
    m2,
    v2,
    q2,
    s2,
    lined,
    lined_q,
    send_g,
    send_m,
    send_v,
    send_q,
    send_s,
    recv_g,
    recv_m,
    recv_v,
    recv_s,
    qx,
    ret_d,
    ret_n,
    gram,
    xg,
    power,
    q_hi,
    q_lo,
    qt_hi,
    qt_lo,
    g_hat,
    m_hat,
    gram_strip,
    basis_strip,
    back_n,
    second2,
    tab_vec,
    tab,
    in_sem,
    send_sem,
    recv_sem,
    own_sem,
):
    me = lax.axis_index("shard")
    rank = lax.axis_index("tensor")
    my_y, my_z, my_c = me // 8, (me // 2) % 4, me % 2

    def peer(t):
        o = (11 * t) % 32
        return (
            ((my_y + o // 8) % 4) * 8 + ((my_z + (o // 2) % 4) % 4) * 2 + (my_c + o % 2) % 2
        )

    barrier = pltpu.get_barrier_semaphore()

    @pl.loop(1, N_SHARD)
    def _(t):
        pl.semaphore_signal(barrier, inc=1, device_id=(peer(t), rank), device_id_type=MESH)

    for dx in range(1, N_TENSOR):
        pl.semaphore_signal(
            barrier, inc=1, device_id=(me, (rank + dx) % N_TENSOR), device_id_type=MESH
        )

    def local(src, dst, n):
        made = pltpu.make_async_copy(src, dst, in_sem.at[n])
        made.start()
        return made

    load_q = local(q_hbm.at[:, 0, :], q2, 0)
    load_g = local(g_hbm, g2, 1)
    load_s = local(s_hbm.at[:, 0, :], s2, 2)
    load_m = local(m_hbm, m2, 3)
    load_v = local(v_hbm, v2, 4)
    tab_vec[...] = table_of(owners[...])
    load_tab = local(tab_vec, tab, 5)
    save_tab = local(tab_vec, tab_out, 6)

    lined[ZERO_CHUNK] = jnp.zeros((ROWS, 128), F32)
    lined_q[ZERO_MAT] = jnp.zeros((ROWS, 128), F32)

    def own_copy(send, recv, unit, off, rows, n):
        own = pl.ds(pl.multiple_of(me * unit + off, 8), rows)
        return pltpu.make_async_copy(send.at[own], recv.at[own], own_sem.at[n])

    def exchange(send, recv, unit, n, off=0, rows=None):
        rows = unit if rows is None else rows

        @pl.loop(1, N_SHARD)
        def _(t):
            dst = peer(t)
            pltpu.make_async_remote_copy(
                src_ref=send.at[pl.ds(pl.multiple_of(dst * unit + off, 8), rows)],
                dst_ref=recv.at[pl.ds(pl.multiple_of(me * unit + off, 8), rows)],
                send_sem=send_sem.at[n],
                recv_sem=recv_sem.at[n],
                device_id=(dst, rank),
                device_id_type=MESH,
            ).start()

        own_copy(send, recv, unit, off, rows, n).start()

    def exchange_done(send, recv, unit, n, off=0, rows=None):
        rows = unit if rows is None else rows
        whole = pl.ds(0, (N_SHARD - 1) * rows)
        every = pltpu.make_async_remote_copy(
            src_ref=send.at[whole],
            dst_ref=recv.at[whole],
            send_sem=send_sem.at[n],
            recv_sem=recv_sem.at[n],
            device_id=((me + 1) % N_SHARD, rank),
            device_id_type=MESH,
        )
        own_copy(send, recv, unit, off, rows, n).wait()
        every.wait_send()
        every.wait_recv()

    def pack(lines, send):
        @pl.loop(0, N_SHARD)
        def _(d):
            for k in range(CAP):
                send[pl.ds(MSG * d + k, ROWS, stride=CAP), :] = lines[tab[d, k]]

    def pack_mats(lines, send):
        @pl.loop(0, N_SHARD)
        def _(d):
            for j in range(2):
                send[pl.ds(QMSG * d + j, ROWS, stride=2), :] = lines[tab[d, 8 + j]]

    load_q.wait()
    align_mats(q2, lined_q)
    load_g.wait()
    align_rows(g2, lined)
    load_tab.wait()
    pack_mats(lined_q, send_q)
    pack(lined, send_g)
    load_s.wait()
    align_mats(s2, lined_q)
    pack_mats(lined_q, send_s)
    pl.semaphore_wait(barrier, N_SHARD - 1 + N_TENSOR - 1)
    exchange(send_q, qx.at[rank], QMSG, 0)
    exchange(send_g, recv_g, MSG, 1)
    exchange(send_s, recv_s, QMSG, 2)

    load_m.wait()
    m2[...] = 0.9 * m2[...] + 0.1 * g2[...]
    save_first = local(m2, first_out, 7)
    align_rows(m2, lined)
    pack(lined, send_m)
    exchange(send_m, recv_m, MSG, 3)

    load_v.wait()
    align_rows(v2, lined)
    pack(lined, send_v)
    exchange(send_v, recv_v, MSG, 4, 0, HEAD)
    exchange(send_v, recv_v, MSG, 10, HEAD, TAIL)

    def spread(src_of, dst_of, n):
        for dx in range(1, N_TENSOR):
            other = (rank + dx) % N_TENSOR
            pltpu.make_async_remote_copy(
                src_ref=src_of(other),
                dst_ref=dst_of(rank),
                send_sem=send_sem.at[n],
                recv_sem=recv_sem.at[n],
                device_id=(me, other),
                device_id_type=MESH,
            ).start()

    def spread_done(three, n):
        every = pltpu.make_async_remote_copy(
            src_ref=three,
            dst_ref=three,
            send_sem=send_sem.at[n],
            recv_sem=recv_sem.at[n],
            device_id=(me, (rank + 1) % N_TENSOR),
            device_id_type=MESH,
        )
        every.wait_send()
        every.wait_recv()

    exchange_done(send_q, qx.at[rank], QMSG, 0)
    q_part = (lambda other: qx.at[rank]), (lambda other: qx.at[other])
    spread(*q_part, 5)

    exchange_done(send_g, recv_g, MSG, 1)
    c0 = tab[me, 10]
    for j in range(2):
        left_h, left_l, right_h, right_l = [], [], [], []
        for k in range(CAP):
            chunk = recv_g[pl.ds(k, D, stride=CAP), :]
            mine = (k < c0) if j == 0 else (k >= c0)
            high, low = split(chunk)
            right_h.append(high)
            right_l.append(low)
            high, low = split(jnp.where(mine, chunk, 0.0))
            left_h.append(high)
            left_l.append(low)
        cat = functools.partial(jnp.concatenate, axis=1)
        gram[j] = dot3((cat(left_h), cat(left_l)), (cat(right_h), cat(right_l)), NT)

    def strip(x):
        return pl.ds(pl.multiple_of(96 * x, 8), 96)

    g_part = (lambda other: gram.at[:, strip(other), :]), (lambda other: xg.at[other])
    spread(*g_part, 6)

    spread_done(qx.at[pl.ds(0, 3)], 5)
    lane = lax.broadcasted_iota(jnp.int32, (D, 128), 1)
    for j in range(2):
        parts = [qx[x, pl.ds(j, D, stride=2), :] for x in range(4)]
        full = jnp.concatenate(
            [
                jnp.where(lane < 96, parts[0], pltpu.roll(parts[1], 96, 1)),
                jnp.where(lane < 64, pltpu.roll(parts[1], 96, 1), pltpu.roll(parts[2], 64, 1)),
                jnp.where(lane < 32, pltpu.roll(parts[2], 64, 1), pltpu.roll(parts[3], 32, 1)),
            ],
            axis=1,
        )
        q_hi[j], q_lo[j] = split(full)
        qt_hi[j], qt_lo[j] = split(full.T)

    exchange_done(send_s, recv_s, QMSG, 2)
    exchange_done(send_m, recv_m, MSG, 3)

    @pl.loop(0, CAP)
    def _(k):
        sel = jnp.where(k >= c0, 1, 0)
        both = jnp.concatenate(
            [recv_g[pl.ds(k, D, stride=CAP), :], recv_m[pl.ds(k, D, stride=CAP), :]], axis=1
        )
        hat = dot3((qt_hi[sel], qt_lo[sel]), split(both), NN)
        g_hat[pl.ds(k, D, stride=CAP), :] = hat[:, :128]
        m_hat[pl.ds(k, D, stride=CAP), :] = hat[:, 128:]

    spread_done(xg.at[pl.ds(0, 3)], 6)
    for j in range(2):
        total = gram[j, strip(rank), :]
        for dx in range(1, N_TENSOR):
            total = total + xg[(rank + dx) % N_TENSOR, j]
        held = recv_s[pl.ds(j, D, stride=2), :].T[:96]
        fresh = 0.95 * held + 0.05 * total
        gram_strip[j] = fresh
        power[j, strip(rank), :] = dot3(split(fresh), (q_hi[j], q_lo[j]), NN)
    p_part = (
        (lambda other: power.at[:, strip(rank), :]),
        (lambda other: power.at[:, strip(other), :]),
    )
    spread(*p_part, 7)

    for n, off, rows in ((4, 0, HEAD), (10, HEAD, TAIL)):
        exchange_done(send_v, recv_v, MSG, n, off, rows)

        @pl.loop(0, N_SHARD)
        def _(s):
            here = pl.ds(pl.multiple_of(MSG * s + off, 8), rows)
            rot = g_hat[here, :]
            ret_n[here, :] = 0.95 * recv_v[here, :] + 0.05 * rot * rot

        exchange(ret_n, back_n, MSG, 8 if off == 0 else 11, off, rows)

    @pl.loop(0, N_SHARD)
    def _(s):
        here = pl.ds(pl.multiple_of(MSG * s, 8), MSG)
        m_hat[here, :] = m_hat[here, :] / CORR_ONE / (jnp.sqrt(ret_n[here, :] / CORR_TWO) + 1e-08)

    @pl.loop(0, CAP)
    def _(k):
        sel = jnp.where(k >= c0, 1, 0)
        ret_d[pl.ds(k, D, stride=CAP), :] = dot3((q_hi[sel], q_lo[sel]), split(m_hat[pl.ds(k, D, stride=CAP), :]), NN)

    exchange(ret_d, back_d, MSG, 9)

    spread_done(power.at[:, pl.ds(0, 288), :], 7)
    for j in range(2):
        full = power[j]
        norm = jnp.sqrt(jnp.sum(full * full, keepdims=True) + 1e-06)
        power[j] = full / norm

    @pl.loop(0, NS_STEPS)
    def _(sweep):
        for j in range(2):
            frame = power[j]
            pieces = split(frame)
            square = dot3(pieces, pieces, NT)
            power[j] = 1.5 * frame - 0.5 * dot3(split(square), pieces, NN)

    for x in range(N_TENSOR):

        @pl.when(rank == x)
        def _():
            for j in range(2):
                basis_strip[j] = power[j, :, 96 * x : 96 * x + 96].T

    save_basis = local(basis_strip, basis_out, 8)
    save_gram = local(gram_strip, gram_out, 9)
    exchange_done(ret_n, back_n, MSG, 8, 0, HEAD)
    exchange_done(ret_n, back_n, MSG, 11, HEAD, TAIL)

    def write_second(here, val):
        second2[here, :] = val

    unpack(back_n, owner, tab, write_second)
    save_second = local(second2, second_out, 10)
    for save in (save_tab, save_first, save_basis, save_gram, save_second):
        save.wait()
    exchange_done(ret_d, back_d, MSG, 9)


def unpack_kernel(
    owner,
    tab,
    back_d,
    w_hbm,
    second,
    first,
    basis,
    gram,
    bias_g,
    bias_w,
    bias_m,
    bias_v,
    weight_out,
    first_out,
    second_out,
    basis_out,
    gram_out,
    bias_w_out,
    bias_m_out,
    bias_v_out,
    dv,
    w2,
    n2,
    f2,
    b2,
    s2,
    sem,
    sem_out,
):
    def copy(src, dst, n, sems=sem):
        made = pltpu.make_async_copy(src, dst, sems.at[n])
        made.start()
        return made

    load_d = copy(back_d, dv, 0)
    load_w = copy(w_hbm, w2, 1)
    passed = []
    for n, (src, held, dst) in enumerate(
        (
            (second, n2, second_out),
            (first, f2, first_out),
            (basis, b2, basis_out),
            (gram, s2, gram_out),
        )
    ):
        passed.append((copy(src, held, 2 + n), held, dst))

    moment = 0.9 * bias_m[...] + 0.1 * bias_g[...]
    moment_two = 0.95 * bias_v[...] + 0.05 * bias_g[...] * bias_g[...]
    bias_m_out[...] = moment
    bias_v_out[...] = moment_two
    bias_w_out[...] = bias_w[...] - 0.01 * (
        moment / CORR_ONE / (jnp.sqrt(moment_two / CORR_TWO) + 1e-08)
    )

    def write_weight(here, val):
        w = w2[here, :]
        w2[here, :] = w - 0.01 * (val + 0.1 * w)

    load_d.wait()
    load_w.wait()
    saves = []
    for n, (load, held, dst) in enumerate(passed):
        load.wait()
        saves.append(copy(held, dst, n, sem_out))
    unpack(dv, owner, tab, write_weight)
    saves.append(copy(w2, weight_out, 4, sem_out))
    for save in saves:
        save.wait()


def body(
    gradient,
    weight,
    first_moment,
    second_moment,
    left_basis,
    left_gram,
    owner_table,
    bias_gradient,
    bias_weight,
    bias_first,
    bias_second,
):
    smem = pl.BlockSpec(memory_space=pltpu.SMEM)
    vmem = pl.BlockSpec(memory_space=pltpu.VMEM)
    hbm = pl.BlockSpec(memory_space=pltpu.HBM)
    flat = (ROWS * LINE, 128)
    g, w, m, v = (a.reshape(flat) for a in (gradient, weight, first_moment, second_moment))
    wide = pltpu.VMEM((N_SHARD * MSG, 128), F32)
    mats = pltpu.VMEM((N_SHARD * QMSG, 128), F32)
    full = pltpu.VMEM((2, D, D), F32)
    half = pltpu.VMEM((2, D, D), BF16)
    strips = pltpu.VMEM((2, 96, D), F32)
    rows = pltpu.VMEM(flat, F32)
    rows_q = pltpu.VMEM((ROWS * QLINE, 128), F32)
    wide_out = jax.ShapeDtypeStruct((N_SHARD * MSG, 128), F32)
    flat_out = jax.ShapeDtypeStruct(flat, F32)
    strip_out = jax.ShapeDtypeStruct((2, 96, D), F32)
    tab_shape = (N_SHARD, 128)
    flat_q = (ROWS * QLINE, 1, 128)
    owner = owner_table.T
    back_d, second, first, basis, gram, tab = pl.pallas_call(
        main_kernel,
        out_shape=(
            wide_out,
            flat_out,
            flat_out,
            strip_out,
            strip_out,
            jax.ShapeDtypeStruct(tab_shape, jnp.int32),
        ),
        in_specs=[smem, vmem] + [hbm] * 5,
        out_specs=(hbm,) * 6,
        scratch_shapes=[rows] * 3
        + [rows_q] * 2
        + [pltpu.VMEM((ZERO_CHUNK + 1, ROWS, 128), F32), pltpu.VMEM((ZERO_MAT + 1, ROWS, 128), F32)]
        + [wide] * 3
        + [mats] * 2
        + [wide] * 3
        + [mats]
        + [pltpu.VMEM((N_TENSOR, N_SHARD * QMSG, 128), F32)]
        + [wide] * 2
        + [full, pltpu.VMEM((N_TENSOR, 2, 96, D), F32), full]
        + [half] * 4
        + [wide] * 2
        + [strips] * 2
        + [wide, rows]
        + [pltpu.VMEM(tab_shape, jnp.int32), pltpu.SMEM(tab_shape, jnp.int32)]
        + [pltpu.SemaphoreType.DMA((n,)) for n in (11, 12, 12, 12)],
        compiler_params=pltpu.CompilerParams(
            collective_id=0, has_side_effects=True, vmem_limit_bytes=VMEM_ALL
        ),
        name="exchange_and_rotate",
    )(owner, owner, g, m, v, left_basis.reshape(flat_q), left_gram.reshape(flat_q))
    bias_out = jax.ShapeDtypeStruct(bias_gradient.shape, F32)
    outs = pl.pallas_call(
        unpack_kernel,
        out_shape=(flat_out,) * 3 + (strip_out,) * 2 + (bias_out,) * 3,
        in_specs=[smem] * 2 + [hbm] * 6 + [vmem] * 4,
        out_specs=(hbm,) * 5 + (vmem,) * 3,
        scratch_shapes=[wide]
        + [rows] * 3
        + [strips] * 2
        + [pltpu.SemaphoreType.DMA((6,)), pltpu.SemaphoreType.DMA((5,))],
        compiler_params=pltpu.CompilerParams(vmem_limit_bytes=VMEM_ALL),
        name="unpack",
    )(
        owner,
        tab,
        back_d,
        w,
        second,
        first,
        basis,
        gram,
        bias_gradient,
        bias_weight,
        bias_first,
        bias_second,
    )
    weight_new, first_new, second_new, basis_new, gram_new = outs[:5]
    return (
        weight_new.reshape(weight.shape),
        first_new.reshape(weight.shape),
        second_new.reshape(weight.shape),
        basis_new.transpose(0, 2, 1)[None],
        gram_new.transpose(0, 2, 1)[None],
        *outs[5:],
    )


def solution(mesh):
    rows = P("shard", "tensor", None)
    flat = P(("shard", "tensor"))
    owned = P("shard", None, None, "tensor")
    return jax.shard_map(
        body,
        mesh=mesh,
        in_specs=(rows,) * 6 + (P(),) + (flat,) * 4,
        out_specs=(rows,) * 3 + (owned,) * 2 + (flat,) * 3,
        check_vma=False,
    )
```

```python
import functools

import jax
import jax.numpy as jnp
from jax import lax
from jax.experimental import pallas as pl
from jax.experimental.pallas import tpu as pltpu
from jax.sharding import PartitionSpec as P

MESH = pl.DeviceIdType.MESH
STEP = 10
NS_STEPS = 5
N_SHARD = 32
N_TENSOR = 4
D = 384
ROWS = 12
PAIRS = 6
TYPE_TILES = (3, 1, 4, 4, 6)
TYPE_START = (0, 3, 4, 8, 12)
TYPE_CHUNKS = (3, 1, 3, 3, 5)
CHUNK_START = (0, 3, 4, 7, 10)
CAP = 6
MSG = ROWS * CAP
QMSG = ROWS * 2
LINE = 162
QLINE = 45
ZERO_CHUNK = 180
ZERO_MAT = 60
CORR_ONE = 1.0 - 0.9**STEP
CORR_TWO = 1.0 - 0.95**STEP
NO_CODE = (ZERO_MAT << 16) + (ZERO_CHUNK << 8)
HEAD = 48
TAIL = 24
VMEM_ALL = 67043328
F32 = jnp.float32


def send_order():
    rings = (
        ((2, 2),),
        ((1, 2), (2, 1), (3, 2), (2, 3)),
        ((1, 1), (3, 3), (1, 3), (3, 1)),
        ((2, 0), (0, 2)),
        ((1, 0), (0, 1), (3, 0), (0, 3)),
    )
    order = [(dy, dz, dc) for ring in rings for dc in range(2) for dy, dz in ring]
    return order + [(0, 0, 1)]


ORDER = send_order()
BF16 = jnp.bfloat16


def table_of(owners):
    group = lax.broadcasted_iota(jnp.int32, (N_SHARD, 12), 0)
    layer = lax.broadcasted_iota(jnp.int32, (N_SHARD, 12), 1)
    low = jnp.full((N_SHARD, 12), NO_CODE, jnp.int32)
    high = jnp.full((N_SHARD, 12), -1, jnp.int32)
    for kind in range(5):
        code = ((5 * layer + kind) << 16) + ((15 * layer + CHUNK_START[kind]) << 8)
        code = code + TYPE_CHUNKS[kind]
        hit = owners[kind : kind + 1, :] == group
        low = jnp.minimum(low, jnp.where(hit, code, NO_CODE))
        high = jnp.maximum(high, jnp.where(hit, code, -1))
    first = jnp.min(low, axis=1, keepdims=True)
    second = jnp.max(high, axis=1, keepdims=True)
    second = jnp.where((second < 0) | (second == first), NO_CODE, second)
    c0, c1 = first & 255, second & 255
    at0, at1 = (first >> 8) & 255, (second >> 8) & 255
    k = lax.broadcasted_iota(jnp.int32, (N_SHARD, 128), 1)
    rest = jnp.where(k - c0 < c1, at1 + k - c0, ZERO_CHUNK)
    table = jnp.where(k < c0, at0 + k, rest)
    table = jnp.where(k == 8, first >> 16, table)
    table = jnp.where(k == 9, second >> 16, table)
    return jnp.where(k == 10, c0, table)


def place_of(owner, tab, pair, mat):
    group = owner[mat % 5, 2 * pair + mat // 5]
    base = jnp.where(tab[group, 8] == 10 * pair + mat, 0, tab[group, 10])
    return MSG * group + base


def align_rows(src, dst):
    lane = lax.broadcasted_iota(jnp.int32, (ROWS, 128), 1)

    @pl.loop(0, PAIRS)
    def _(pair):
        for half in range(2):
            for kind in range(5):
                for j in range(TYPE_CHUNKS[kind]):
                    col = 1728 * half + 96 * TYPE_START[kind] + 128 * j
                    at, shift = divmod(col, 128)
                    valid = min(128, 96 * TYPE_TILES[kind] - 128 * j)
                    val = src[pl.ds(27 * pair + at, ROWS, stride=LINE), :]
                    if shift:
                        val = pltpu.roll(val, 128 - shift, 1)
                        if valid > 128 - shift:
                            nxt = src[pl.ds(27 * pair + at + 1, ROWS, stride=LINE), :]
                            nxt = pltpu.roll(nxt, 128 - shift, 1)
                            val = jnp.where(lane < 128 - shift, val, nxt)
                    if valid < 128:
                        val = jnp.where(lane < valid, val, 0.0)
                    dst[30 * pair + 15 * half + CHUNK_START[kind] + j] = val


def align_mats(src, dst):
    lane = lax.broadcasted_iota(jnp.int32, (ROWS, 128), 1)

    @pl.loop(0, 3)
    def _(step):
        for part in range(20):
            at, shift = divmod(96 * part, 128)
            val = src[pl.ds(15 * step + at, ROWS, stride=QLINE), :]
            if shift:
                val = pltpu.roll(val, 128 - shift, 1)
                if 96 > 128 - shift:
                    nxt = src[pl.ds(15 * step + at + 1, ROWS, stride=QLINE), :]
                    nxt = pltpu.roll(nxt, 128 - shift, 1)
                    val = jnp.where(lane < 128 - shift, val, nxt)
            dst[20 * step + part] = jnp.where(lane < 96, val, 0.0)


def split(x):
    high = x.astype(BF16)
    return high, (x - high.astype(F32)).astype(BF16)


def dot3(a, b, dims):
    ah, al = a
    bh, bl = b
    dot = functools.partial(
        lax.dot_general, dimension_numbers=(dims, ((), ())), preferred_element_type=F32
    )
    return dot(ah, bh) + (dot(ah, bl) + dot(al, bh))


NN = ((1,), (0,))
NT = ((1,), (1,))


def out_pieces():
    owner_of = []
    for half in range(2):
        for kind in range(5):
            start = 1728 * half + 96 * TYPE_START[kind]
            for c in range(96 * TYPE_TILES[kind]):
                owner_of.append((5 * half + kind, start))
    table = []
    for chunk in range(27):
        pieces = []
        for lane in range(128):
            col = 128 * chunk + lane
            mat, start = owner_of[col]
            j, src = divmod(col - start, 128)
            key = (mat, j, (lane - src) % 128)
            if pieces and pieces[-1][0] == key:
                pieces[-1][2] = lane + 1
            else:
                pieces.append([key, lane, lane + 1])
        table.append(pieces)
    return table


def unpack(back, place, write, first=0, last=PAIRS):
    lane = lax.broadcasted_iota(jnp.int32, (ROWS, 128), 1)
    table = out_pieces()

    @pl.loop(first, last)
    def _(pair):
        for chunk in range(27):
            out = None
            for (mat, j, turn), _lo, hi in reversed(table[chunk]):
                val = back[pl.ds(place[10 * pair + mat] + j, ROWS, stride=CAP), :]
                if turn:
                    val = pltpu.roll(val, turn, 1)
                out = val if out is None else jnp.where(lane < hi, val, out)
            write(pl.ds(27 * pair + chunk, ROWS, stride=LINE), out)


def main_kernel(
    owner,
    owners,
    g_hbm,
    m_hbm,
    v_hbm,
    q_hbm,
    s_hbm,
    back_d,
    second_out,
    first_out,
    basis_out,
    gram_out,
    places_out,
    g2,
    m2,
    v2,
    q2,
    s2,
    lined,
    lined_q,
    send_g,
    send_m,
    send_v,
    send_q,
    send_s,
    recv_g,
    recv_m,
    recv_v,
    recv_s,
    qx,
    ret_d,
    ret_n,
    gram,
    xg,
    power,
    q_hi,
    q_lo,
    qt_hi,
    qt_lo,
    g_hat,
    m_hat,
    gram_strip,
    basis_strip,
    back_n,
    second2,
    tab_vec,
    tab,
    places,
    in_sem,
    send_sem,
    recv_sem,
    own_sem,
):
    me = lax.axis_index("shard")
    rank = lax.axis_index("tensor")
    my_y, my_z, my_c = me // 8, (me // 2) % 4, me % 2

    def peer(offset):
        dy, dz, dc = offset
        return ((my_y + dy) % 4) * 8 + ((my_z + dz) % 4) * 2 + (my_c + dc) % 2

    def local(src, dst, n):
        made = pltpu.make_async_copy(src, dst, in_sem.at[n])
        made.start()
        return made

    load_q = local(q_hbm.at[:, 0, :], q2, 0)
    barrier = pltpu.get_barrier_semaphore()

    for offset in ORDER:
        pl.semaphore_signal(
            barrier, inc=1, device_id=(peer(offset), rank), device_id_type=MESH
        )

    for dx in range(1, N_TENSOR):
        pl.semaphore_signal(
            barrier, inc=1, device_id=(me, (rank + dx) % N_TENSOR), device_id_type=MESH
        )

    load_g = local(g_hbm, g2, 1)
    load_s = local(s_hbm.at[:, 0, :], s2, 2)
    load_m = local(m_hbm, m2, 3)
    load_v = local(v_hbm, v2, 4)
    tab_vec[...] = table_of(owners[...])
    load_tab = local(tab_vec, tab, 5)

    lined[ZERO_CHUNK] = jnp.zeros((ROWS, 128), F32)
    lined_q[ZERO_MAT] = jnp.zeros((ROWS, 128), F32)

    def own_copy(send, recv, unit, off, rows, n):
        own = pl.ds(pl.multiple_of(me * unit + off, 8), rows)
        return pltpu.make_async_copy(send.at[own], recv.at[own], own_sem.at[n])

    def exchange(send, recv, unit, n, off=0, rows=None):
        rows = unit if rows is None else rows

        for offset in ORDER:
            dst = peer(offset)
            pltpu.make_async_remote_copy(
                src_ref=send.at[pl.ds(pl.multiple_of(dst * unit + off, 8), rows)],
                dst_ref=recv.at[pl.ds(pl.multiple_of(me * unit + off, 8), rows)],
                send_sem=send_sem.at[n],
                recv_sem=recv_sem.at[n],
                device_id=(dst, rank),
                device_id_type=MESH,
            ).start()

        own_copy(send, recv, unit, off, rows, n).start()

    def exchange_done(send, recv, unit, n, off=0, rows=None):
        rows = unit if rows is None else rows
        whole = pl.ds(0, (N_SHARD - 1) * rows)
        every = pltpu.make_async_remote_copy(
            src_ref=send.at[whole],
            dst_ref=recv.at[whole],
            send_sem=send_sem.at[n],
            recv_sem=recv_sem.at[n],
            device_id=((me + 1) % N_SHARD, rank),
            device_id_type=MESH,
        )
        own_copy(send, recv, unit, off, rows, n).wait()
        every.wait_send()
        every.wait_recv()

    def pack(lines, send):
        @pl.loop(0, N_SHARD)
        def _(d):
            for k in range(CAP):
                send[pl.ds(MSG * d + k, ROWS, stride=CAP), :] = lines[tab[d, k]]

    def pack_mats(lines, send):
        @pl.loop(0, N_SHARD)
        def _(d):
            for j in range(2):
                send[pl.ds(QMSG * d + j, ROWS, stride=2), :] = lines[tab[d, 8 + j]]

    load_q.wait()
    align_mats(q2, lined_q)
    load_tab.wait()
    pack_mats(lined_q, send_q)
    pl.semaphore_wait(barrier, N_SHARD - 1 + N_TENSOR - 1)
    exchange(send_q, qx.at[rank], QMSG, 0)

    load_g.wait()
    align_rows(g2, lined)
    pack(lined, send_g)
    exchange(send_g, recv_g, MSG, 1)

    load_s.wait()
    align_mats(s2, lined_q)
    pack_mats(lined_q, send_s)
    exchange(send_s, recv_s, QMSG, 2)

    load_m.wait()
    m2[...] = 0.9 * m2[...] + 0.1 * g2[...]
    save_first = local(m2, first_out, 7)
    align_rows(m2, lined)
    pack(lined, send_m)
    exchange(send_m, recv_m, MSG, 3)

    load_v.wait()
    align_rows(v2, lined)
    pack(lined, send_v)
    exchange(send_v, recv_v, MSG, 4, 0, HEAD)
    exchange(send_v, recv_v, MSG, 10, HEAD, TAIL)

    @pl.loop(0, PAIRS)
    def _(pair):
        for mat in range(10):
            places[10 * pair + mat] = place_of(owner, tab, pair, mat)

    save_places = local(places, places_out, 6)

    def spread(src_of, dst_of, n):
        for dx in range(1, N_TENSOR):
            other = (rank + dx) % N_TENSOR
            pltpu.make_async_remote_copy(
                src_ref=src_of(other),
                dst_ref=dst_of(rank),
                send_sem=send_sem.at[n],
                recv_sem=recv_sem.at[n],
                device_id=(me, other),
                device_id_type=MESH,
            ).start()

    def spread_done(three, n):
        every = pltpu.make_async_remote_copy(
            src_ref=three,
            dst_ref=three,
            send_sem=send_sem.at[n],
            recv_sem=recv_sem.at[n],
            device_id=(me, (rank + 1) % N_TENSOR),
            device_id_type=MESH,
        )
        every.wait_send()
        every.wait_recv()

    exchange_done(send_q, qx.at[rank], QMSG, 0)
    q_part = (lambda other: qx.at[rank]), (lambda other: qx.at[other])
    spread(*q_part, 5)

    exchange_done(send_g, recv_g, MSG, 1)
    c0 = tab[me, 10]
    for j in range(2):
        left_h, left_l, right_h, right_l = [], [], [], []
        for k in range(CAP):
            chunk = recv_g[pl.ds(k, D, stride=CAP), :]
            mine = (k < c0) if j == 0 else (k >= c0)
            high, low = split(chunk)
            right_h.append(high)
            right_l.append(low)
            high, low = split(jnp.where(mine, chunk, 0.0))
            left_h.append(high)
            left_l.append(low)
        cat = functools.partial(jnp.concatenate, axis=1)
        gram[j] = dot3((cat(left_h), cat(left_l)), (cat(right_h), cat(right_l)), NT)

    def strip(x):
        return pl.ds(pl.multiple_of(96 * x, 8), 96)

    g_part = (lambda other: gram.at[:, strip(other), :]), (lambda other: xg.at[other])
    spread(*g_part, 6)

    spread_done(qx.at[pl.ds(0, 3)], 5)
    lane = lax.broadcasted_iota(jnp.int32, (D, 128), 1)
    for j in range(2):
        parts = [qx[x, pl.ds(j, D, stride=2), :] for x in range(4)]
        full = jnp.concatenate(
            [
                jnp.where(lane < 96, parts[0], pltpu.roll(parts[1], 96, 1)),
                jnp.where(lane < 64, pltpu.roll(parts[1], 96, 1), pltpu.roll(parts[2], 64, 1)),
                jnp.where(lane < 32, pltpu.roll(parts[2], 64, 1), pltpu.roll(parts[3], 32, 1)),
            ],
            axis=1,
        )
        q_hi[j], q_lo[j] = split(full)
        qt_hi[j], qt_lo[j] = split(full.T)

    exchange_done(send_s, recv_s, QMSG, 2)
    exchange_done(send_m, recv_m, MSG, 3)

    @pl.loop(0, CAP)
    def _(k):
        sel = jnp.where(k >= c0, 1, 0)
        both = jnp.concatenate(
            [recv_g[pl.ds(k, D, stride=CAP), :], recv_m[pl.ds(k, D, stride=CAP), :]], axis=1
        )
        hat = dot3((qt_hi[sel], qt_lo[sel]), split(both), NN)
        g_hat[pl.ds(k, D, stride=CAP), :] = hat[:, :128]
        m_hat[pl.ds(k, D, stride=CAP), :] = hat[:, 128:]

    spread_done(xg.at[pl.ds(0, 3)], 6)
    for j in range(2):
        total = gram[j, strip(rank), :]
        for dx in range(1, N_TENSOR):
            total = total + xg[(rank + dx) % N_TENSOR, j]
        held = recv_s[pl.ds(j, D, stride=2), :].T[:96]
        fresh = 0.95 * held + 0.05 * total
        gram_strip[j] = fresh
        power[j, strip(rank), :] = dot3(split(fresh), (q_hi[j], q_lo[j]), NN)
    p_part = (
        (lambda other: power.at[:, strip(rank), :]),
        (lambda other: power.at[:, strip(other), :]),
    )
    spread(*p_part, 7)

    for n, off, rows in ((4, 0, HEAD), (10, HEAD, TAIL)):
        exchange_done(send_v, recv_v, MSG, n, off, rows)

        @pl.loop(0, N_SHARD)
        def _(s):
            here = pl.ds(pl.multiple_of(MSG * s + off, 8), rows)
            rot = g_hat[here, :]
            ret_n[here, :] = 0.95 * recv_v[here, :] + 0.05 * rot * rot

        exchange(ret_n, back_n, MSG, 8 if off == 0 else 11, off, rows)

    @pl.loop(0, N_SHARD)
    def _(s):
        here = pl.ds(pl.multiple_of(MSG * s, 8), MSG)
        m_hat[here, :] = m_hat[here, :] / CORR_ONE / (jnp.sqrt(ret_n[here, :] / CORR_TWO) + 1e-08)

    @pl.loop(0, CAP)
    def _(k):
        sel = jnp.where(k >= c0, 1, 0)
        ret_d[pl.ds(k, D, stride=CAP), :] = dot3((q_hi[sel], q_lo[sel]), split(m_hat[pl.ds(k, D, stride=CAP), :]), NN)

    exchange(ret_d, back_d, MSG, 9)

    spread_done(power.at[:, pl.ds(0, 288), :], 7)
    for j in range(2):
        full = power[j]
        norm = jnp.sqrt(jnp.sum(full * full, keepdims=True) + 1e-06)
        power[j] = full / norm

    @pl.loop(0, NS_STEPS)
    def _(sweep):
        for j in range(2):
            frame = power[j]
            pieces = split(frame)
            square = dot3(pieces, pieces, NT)
            power[j] = 1.5 * frame - 0.5 * dot3(split(square), pieces, NN)

    for x in range(N_TENSOR):

        @pl.when(rank == x)
        def _():
            for j in range(2):
                basis_strip[j] = power[j, :, 96 * x : 96 * x + 96].T

    save_basis = local(basis_strip, basis_out, 8)
    save_gram = local(gram_strip, gram_out, 9)
    exchange_done(ret_n, back_n, MSG, 8, 0, HEAD)
    exchange_done(ret_n, back_n, MSG, 11, HEAD, TAIL)

    def write_second(here, val):
        second2[here, :] = val

    unpack(back_n, places, write_second)
    save_second = local(second2, second_out, 10)
    for save in (save_places, save_first, save_basis, save_gram, save_second):
        save.wait()
    exchange_done(ret_d, back_d, MSG, 9)


def unpack_kernel(
    places,
    back_d,
    w_hbm,
    second,
    first,
    basis,
    gram,
    bias_g,
    bias_w,
    bias_m,
    bias_v,
    weight_out,
    first_out,
    second_out,
    basis_out,
    gram_out,
    bias_w_out,
    bias_m_out,
    bias_v_out,
    place,
    dv,
    w2,
    n2,
    f2,
    b2,
    s2,
    bias,
    sem,
    sem_out,
):
    def copy(src, dst, n, sems=sem):
        made = pltpu.make_async_copy(src, dst, sems.at[n])
        made.start()
        return made

    load_p = copy(places, place, 0)
    load_d = copy(back_d, dv, 1)
    load_w = copy(w_hbm, w2, 2)
    loads = [
        copy(src, bias.at[n, 0], 3 + n) for n, src in enumerate((bias_g, bias_w, bias_m, bias_v))
    ]
    passed = []
    for n, (src, held, dst) in enumerate(
        (
            (second, n2, second_out),
            (first, f2, first_out),
            (basis, b2, basis_out),
            (gram, s2, gram_out),
        )
    ):
        passed.append((copy(src, held, 7 + n), held, dst))

    for load in loads:
        load.wait()
    moment = 0.9 * bias[2] + 0.1 * bias[0]
    moment_two = 0.95 * bias[3] + 0.05 * bias[0] * bias[0]
    bias[5] = moment
    bias[6] = moment_two
    bias[4] = bias[1] - 0.01 * (moment / CORR_ONE / (jnp.sqrt(moment_two / CORR_TWO) + 1e-08))
    saves = [
        copy(bias.at[4 + n, 0], dst, n, sem_out)
        for n, dst in enumerate((bias_w_out, bias_m_out, bias_v_out))
    ]

    def write_weight(here, val):
        w = w2[here, :]
        w2[here, :] = w - 0.01 * (val + 0.1 * w)

    load_p.wait()
    load_d.wait()
    load_w.wait()
    unpack(dv, place, write_weight, 0, PAIRS // 2)
    for n, (load, held, dst) in enumerate(passed):
        load.wait()
        saves.append(copy(held, dst, 3 + n, sem_out))
    unpack(dv, place, write_weight, PAIRS // 2, PAIRS)
    saves.append(copy(w2, weight_out, 7, sem_out))
    for save in saves:
        save.wait()


def body(
    gradient,
    weight,
    first_moment,
    second_moment,
    left_basis,
    left_gram,
    owner_table,
    bias_gradient,
    bias_weight,
    bias_first,
    bias_second,
):
    smem = pl.BlockSpec(memory_space=pltpu.SMEM)
    vmem = pl.BlockSpec(memory_space=pltpu.VMEM)
    hbm = pl.BlockSpec(memory_space=pltpu.HBM)
    flat = (ROWS * LINE, 128)
    g, w, m, v = (a.reshape(flat) for a in (gradient, weight, first_moment, second_moment))
    wide = pltpu.VMEM((N_SHARD * MSG, 128), F32)
    mats = pltpu.VMEM((N_SHARD * QMSG, 128), F32)
    full = pltpu.VMEM((2, D, D), F32)
    half = pltpu.VMEM((2, D, D), BF16)
    strips = pltpu.VMEM((2, 96, D), F32)
    rows = pltpu.VMEM(flat, F32)
    rows_q = pltpu.VMEM((ROWS * QLINE, 128), F32)
    wide_out = jax.ShapeDtypeStruct((N_SHARD * MSG, 128), F32)
    flat_out = jax.ShapeDtypeStruct(flat, F32)
    strip_out = jax.ShapeDtypeStruct((2, 96, D), F32)
    tab_shape = (N_SHARD, 128)
    flat_q = (ROWS * QLINE, 1, 128)
    owner = owner_table.T
    back_d, second, first, basis, gram, places = pl.pallas_call(
        main_kernel,
        out_shape=(
            wide_out,
            flat_out,
            flat_out,
            strip_out,
            strip_out,
            jax.ShapeDtypeStruct((128,), jnp.int32),
        ),
        in_specs=[smem, vmem] + [hbm] * 5,
        out_specs=(hbm,) * 6,
        scratch_shapes=[rows] * 3
        + [rows_q] * 2
        + [pltpu.VMEM((ZERO_CHUNK + 1, ROWS, 128), F32), pltpu.VMEM((ZERO_MAT + 1, ROWS, 128), F32)]
        + [wide] * 3
        + [mats] * 2
        + [wide] * 3
        + [mats]
        + [pltpu.VMEM((N_TENSOR, N_SHARD * QMSG, 128), F32)]
        + [wide] * 2
        + [full, pltpu.VMEM((N_TENSOR, 2, 96, D), F32), full]
        + [half] * 4
        + [wide] * 2
        + [strips] * 2
        + [wide, rows]
        + [pltpu.VMEM(tab_shape, jnp.int32), pltpu.SMEM(tab_shape, jnp.int32)]
        + [pltpu.SMEM((128,), jnp.int32)]
        + [pltpu.SemaphoreType.DMA((n,)) for n in (11, 12, 12, 12)],
        compiler_params=pltpu.CompilerParams(
            collective_id=0, has_side_effects=True, vmem_limit_bytes=VMEM_ALL
        ),
        name="exchange_and_rotate",
    )(owner, owner, g, m, v, left_basis.reshape(flat_q), left_gram.reshape(flat_q))
    bias_out = jax.ShapeDtypeStruct(bias_gradient.shape, F32)
    outs = pl.pallas_call(
        unpack_kernel,
        out_shape=(flat_out,) * 3 + (strip_out,) * 2 + (bias_out,) * 3,
        in_specs=[hbm] * 11,
        out_specs=(hbm,) * 8,
        scratch_shapes=[pltpu.SMEM((128,), jnp.int32), wide]
        + [rows] * 3
        + [strips] * 2
        + [pltpu.VMEM((7, 1) + bias_gradient.shape, F32)]
        + [pltpu.SemaphoreType.DMA((11,)), pltpu.SemaphoreType.DMA((8,))],
        compiler_params=pltpu.CompilerParams(vmem_limit_bytes=VMEM_ALL),
        name="unpack",
    )(
        places,
        back_d,
        w,
        second,
        first,
        basis,
        gram,
        bias_gradient,
        bias_weight,
        bias_first,
        bias_second,
    )
    weight_new, first_new, second_new, basis_new, gram_new = outs[:5]
    return (
        weight_new.reshape(weight.shape),
        first_new.reshape(weight.shape),
        second_new.reshape(weight.shape),
        basis_new.transpose(0, 2, 1)[None],
        gram_new.transpose(0, 2, 1)[None],
        *outs[5:],
    )


def solution(mesh):
    rows = P("shard", "tensor", None)
    flat = P(("shard", "tensor"))
    owned = P("shard", None, None, "tensor")
    return jax.shard_map(
        body,
        mesh=mesh,
        in_specs=(rows,) * 6 + (P(),) + (flat,) * 4,
        out_specs=(rows,) * 3 + (owned,) * 2 + (flat,) * 3,
        check_vma=False,
    )
```

```python
import functools

import jax
import jax.numpy as jnp
from jax import lax
from jax.experimental import pallas as pl
from jax.experimental.pallas import tpu as pltpu
from jax.sharding import PartitionSpec as P

MESH = pl.DeviceIdType.MESH
STEP = 10
NS_STEPS = 5
N_SHARD = 32
N_TENSOR = 4
D = 384
ROWS = 12
PAIRS = 6
TYPE_TILES = (3, 1, 4, 4, 6)
TYPE_START = (0, 3, 4, 8, 12)
TYPE_CHUNKS = (3, 1, 3, 3, 5)
CHUNK_START = (0, 3, 4, 7, 10)
CAP = 6
MSG = ROWS * CAP
QMSG = ROWS * 3
LINE = 162
QLINE = 45
ZERO_CHUNK = 180
ZERO_MAT = 60
CORR_ONE = 1.0 - 0.9**STEP
CORR_TWO = 1.0 - 0.95**STEP
NO_CODE = (ZERO_MAT << 16) + (ZERO_CHUNK << 8)
HEAD = 48
TAIL = 24
VMEM_ALL = 67043328
F32 = jnp.float32


def send_order():
    rings = (
        ((2, 2),),
        ((1, 2), (2, 1), (3, 2), (2, 3)),
        ((1, 1), (3, 3), (1, 3), (3, 1)),
        ((2, 0), (0, 2)),
        ((1, 0), (0, 1), (3, 0), (0, 3)),
    )
    order = [(dy, dz, dc) for ring in rings for dc in range(2) for dy, dz in ring]
    return order + [(0, 0, 1)]


ORDER = send_order()
BF16 = jnp.bfloat16


def table_of(owners):
    group = lax.broadcasted_iota(jnp.int32, (N_SHARD, 12), 0)
    layer = lax.broadcasted_iota(jnp.int32, (N_SHARD, 12), 1)
    low = jnp.full((N_SHARD, 12), NO_CODE, jnp.int32)
    high = jnp.full((N_SHARD, 12), -1, jnp.int32)
    for kind in range(5):
        code = ((5 * layer + kind) << 16) + ((15 * layer + CHUNK_START[kind]) << 8)
        code = code + TYPE_CHUNKS[kind]
        hit = owners[kind : kind + 1, :] == group
        low = jnp.minimum(low, jnp.where(hit, code, NO_CODE))
        high = jnp.maximum(high, jnp.where(hit, code, -1))
    first = jnp.min(low, axis=1, keepdims=True)
    second = jnp.max(high, axis=1, keepdims=True)
    second = jnp.where((second < 0) | (second == first), NO_CODE, second)
    c0, c1 = first & 255, second & 255
    at0, at1 = (first >> 8) & 255, (second >> 8) & 255
    k = lax.broadcasted_iota(jnp.int32, (N_SHARD, 128), 1)
    rest = jnp.where(k - c0 < c1, at1 + k - c0, ZERO_CHUNK)
    table = jnp.where(k < c0, at0 + k, rest)
    table = jnp.where(k == 8, first >> 16, table)
    table = jnp.where(k == 9, second >> 16, table)
    return jnp.where(k == 10, c0, table)


def place_of(owner, tab, pair, mat):
    group = owner[mat % 5, 2 * pair + mat // 5]
    base = jnp.where(tab[group, 8] == 10 * pair + mat, 0, tab[group, 10])
    return MSG * group + base


def align_rows(src, dst):
    lane = lax.broadcasted_iota(jnp.int32, (ROWS, 128), 1)

    @pl.loop(0, PAIRS)
    def _(pair):
        for half in range(2):
            for kind in range(5):
                for j in range(TYPE_CHUNKS[kind]):
                    col = 1728 * half + 96 * TYPE_START[kind] + 128 * j
                    at, shift = divmod(col, 128)
                    valid = min(128, 96 * TYPE_TILES[kind] - 128 * j)
                    val = src[pl.ds(27 * pair + at, ROWS, stride=LINE), :]
                    if shift:
                        val = pltpu.roll(val, 128 - shift, 1)
                        if valid > 128 - shift:
                            nxt = src[pl.ds(27 * pair + at + 1, ROWS, stride=LINE), :]
                            nxt = pltpu.roll(nxt, 128 - shift, 1)
                            val = jnp.where(lane < 128 - shift, val, nxt)
                    if valid < 128:
                        val = jnp.where(lane < valid, val, 0.0)
                    dst[30 * pair + 15 * half + CHUNK_START[kind] + j] = val


def align_mats(src, dst):
    lane = lax.broadcasted_iota(jnp.int32, (ROWS, 128), 1)

    @pl.loop(0, 3)
    def _(step):
        for part in range(20):
            at, shift = divmod(96 * part, 128)
            val = src[pl.ds(15 * step + at, ROWS, stride=QLINE), :]
            if shift:
                val = pltpu.roll(val, 128 - shift, 1)
                if 96 > 128 - shift:
                    nxt = src[pl.ds(15 * step + at + 1, ROWS, stride=QLINE), :]
                    nxt = pltpu.roll(nxt, 128 - shift, 1)
                    val = jnp.where(lane < 128 - shift, val, nxt)
            dst[20 * step + part] = jnp.where(lane < 96, val, 0.0)


def split(x):
    high = x.astype(BF16)
    return high, (x - high.astype(F32)).astype(BF16)


def dot3(a, b, dims):
    ah, al = a
    bh, bl = b
    dot = functools.partial(
        lax.dot_general, dimension_numbers=(dims, ((), ())), preferred_element_type=F32
    )
    return dot(ah, bh) + (dot(ah, bl) + dot(al, bh))


NN = ((1,), (0,))
NT = ((1,), (1,))


def out_pieces():
    owner_of = []
    for half in range(2):
        for kind in range(5):
            start = 1728 * half + 96 * TYPE_START[kind]
            for c in range(96 * TYPE_TILES[kind]):
                owner_of.append((5 * half + kind, start))
    table = []
    for chunk in range(27):
        pieces = []
        for lane in range(128):
            col = 128 * chunk + lane
            mat, start = owner_of[col]
            j, src = divmod(col - start, 128)
            key = (mat, j, (lane - src) % 128)
            if pieces and pieces[-1][0] == key:
                pieces[-1][2] = lane + 1
            else:
                pieces.append([key, lane, lane + 1])
        table.append(pieces)
    return table


def unpack(back, place, write, first=0, last=PAIRS):
    lane = lax.broadcasted_iota(jnp.int32, (ROWS, 128), 1)
    table = out_pieces()

    @pl.loop(first, last)
    def _(pair):
        for chunk in range(27):
            out = None
            for (mat, j, turn), _lo, hi in reversed(table[chunk]):
                val = back[pl.ds(place[10 * pair + mat] + j, ROWS, stride=CAP), :]
                if turn:
                    val = pltpu.roll(val, turn, 1)
                out = val if out is None else jnp.where(lane < hi, val, out)
            write(pl.ds(27 * pair + chunk, ROWS, stride=LINE), out)


def main_kernel(
    owner_hbm,
    g_hbm,
    m_hbm,
    v_hbm,
    q_hbm,
    s_hbm,
    back_d,
    second_out,
    first_out,
    basis_out,
    gram_out,
    places_out,
    g2,
    m2,
    v2,
    q2,
    s2,
    lined,
    lined_q,
    lined_s,
    send_g,
    send_m,
    send_v,
    send_qs,
    recv_g,
    recv_m,
    recv_v,
    recv_qs,
    nat,
    qx,
    ret_d,
    ret_n,
    gram,
    xg,
    power,
    q_hi,
    q_lo,
    qt_hi,
    qt_lo,
    g_hat,
    m_hat,
    gram_strip,
    basis_strip,
    back_n,
    second2,
    owner,
    owners,
    tab_vec,
    tab,
    places,
    in_sem,
    send_sem,
    recv_sem,
    own_sem,
):
    me = lax.axis_index("shard")
    rank = lax.axis_index("tensor")
    my_y, my_z, my_c = me // 8, (me // 2) % 4, me % 2

    def peer(offset):
        dy, dz, dc = offset
        return ((my_y + dy) % 4) * 8 + ((my_z + dz) % 4) * 2 + (my_c + dc) % 2

    def local(src, dst, n):
        made = pltpu.make_async_copy(src, dst, in_sem.at[n])
        made.start()
        return made

    load_owner = local(owner_hbm, owner, 11)
    load_owners = local(owner_hbm, owners, 12)
    load_q = local(q_hbm.at[:, 0, :], q2, 0)
    load_s = local(s_hbm.at[:, 0, :], s2, 2)
    barrier = pltpu.get_barrier_semaphore()

    for offset in ORDER:
        pl.semaphore_signal(
            barrier, inc=1, device_id=(peer(offset), rank), device_id_type=MESH
        )

    for dx in range(1, N_TENSOR):
        pl.semaphore_signal(
            barrier, inc=1, device_id=(me, (rank + dx) % N_TENSOR), device_id_type=MESH
        )

    load_g = local(g_hbm, g2, 1)
    load_m = local(m_hbm, m2, 3)
    load_v = local(v_hbm, v2, 4)
    load_owner.wait()
    load_owners.wait()
    tab_vec[...] = table_of(owners[...])
    load_tab = local(tab_vec, tab, 5)

    lined[ZERO_CHUNK] = jnp.zeros((ROWS, 128), F32)
    lined_q[ZERO_MAT] = jnp.zeros((ROWS, 128), F32)
    lined_s[ZERO_MAT] = jnp.zeros((ROWS, 128), F32)

    def own_copy(send, recv, unit, off, rows, n):
        own = pl.ds(pl.multiple_of(me * unit + off, 8), rows)
        return pltpu.make_async_copy(send.at[own], recv.at[own], own_sem.at[n])

    def exchange(send, recv, unit, n, off=0, rows=None):
        rows = unit if rows is None else rows

        for offset in ORDER:
            dst = peer(offset)
            pltpu.make_async_remote_copy(
                src_ref=send.at[pl.ds(pl.multiple_of(dst * unit + off, 8), rows)],
                dst_ref=recv.at[pl.ds(pl.multiple_of(me * unit + off, 8), rows)],
                send_sem=send_sem.at[n],
                recv_sem=recv_sem.at[n],
                device_id=(dst, rank),
                device_id_type=MESH,
            ).start()

        own_copy(send, recv, unit, off, rows, n).start()

    def exchange_done(send, recv, unit, n, off=0, rows=None):
        rows = unit if rows is None else rows
        whole = pl.ds(0, (N_SHARD - 1) * rows)
        every = pltpu.make_async_remote_copy(
            src_ref=send.at[whole],
            dst_ref=recv.at[whole],
            send_sem=send_sem.at[n],
            recv_sem=recv_sem.at[n],
            device_id=((me + 1) % N_SHARD, rank),
            device_id_type=MESH,
        )
        own_copy(send, recv, unit, off, rows, n).wait()
        every.wait_send()
        every.wait_recv()

    def pack(lines, send):
        @pl.loop(0, N_SHARD)
        def _(d):
            for k in range(CAP):
                send[pl.ds(MSG * d + k, ROWS, stride=CAP), :] = lines[tab[d, k]]

    def mats_copy():
        return pltpu.make_async_copy(send_qs.at[me], recv_qs.at[me], own_sem.at[0])

    def pack_mats():
        lane = lax.broadcasted_iota(jnp.int32, (ROWS, 128), 1)

        @pl.loop(0, N_SHARD)
        def _(d):
            one, two = tab[d, 8], tab[d, 9]
            q_two = pltpu.roll(lined_q[two], 96, 1)
            s_one = pltpu.roll(lined_s[one], 64, 1)
            s_two = pltpu.roll(lined_s[two], 32, 1)
            send_qs[d, pl.ds(0, ROWS, stride=3), :] = jnp.where(lane < 96, lined_q[one], q_two)
            send_qs[d, pl.ds(1, ROWS, stride=3), :] = jnp.where(lane < 64, q_two, s_one)
            send_qs[d, pl.ds(2, ROWS, stride=3), :] = jnp.where(lane < 32, s_one, s_two)

    load_q.wait()
    align_mats(q2, lined_q)
    load_s.wait()
    align_mats(s2, lined_s)
    load_tab.wait()
    pack_mats()
    pl.semaphore_wait(barrier, N_SHARD - 1 + N_TENSOR - 1)
    for offset in ORDER:
        dst = peer(offset)
        pltpu.make_async_remote_copy(
            src_ref=send_qs.at[dst],
            dst_ref=recv_qs.at[me],
            send_sem=send_sem.at[0],
            recv_sem=recv_sem.at[0],
            device_id=(dst, rank),
            device_id_type=MESH,
        ).start()
    mats_copy().start()

    load_g.wait()
    align_rows(g2, lined)
    pack(lined, send_g)
    exchange(send_g, recv_g, MSG, 1)

    load_m.wait()
    m2[...] = 0.9 * m2[...] + 0.1 * g2[...]
    save_first = local(m2, first_out, 7)
    align_rows(m2, lined)
    pack(lined, send_m)
    exchange(send_m, recv_m, MSG, 3)

    load_v.wait()
    align_rows(v2, lined)
    pack(lined, send_v)
    exchange(send_v, recv_v, MSG, 4, 0, HEAD)
    exchange(send_v, recv_v, MSG, 10, HEAD, TAIL)

    @pl.loop(0, PAIRS)
    def _(pair):
        for mat in range(10):
            places[10 * pair + mat] = place_of(owner, tab, pair, mat)

    save_places = local(places, places_out, 6)

    def spread(src_of, dst_of, n):
        for dx in range(1, N_TENSOR):
            other = (rank + dx) % N_TENSOR
            pltpu.make_async_remote_copy(
                src_ref=src_of(other),
                dst_ref=dst_of(rank),
                send_sem=send_sem.at[n],
                recv_sem=recv_sem.at[n],
                device_id=(me, other),
                device_id_type=MESH,
            ).start()

    def spread_done(three, n):
        every = pltpu.make_async_remote_copy(
            src_ref=three,
            dst_ref=three,
            send_sem=send_sem.at[n],
            recv_sem=recv_sem.at[n],
            device_id=(me, (rank + 1) % N_TENSOR),
            device_id_type=MESH,
        )
        every.wait_send()
        every.wait_recv()

    most = pl.ds(0, N_SHARD - 1)
    every_mat = pltpu.make_async_remote_copy(
        src_ref=send_qs.at[most],
        dst_ref=recv_qs.at[most],
        send_sem=send_sem.at[0],
        recv_sem=recv_sem.at[0],
        device_id=((me + 1) % N_SHARD, rank),
        device_id_type=MESH,
    )
    mats_copy().wait()
    every_mat.wait_send()
    every_mat.wait_recv()
    for k in range(3):
        into = nat if k == 2 else qx.at[rank, k]
        for s in range(0, N_SHARD, 2):
            pair = [recv_qs[s + n, pl.ds(k, ROWS, stride=3), :] for n in range(2)]
            into[pl.ds(ROWS * s, 2 * ROWS), :] = jnp.concatenate(pair, axis=0)
    q_part = (lambda other: qx.at[rank]), (lambda other: qx.at[other])
    spread(*q_part, 5)

    exchange_done(send_g, recv_g, MSG, 1)
    c0 = tab[me, 10]
    for j in range(2):
        left_h, left_l, right_h, right_l = [], [], [], []
        for k in range(CAP):
            chunk = recv_g[pl.ds(k, D, stride=CAP), :]
            mine = (k < c0) if j == 0 else (k >= c0)
            high, low = split(chunk)
            right_h.append(high)
            right_l.append(low)
            high, low = split(jnp.where(mine, chunk, 0.0))
            left_h.append(high)
            left_l.append(low)
        cat = functools.partial(jnp.concatenate, axis=1)
        gram[j] = dot3((cat(left_h), cat(left_l)), (cat(right_h), cat(right_l)), NT)

    def strip(x):
        return pl.ds(pl.multiple_of(96 * x, 8), 96)

    g_part = (lambda other: gram.at[:, strip(other), :]), (lambda other: xg.at[other])
    spread(*g_part, 6)

    spread_done(qx.at[pl.ds(0, 3)], 5)
    lane = lax.broadcasted_iota(jnp.int32, (D, 128), 1)
    for j in range(2):
        parts = [qx[x, 0] for x in range(4)]
        if j == 1:
            parts = [
                pltpu.roll(jnp.where(lane >= 96, part, qx[x, 1]), 32, 1)
                for x, part in enumerate(parts)
            ]
        full = jnp.concatenate(
            [
                jnp.where(lane < 96, parts[0], pltpu.roll(parts[1], 96, 1)),
                jnp.where(lane < 64, pltpu.roll(parts[1], 96, 1), pltpu.roll(parts[2], 64, 1)),
                jnp.where(lane < 32, pltpu.roll(parts[2], 64, 1), pltpu.roll(parts[3], 32, 1)),
            ],
            axis=1,
        )
        q_hi[j], q_lo[j] = split(full)
        qt_hi[j], qt_lo[j] = split(full.T)

    exchange_done(send_m, recv_m, MSG, 3)

    @pl.loop(0, CAP)
    def _(k):
        sel = jnp.where(k >= c0, 1, 0)
        both = jnp.concatenate(
            [recv_g[pl.ds(k, D, stride=CAP), :], recv_m[pl.ds(k, D, stride=CAP), :]], axis=1
        )
        hat = dot3((qt_hi[sel], qt_lo[sel]), split(both), NN)
        g_hat[pl.ds(k, D, stride=CAP), :] = hat[:, :128]
        m_hat[pl.ds(k, D, stride=CAP), :] = hat[:, 128:]

    spread_done(xg.at[pl.ds(0, 3)], 6)
    gram_parts = (
        pltpu.roll(jnp.where(lane >= 64, qx[rank, 1], nat[...]), 64, 1),
        pltpu.roll(nat[...], 96, 1),
    )
    for j in range(2):
        total = gram[j, strip(rank), :]
        for dx in range(1, N_TENSOR):
            total = total + xg[(rank + dx) % N_TENSOR, j]
        held = gram_parts[j].T[:96]
        fresh = 0.95 * held + 0.05 * total
        gram_strip[j] = fresh
        power[j, strip(rank), :] = dot3(split(fresh), (q_hi[j], q_lo[j]), NN)
    p_part = (
        (lambda other: power.at[:, strip(rank), :]),
        (lambda other: power.at[:, strip(other), :]),
    )
    spread(*p_part, 7)

    for n, off, rows in ((4, 0, HEAD), (10, HEAD, TAIL)):
        exchange_done(send_v, recv_v, MSG, n, off, rows)

        @pl.loop(0, N_SHARD)
        def _(s):
            here = pl.ds(pl.multiple_of(MSG * s + off, 8), rows)
            rot = g_hat[here, :]
            ret_n[here, :] = 0.95 * recv_v[here, :] + 0.05 * rot * rot

        exchange(ret_n, back_n, MSG, 8 if off == 0 else 11, off, rows)

    @pl.loop(0, N_SHARD)
    def _(s):
        here = pl.ds(pl.multiple_of(MSG * s, 8), MSG)
        m_hat[here, :] = m_hat[here, :] / CORR_ONE / (jnp.sqrt(ret_n[here, :] / CORR_TWO) + 1e-08)

    @pl.loop(0, CAP)
    def _(k):
        sel = jnp.where(k >= c0, 1, 0)
        ret_d[pl.ds(k, D, stride=CAP), :] = dot3((q_hi[sel], q_lo[sel]), split(m_hat[pl.ds(k, D, stride=CAP), :]), NN)

    exchange(ret_d, back_d, MSG, 9)

    spread_done(power.at[:, pl.ds(0, 288), :], 7)
    for j in range(2):
        full = power[j]
        norm = jnp.sqrt(jnp.sum(full * full, keepdims=True) + 1e-06)
        power[j] = full / norm

    @pl.loop(0, NS_STEPS)
    def _(sweep):
        for j in range(2):
            frame = power[j]
            pieces = split(frame)
            square = dot3(pieces, pieces, NT)
            power[j] = 1.5 * frame - 0.5 * dot3(split(square), pieces, NN)

    for x in range(N_TENSOR):

        @pl.when(rank == x)
        def _():
            for j in range(2):
                basis_strip[j] = power[j, :, 96 * x : 96 * x + 96].T

    save_basis = local(basis_strip, basis_out, 8)
    save_gram = local(gram_strip, gram_out, 9)
    exchange_done(ret_n, back_n, MSG, 8, 0, HEAD)
    exchange_done(ret_n, back_n, MSG, 11, HEAD, TAIL)

    def write_second(here, val):
        second2[here, :] = val

    unpack(back_n, places, write_second)
    save_second = local(second2, second_out, 10)
    for save in (save_places, save_first, save_basis, save_gram, save_second):
        save.wait()
    exchange_done(ret_d, back_d, MSG, 9)


def unpack_kernel(
    places,
    back_d,
    w_hbm,
    second,
    first,
    basis,
    gram,
    bias_g,
    bias_w,
    bias_m,
    bias_v,
    weight_out,
    first_out,
    second_out,
    basis_out,
    gram_out,
    bias_w_out,
    bias_m_out,
    bias_v_out,
    place,
    dv,
    w2,
    n2,
    f2,
    b2,
    s2,
    bias,
    sem,
    sem_out,
):
    def copy(src, dst, n, sems=sem):
        made = pltpu.make_async_copy(src, dst, sems.at[n])
        made.start()
        return made

    load_p = copy(places, place, 0)
    load_d = copy(back_d, dv, 1)
    load_w = copy(w_hbm, w2, 2)
    loads = [
        copy(src, bias.at[n, 0], 3 + n) for n, src in enumerate((bias_g, bias_w, bias_m, bias_v))
    ]
    passed = []
    for n, (src, held, dst) in enumerate(
        (
            (second, n2, second_out),
            (first, f2, first_out),
            (basis, b2, basis_out),
            (gram, s2, gram_out),
        )
    ):
        passed.append((copy(src, held, 7 + n), held, dst))

    def write_weight(here, val):
        w = w2[here, :]
        w2[here, :] = w - 0.01 * (val + 0.1 * w)

    load_p.wait()
    load_d.wait()
    load_w.wait()
    unpack(dv, place, write_weight, 0, PAIRS // 2)
    for load in loads:
        load.wait()
    moment = 0.9 * bias[2] + 0.1 * bias[0]
    moment_two = 0.95 * bias[3] + 0.05 * bias[0] * bias[0]
    bias[5] = moment
    bias[6] = moment_two
    bias[4] = bias[1] - 0.01 * (moment / CORR_ONE / (jnp.sqrt(moment_two / CORR_TWO) + 1e-08))
    saves = [
        copy(bias.at[4 + n, 0], dst, n, sem_out)
        for n, dst in enumerate((bias_w_out, bias_m_out, bias_v_out))
    ]
    for n, (load, held, dst) in enumerate(passed):
        load.wait()
        saves.append(copy(held, dst, 3 + n, sem_out))
    unpack(dv, place, write_weight, PAIRS // 2, PAIRS)
    saves.append(copy(w2, weight_out, 7, sem_out))
    for save in saves:
        save.wait()


def body(
    gradient,
    weight,
    first_moment,
    second_moment,
    left_basis,
    left_gram,
    owner_table,
    bias_gradient,
    bias_weight,
    bias_first,
    bias_second,
):
    hbm = pl.BlockSpec(memory_space=pltpu.HBM)
    flat = (ROWS * LINE, 128)
    g, w, m, v = (a.reshape(flat) for a in (gradient, weight, first_moment, second_moment))
    wide = pltpu.VMEM((N_SHARD * MSG, 128), F32)
    mats = pltpu.VMEM((N_SHARD, QMSG, 128), F32)
    lines_q = pltpu.VMEM((ZERO_MAT + 1, ROWS, 128), F32)
    full = pltpu.VMEM((2, D, D), F32)
    half = pltpu.VMEM((2, D, D), BF16)
    strips = pltpu.VMEM((2, 96, D), F32)
    rows = pltpu.VMEM(flat, F32)
    rows_q = pltpu.VMEM((ROWS * QLINE, 128), F32)
    wide_out = jax.ShapeDtypeStruct((N_SHARD * MSG, 128), F32)
    flat_out = jax.ShapeDtypeStruct(flat, F32)
    strip_out = jax.ShapeDtypeStruct((2, 96, D), F32)
    tab_shape = (N_SHARD, 128)
    flat_q = (ROWS * QLINE, 1, 128)
    owner = owner_table.T
    back_d, second, first, basis, gram, places = pl.pallas_call(
        main_kernel,
        out_shape=(
            wide_out,
            flat_out,
            flat_out,
            strip_out,
            strip_out,
            jax.ShapeDtypeStruct((128,), jnp.int32),
        ),
        in_specs=[hbm] * 6,
        out_specs=(hbm,) * 6,
        scratch_shapes=[rows] * 3
        + [rows_q] * 2
        + [pltpu.VMEM((ZERO_CHUNK + 1, ROWS, 128), F32), lines_q, lines_q]
        + [wide] * 3
        + [mats]
        + [wide] * 3
        + [mats, pltpu.VMEM((D, 128), F32)]
        + [pltpu.VMEM((N_TENSOR, 2, D, 128), F32)]
        + [wide] * 2
        + [full, pltpu.VMEM((N_TENSOR, 2, 96, D), F32), full]
        + [half] * 4
        + [wide] * 2
        + [strips] * 2
        + [wide, rows]
        + [pltpu.SMEM(owner.shape, jnp.int32), pltpu.VMEM(owner.shape, jnp.int32)]
        + [pltpu.VMEM(tab_shape, jnp.int32), pltpu.SMEM(tab_shape, jnp.int32)]
        + [pltpu.SMEM((128,), jnp.int32)]
        + [pltpu.SemaphoreType.DMA((n,)) for n in (13, 12, 12, 12)],
        compiler_params=pltpu.CompilerParams(
            collective_id=0, has_side_effects=True, vmem_limit_bytes=VMEM_ALL
        ),
        name="exchange_and_rotate",
    )(owner, g, m, v, left_basis.reshape(flat_q), left_gram.reshape(flat_q))
    bias_out = jax.ShapeDtypeStruct(bias_gradient.shape, F32)
    outs = pl.pallas_call(
        unpack_kernel,
        out_shape=(flat_out,) * 3 + (strip_out,) * 2 + (bias_out,) * 3,
        in_specs=[hbm] * 11,
        out_specs=(hbm,) * 8,
        scratch_shapes=[pltpu.SMEM((128,), jnp.int32), wide]
        + [rows] * 3
        + [strips] * 2
        + [pltpu.VMEM((7, 1) + bias_gradient.shape, F32)]
        + [pltpu.SemaphoreType.DMA((11,)), pltpu.SemaphoreType.DMA((8,))],
        compiler_params=pltpu.CompilerParams(vmem_limit_bytes=VMEM_ALL),
        name="unpack",
    )(
        places,
        back_d,
        w,
        second,
        first,
        basis,
        gram,
        bias_gradient,
        bias_weight,
        bias_first,
        bias_second,
    )
    weight_new, first_new, second_new, basis_new, gram_new = outs[:5]
    return (
        weight_new.reshape(weight.shape),
        first_new.reshape(weight.shape),
        second_new.reshape(weight.shape),
        basis_new.transpose(0, 2, 1)[None],
        gram_new.transpose(0, 2, 1)[None],
        *outs[5:],
    )


def solution(mesh):
    rows = P("shard", "tensor", None)
    flat = P(("shard", "tensor"))
    owned = P("shard", None, None, "tensor")
    return jax.shard_map(
        body,
        mesh=mesh,
        in_specs=(rows,) * 6 + (P(),) + (flat,) * 4,
        out_specs=(rows,) * 3 + (owned,) * 2 + (flat,) * 3,
        check_vma=False,
    )
```

```python
import functools

import jax
import jax.numpy as jnp
from jax import lax
from jax.experimental import pallas as pl
from jax.experimental.pallas import tpu as pltpu
from jax.sharding import PartitionSpec as P

MESH = pl.DeviceIdType.MESH
STEP = 10
NS_STEPS = 5
N_SHARD = 32
N_TENSOR = 4
D = 384
ROWS = 12
PAIRS = 6
TYPE_TILES = (3, 1, 4, 4, 6)
TYPE_START = (0, 3, 4, 8, 12)
TYPE_CHUNKS = (3, 1, 3, 3, 5)
CHUNK_START = (0, 3, 4, 7, 10)
CAP = 6
MSG = ROWS * CAP
QMSG = ROWS * 3
LINE = 162
QLINE = 45
ZERO_CHUNK = 180
ZERO_MAT = 60
CORR_ONE = 1.0 - 0.9**STEP
CORR_TWO = 1.0 - 0.95**STEP
NO_CODE = (ZERO_MAT << 16) + (ZERO_CHUNK << 8)
HEAD = 48
TAIL = 24
VMEM_ALL = 67043328
F32 = jnp.float32


def send_order():
    rings = (
        ((2, 2),),
        ((1, 2), (2, 1), (3, 2), (2, 3)),
        ((1, 1), (3, 3), (1, 3), (3, 1)),
        ((2, 0), (0, 2)),
        ((1, 0), (0, 1), (3, 0), (0, 3)),
    )
    order = [(dy, dz, dc) for ring in rings for dc in range(2) for dy, dz in ring]
    return order + [(0, 0, 1)]


ORDER = send_order()
BF16 = jnp.bfloat16


def table_of(owners):
    group = lax.broadcasted_iota(jnp.int32, (N_SHARD, 12), 0)
    layer = lax.broadcasted_iota(jnp.int32, (N_SHARD, 12), 1)
    low = jnp.full((N_SHARD, 12), NO_CODE, jnp.int32)
    high = jnp.full((N_SHARD, 12), -1, jnp.int32)
    for kind in range(5):
        code = ((5 * layer + kind) << 16) + ((15 * layer + CHUNK_START[kind]) << 8)
        code = code + TYPE_CHUNKS[kind]
        hit = owners[kind : kind + 1, :] == group
        low = jnp.minimum(low, jnp.where(hit, code, NO_CODE))
        high = jnp.maximum(high, jnp.where(hit, code, -1))
    first = jnp.min(low, axis=1, keepdims=True)
    second = jnp.max(high, axis=1, keepdims=True)
    second = jnp.where((second < 0) | (second == first), NO_CODE, second)
    c0, c1 = first & 255, second & 255
    at0, at1 = (first >> 8) & 255, (second >> 8) & 255
    k = lax.broadcasted_iota(jnp.int32, (N_SHARD, 128), 1)
    rest = jnp.where(k - c0 < c1, at1 + k - c0, ZERO_CHUNK)
    table = jnp.where(k < c0, at0 + k, rest)
    table = jnp.where(k == 8, first >> 16, table)
    table = jnp.where(k == 9, second >> 16, table)
    return jnp.where(k == 10, c0, table)


def place_of(owner, tab, pair, mat):
    group = owner[mat % 5, 2 * pair + mat // 5]
    base = jnp.where(tab[group, 8] == 10 * pair + mat, 0, tab[group, 10])
    return MSG * group + base


def align_rows(src, dst):
    lane = lax.broadcasted_iota(jnp.int32, (ROWS, 128), 1)

    @pl.loop(0, PAIRS)
    def _(pair):
        for half in range(2):
            for kind in range(5):
                for j in range(TYPE_CHUNKS[kind]):
                    col = 1728 * half + 96 * TYPE_START[kind] + 128 * j
                    at, shift = divmod(col, 128)
                    valid = min(128, 96 * TYPE_TILES[kind] - 128 * j)
                    val = src[pl.ds(27 * pair + at, ROWS, stride=LINE), :]
                    if shift:
                        val = pltpu.roll(val, 128 - shift, 1)
                        if valid > 128 - shift:
                            nxt = src[pl.ds(27 * pair + at + 1, ROWS, stride=LINE), :]
                            nxt = pltpu.roll(nxt, 128 - shift, 1)
                            val = jnp.where(lane < 128 - shift, val, nxt)
                    if valid < 128:
                        val = jnp.where(lane < valid, val, 0.0)
                    dst[30 * pair + 15 * half + CHUNK_START[kind] + j] = val


def align_mats(src, dst):
    lane = lax.broadcasted_iota(jnp.int32, (ROWS, 128), 1)

    @pl.loop(0, 3)
    def _(step):
        for part in range(20):
            at, shift = divmod(96 * part, 128)
            val = src[pl.ds(15 * step + at, ROWS, stride=QLINE), :]
            if shift:
                val = pltpu.roll(val, 128 - shift, 1)
                if 96 > 128 - shift:
                    nxt = src[pl.ds(15 * step + at + 1, ROWS, stride=QLINE), :]
                    nxt = pltpu.roll(nxt, 128 - shift, 1)
                    val = jnp.where(lane < 128 - shift, val, nxt)
            dst[20 * step + part] = jnp.where(lane < 96, val, 0.0)


def split(x):
    high = x.astype(BF16)
    return high, (x - high.astype(F32)).astype(BF16)


def dot3(a, b, dims):
    ah, al = a
    bh, bl = b
    dot = functools.partial(
        lax.dot_general, dimension_numbers=(dims, ((), ())), preferred_element_type=F32
    )
    return dot(ah, bh) + (dot(ah, bl) + dot(al, bh))


NN = ((1,), (0,))
NT = ((1,), (1,))


def outer3(pieces):
    high, low = pieces
    dot = functools.partial(
        lax.dot_general, dimension_numbers=(NT, ((), ())), preferred_element_type=F32
    )
    mixed = dot(high, low)
    return dot(high, high) + (mixed + mixed.T)


def out_pieces():
    owner_of = []
    for half in range(2):
        for kind in range(5):
            start = 1728 * half + 96 * TYPE_START[kind]
            for c in range(96 * TYPE_TILES[kind]):
                owner_of.append((5 * half + kind, start))
    table = []
    for chunk in range(27):
        pieces = []
        for lane in range(128):
            col = 128 * chunk + lane
            mat, start = owner_of[col]
            j, src = divmod(col - start, 128)
            key = (mat, j, (lane - src) % 128)
            if pieces and pieces[-1][0] == key:
                pieces[-1][2] = lane + 1
            else:
                pieces.append([key, lane, lane + 1])
        table.append(pieces)
    return table


def unpack(back, place, write, first=0, last=PAIRS):
    lane = lax.broadcasted_iota(jnp.int32, (ROWS, 128), 1)
    table = out_pieces()

    @pl.loop(first, last)
    def _(pair):
        for chunk in range(27):
            out = None
            for (mat, j, turn), _lo, hi in reversed(table[chunk]):
                val = back[pl.ds(place[10 * pair + mat] + j, ROWS, stride=CAP), :]
                if turn:
                    val = pltpu.roll(val, turn, 1)
                out = val if out is None else jnp.where(lane < hi, val, out)
            write(pl.ds(27 * pair + chunk, ROWS, stride=LINE), out)


def main_kernel(
    owner_hbm,
    g_hbm,
    m_hbm,
    v_hbm,
    q_hbm,
    s_hbm,
    back_d,
    second_out,
    first_out,
    basis_out,
    gram_out,
    places_out,
    g2,
    m2,
    v2,
    q2,
    s2,
    lined,
    lined_q,
    lined_s,
    send_g,
    send_m,
    send_v,
    send_qs,
    recv_g,
    recv_m,
    recv_v,
    recv_qs,
    nat,
    qx,
    ret_d,
    ret_n,
    gram,
    xg,
    power,
    q_hi,
    q_lo,
    qt_hi,
    qt_lo,
    g_hat,
    m_hat,
    gram_strip,
    basis_strip,
    back_n,
    second2,
    owner,
    owners,
    tab_vec,
    tab,
    places,
    in_sem,
    send_sem,
    recv_sem,
    own_sem,
):
    me = lax.axis_index("shard")
    rank = lax.axis_index("tensor")
    my_y, my_z, my_c = me // 8, (me // 2) % 4, me % 2

    def peer(offset):
        dy, dz, dc = offset
        return ((my_y + dy) % 4) * 8 + ((my_z + dz) % 4) * 2 + (my_c + dc) % 2

    def local(src, dst, n):
        made = pltpu.make_async_copy(src, dst, in_sem.at[n])
        made.start()
        return made

    load_owner = local(owner_hbm, owner, 11)
    load_owners = local(owner_hbm, owners, 12)
    load_q = local(q_hbm.at[:, 0, :], q2, 0)
    load_s = local(s_hbm.at[:, 0, :], s2, 2)
    barrier = pltpu.get_barrier_semaphore()

    for offset in ORDER:
        pl.semaphore_signal(
            barrier, inc=1, device_id=(peer(offset), rank), device_id_type=MESH
        )

    for dx in range(1, N_TENSOR):
        pl.semaphore_signal(
            barrier, inc=1, device_id=(me, (rank + dx) % N_TENSOR), device_id_type=MESH
        )

    load_g = local(g_hbm, g2, 1)
    load_m = local(m_hbm, m2, 3)
    load_v = local(v_hbm, v2, 4)
    load_owner.wait()
    load_owners.wait()
    tab_vec[...] = table_of(owners[...])
    load_tab = local(tab_vec, tab, 5)

    lined[ZERO_CHUNK] = jnp.zeros((ROWS, 128), F32)
    lined_q[ZERO_MAT] = jnp.zeros((ROWS, 128), F32)
    lined_s[ZERO_MAT] = jnp.zeros((ROWS, 128), F32)

    def own_copy(send, recv, unit, off, rows, n):
        own = pl.ds(pl.multiple_of(me * unit + off, 8), rows)
        return pltpu.make_async_copy(send.at[own], recv.at[own], own_sem.at[n])

    def exchange(send, recv, unit, n, off=0, rows=None):
        rows = unit if rows is None else rows
        for offset in ORDER:
            dst = peer(offset)
            pltpu.make_async_remote_copy(
                src_ref=send.at[pl.ds(pl.multiple_of(dst * unit + off, 8), rows)],
                dst_ref=recv.at[pl.ds(pl.multiple_of(me * unit + off, 8), rows)],
                send_sem=send_sem.at[n],
                recv_sem=recv_sem.at[n],
                device_id=(dst, rank),
                device_id_type=MESH,
            ).start()
        own_copy(send, recv, unit, off, rows, n).start()

    def share(send, recv, rows, count, n):
        whole = pl.ds(0, count * rows)
        return pltpu.make_async_remote_copy(
            src_ref=send.at[whole],
            dst_ref=recv.at[whole],
            send_sem=send_sem.at[n],
            recv_sem=recv_sem.at[n],
            device_id=((me + 1) % N_SHARD, rank),
            device_id_type=MESH,
        )

    def exchange_done(send, recv, unit, n, off=0, rows=None):
        rows = unit if rows is None else rows
        own_copy(send, recv, unit, off, rows, n).wait()
        every = share(send, recv, rows, N_SHARD - 1, n)
        every.wait_send()
        every.wait_recv()

    def pack(lines, send):
        @pl.loop(0, N_SHARD)
        def _(d):
            for k in range(CAP):
                send[pl.ds(MSG * d + k, ROWS, stride=CAP), :] = lines[tab[d, k]]

    def mats_copy():
        return pltpu.make_async_copy(send_qs.at[me], recv_qs.at[me], own_sem.at[0])

    def pack_mats():
        lane = lax.broadcasted_iota(jnp.int32, (ROWS, 128), 1)

        @pl.loop(0, N_SHARD // 8)
        def _(step):
            held = []
            for n in range(8):
                one, two = tab[8 * step + n, 8], tab[8 * step + n, 9]
                held.append((lined_q[one], lined_q[two], lined_s[one], lined_s[two]))
            for n, (q_one, q_two, s_one, s_two) in enumerate(held):
                d = 8 * step + n
                q_two = pltpu.roll(q_two, 96, 1)
                s_one = pltpu.roll(s_one, 64, 1)
                s_two = pltpu.roll(s_two, 32, 1)
                send_qs[d, pl.ds(0, ROWS, stride=3), :] = jnp.where(lane < 96, q_one, q_two)
                send_qs[d, pl.ds(1, ROWS, stride=3), :] = jnp.where(lane < 64, q_two, s_one)
                send_qs[d, pl.ds(2, ROWS, stride=3), :] = jnp.where(lane < 32, s_one, s_two)

    load_q.wait()
    align_mats(q2, lined_q)
    load_s.wait()
    align_mats(s2, lined_s)
    load_tab.wait()
    pack_mats()
    pl.semaphore_wait(barrier, N_SHARD - 1 + N_TENSOR - 1)
    for offset in ORDER:
        dst = peer(offset)
        pltpu.make_async_remote_copy(
            src_ref=send_qs.at[dst],
            dst_ref=recv_qs.at[me],
            send_sem=send_sem.at[0],
            recv_sem=recv_sem.at[0],
            device_id=(dst, rank),
            device_id_type=MESH,
        ).start()
    mats_copy().start()

    load_g.wait()
    align_rows(g2, lined)
    pack(lined, send_g)
    exchange(send_g, recv_g, MSG, 1)

    load_m.wait()
    m2[...] = 0.9 * m2[...] + 0.1 * g2[...]
    save_first = local(m2, first_out, 7)
    align_rows(m2, lined)
    pack(lined, send_m)
    exchange(send_m, recv_m, MSG, 3)

    load_v.wait()
    align_rows(v2, lined)
    pack(lined, send_v)
    exchange(send_v, recv_v, MSG, 4, 0, HEAD)
    exchange(send_v, recv_v, MSG, 10, HEAD, TAIL)

    @pl.loop(0, PAIRS)
    def _(pair):
        for mat in range(10):
            places[10 * pair + mat] = place_of(owner, tab, pair, mat)

    save_places = local(places, places_out, 6)

    def spread(src_of, dst_of, n):
        for dx in range(1, N_TENSOR):
            other = (rank + dx) % N_TENSOR
            pltpu.make_async_remote_copy(
                src_ref=src_of(other),
                dst_ref=dst_of(rank),
                send_sem=send_sem.at[n],
                recv_sem=recv_sem.at[n],
                device_id=(me, other),
                device_id_type=MESH,
            ).start()

    def spread_done(three, n):
        every = pltpu.make_async_remote_copy(
            src_ref=three,
            dst_ref=three,
            send_sem=send_sem.at[n],
            recv_sem=recv_sem.at[n],
            device_id=(me, (rank + 1) % N_TENSOR),
            device_id_type=MESH,
        )
        every.wait_send()
        every.wait_recv()

    most = pl.ds(0, N_SHARD - 1)
    every_mat = pltpu.make_async_remote_copy(
        src_ref=send_qs.at[most],
        dst_ref=recv_qs.at[most],
        send_sem=send_sem.at[0],
        recv_sem=recv_sem.at[0],
        device_id=((me + 1) % N_SHARD, rank),
        device_id_type=MESH,
    )
    mats_copy().wait()
    every_mat.wait_send()
    every_mat.wait_recv()
    lane = lax.broadcasted_iota(jnp.int32, (D, 128), 1)
    lane_half = lax.broadcasted_iota(jnp.int32, (D // 2, 128), 1)
    for k in range(3):
        for s in range(0, N_SHARD, 2):
            pair = [recv_qs[s + n, pl.ds(k, ROWS, stride=3), :] for n in range(2)]
            into = jnp.concatenate(pair, axis=0)
            if k == 0:
                qx[rank, pl.ds(ROWS * s, 2 * ROWS), :] = into
            else:
                nat[k - 1, pl.ds(ROWS * s, 2 * ROWS), :] = into
    qx[rank, pl.ds(D, D // 2), :] = jnp.where(
        lane_half < 64, nat[0, : D // 2], pltpu.roll(nat[0, D // 2 :], 64, 1)
    )
    q_part = (lambda other: qx.at[rank]), (lambda other: qx.at[other])
    spread(*q_part, 5)

    exchange_done(send_g, recv_g, MSG, 1)
    c0 = tab[me, 10]
    for j in range(2):
        chunks = []
        for k in range(CAP):
            mine = (k < c0) if j == 0 else (k >= c0)
            chunks.append(split(jnp.where(mine, recv_g[pl.ds(k, D, stride=CAP), :], 0.0)))
        gram[j] = outer3(tuple(jnp.concatenate(half, axis=1) for half in zip(*chunks)))

    def strip(x):
        return pl.ds(pl.multiple_of(96 * x, 8), 96)

    g_part = (lambda other: gram.at[:, strip(other), :]), (lambda other: xg.at[other])
    spread(*g_part, 6)

    spread_done(qx.at[pl.ds(0, 3)], 5)
    for j in range(2):
        parts = [qx[x, :D] for x in range(4)]
        if j == 1:
            rests = [qx[x, D:] for x in range(4)]
            rests = [jnp.concatenate([r, pltpu.roll(r, 64, 1)], axis=0) for r in rests]
            parts = [
                pltpu.roll(jnp.where(lane >= 96, part, rest), 32, 1)
                for part, rest in zip(parts, rests)
            ]
        full = jnp.concatenate(
            [
                jnp.where(lane < 96, parts[0], pltpu.roll(parts[1], 96, 1)),
                jnp.where(lane < 64, pltpu.roll(parts[1], 96, 1), pltpu.roll(parts[2], 64, 1)),
                jnp.where(lane < 32, pltpu.roll(parts[2], 64, 1), pltpu.roll(parts[3], 32, 1)),
            ],
            axis=1,
        )
        q_hi[j], q_lo[j] = split(full)
        qt_hi[j], qt_lo[j] = split(full.T)

    exchange_done(send_m, recv_m, MSG, 3)

    @pl.loop(0, CAP)
    def _(k):
        sel = jnp.where(k >= c0, 1, 0)
        both = jnp.concatenate(
            [recv_g[pl.ds(k, D, stride=CAP), :], recv_m[pl.ds(k, D, stride=CAP), :]], axis=1
        )
        hat = dot3((qt_hi[sel], qt_lo[sel]), split(both), NN)
        g_hat[pl.ds(k, D, stride=CAP), :] = hat[:, :128]
        m_hat[pl.ds(k, D, stride=CAP), :] = hat[:, 128:]

    spread_done(xg.at[pl.ds(0, 3)], 6)
    gram_parts = (
        pltpu.roll(jnp.where(lane >= 64, nat[0], nat[1]), 64, 1),
        pltpu.roll(nat[1], 96, 1),
    )
    for j in range(2):
        total = gram[j, strip(rank), :]
        for dx in range(1, N_TENSOR):
            total = total + xg[(rank + dx) % N_TENSOR, j]
        held = gram_parts[j].T[:96]
        fresh = 0.95 * held + 0.05 * total
        gram_strip[j] = fresh
        power[j, strip(rank), :] = dot3(split(fresh), (q_hi[j], q_lo[j]), NN)
    p_part = (
        (lambda other: power.at[:, strip(rank), :]),
        (lambda other: power.at[:, strip(other), :]),
    )
    spread(*p_part, 7)

    for n, off, rows in ((4, 0, HEAD), (10, HEAD, TAIL)):
        exchange_done(send_v, recv_v, MSG, n, off, rows)

        @pl.loop(0, N_SHARD)
        def _(s):
            here = pl.ds(pl.multiple_of(MSG * s + off, 8), rows)
            rot = g_hat[here, :]
            ret_n[here, :] = 0.95 * recv_v[here, :] + 0.05 * rot * rot

        exchange(ret_n, back_n, MSG, 8 if off == 0 else 11, off, rows)

    @pl.loop(0, N_SHARD)
    def _(s):
        here = pl.ds(pl.multiple_of(MSG * s, 8), MSG)
        m_hat[here, :] = m_hat[here, :] / CORR_ONE / (jnp.sqrt(ret_n[here, :] / CORR_TWO) + 1e-08)

    @pl.loop(0, CAP)
    def _(k):
        sel = jnp.where(k >= c0, 1, 0)
        ret_d[pl.ds(k, D, stride=CAP), :] = dot3((q_hi[sel], q_lo[sel]), split(m_hat[pl.ds(k, D, stride=CAP), :]), NN)

    exchange(ret_d, back_d, MSG, 9)

    spread_done(power.at[:, pl.ds(0, 288), :], 7)
    for j in range(2):
        full = power[j]
        norm = jnp.sqrt(jnp.sum(full * full, keepdims=True) + 1e-06)
        power[j] = full / norm

    @pl.loop(0, NS_STEPS - 1)
    def _(sweep):
        for j in range(2):
            frame = power[j]
            pieces = split(frame)
            power[j] = 1.5 * frame - 0.5 * dot3(split(outer3(pieces)), pieces, NN)

    for j in range(2):
        gram[j] = power[j].T
        square = split(outer3(split(power[j])))
        mine = gram[j, strip(rank), :]
        basis_strip[j] = 1.5 * mine - 0.5 * dot3(split(mine), square, NN)

    save_basis = local(basis_strip, basis_out, 8)
    save_gram = local(gram_strip, gram_out, 9)
    exchange_done(ret_n, back_n, MSG, 8, 0, HEAD)
    exchange_done(ret_n, back_n, MSG, 11, HEAD, TAIL)

    def write_second(here, val):
        second2[here, :] = val

    unpack(back_n, places, write_second)
    save_second = local(second2, second_out, 10)
    for save in (save_places, save_first, save_basis, save_gram, save_second):
        save.wait()
    exchange_done(ret_d, back_d, MSG, 9)


def unpack_kernel(
    places,
    back_d,
    w_hbm,
    second,
    first,
    basis,
    gram,
    bias_g,
    bias_w,
    bias_m,
    bias_v,
    weight_out,
    first_out,
    second_out,
    basis_out,
    gram_out,
    bias_w_out,
    bias_m_out,
    bias_v_out,
    place,
    dv,
    w2,
    n2,
    f2,
    b2,
    s2,
    bias,
    sem,
    sem_out,
):
    def copy(src, dst, n, sems=sem):
        made = pltpu.make_async_copy(src, dst, sems.at[n])
        made.start()
        return made

    load_p = copy(places, place, 0)
    load_d = copy(back_d, dv, 1)
    load_w = copy(w_hbm, w2, 2)
    loads = [
        copy(src, bias.at[n, 0], 3 + n) for n, src in enumerate((bias_g, bias_w, bias_m, bias_v))
    ]
    passed = []
    for n, (src, held, dst) in enumerate(
        (
            (second, n2, second_out),
            (first, f2, first_out),
            (basis, b2, basis_out),
            (gram, s2, gram_out),
        )
    ):
        passed.append((copy(src, held, 7 + n), held, dst))

    def write_weight(here, val):
        w = w2[here, :]
        w2[here, :] = w - 0.01 * (val + 0.1 * w)

    load_p.wait()
    load_d.wait()
    load_w.wait()
    unpack(dv, place, write_weight, 0, PAIRS // 2)
    for load in loads:
        load.wait()
    moment = 0.9 * bias[2] + 0.1 * bias[0]
    moment_two = 0.95 * bias[3] + 0.05 * bias[0] * bias[0]
    bias[5] = moment
    bias[6] = moment_two
    bias[4] = bias[1] - 0.01 * (moment / CORR_ONE / (jnp.sqrt(moment_two / CORR_TWO) + 1e-08))
    saves = [
        copy(bias.at[4 + n, 0], dst, n, sem_out)
        for n, dst in enumerate((bias_w_out, bias_m_out, bias_v_out))
    ]
    for n, (load, held, dst) in enumerate(passed):
        load.wait()
        saves.append(copy(held, dst, 3 + n, sem_out))
    unpack(dv, place, write_weight, PAIRS // 2, PAIRS)
    saves.append(copy(w2, weight_out, 7, sem_out))
    for save in saves:
        save.wait()


def body(
    gradient,
    weight,
    first_moment,
    second_moment,
    left_basis,
    left_gram,
    owner_table,
    bias_gradient,
    bias_weight,
    bias_first,
    bias_second,
):
    hbm = pl.BlockSpec(memory_space=pltpu.HBM)
    flat = (ROWS * LINE, 128)
    g, w, m, v = (a.reshape(flat) for a in (gradient, weight, first_moment, second_moment))
    wide = pltpu.VMEM((N_SHARD * MSG, 128), F32)
    mats = pltpu.VMEM((N_SHARD, QMSG, 128), F32)
    lines_q = pltpu.VMEM((ZERO_MAT + 1, ROWS, 128), F32)
    full = pltpu.VMEM((2, D, D), F32)
    half = pltpu.VMEM((2, D, D), BF16)
    strips = pltpu.VMEM((2, 96, D), F32)
    rows = pltpu.VMEM(flat, F32)
    rows_q = pltpu.VMEM((ROWS * QLINE, 128), F32)
    wide_out = jax.ShapeDtypeStruct((N_SHARD * MSG, 128), F32)
    flat_out = jax.ShapeDtypeStruct(flat, F32)
    strip_out = jax.ShapeDtypeStruct((2, 96, D), F32)
    tab_shape = (N_SHARD, 128)
    flat_q = (ROWS * QLINE, 1, 128)
    owner = owner_table.T
    back_d, second, first, basis, gram, places = pl.pallas_call(
        main_kernel,
        out_shape=(
            wide_out,
            flat_out,
            flat_out,
            strip_out,
            strip_out,
            jax.ShapeDtypeStruct((128,), jnp.int32),
        ),
        in_specs=[hbm] * 6,
        out_specs=(hbm,) * 6,
        scratch_shapes=[rows] * 3
        + [rows_q] * 2
        + [pltpu.VMEM((ZERO_CHUNK + 1, ROWS, 128), F32), lines_q, lines_q]
        + [wide] * 3
        + [mats]
        + [wide] * 3
        + [mats, pltpu.VMEM((2, D, 128), F32)]
        + [pltpu.VMEM((N_TENSOR, D + D // 2, 128), F32)]
        + [wide] * 2
        + [full, pltpu.VMEM((N_TENSOR, 2, 96, D), F32), full]
        + [half] * 4
        + [wide] * 2
        + [strips] * 2
        + [wide, rows]
        + [pltpu.SMEM(owner.shape, jnp.int32), pltpu.VMEM(owner.shape, jnp.int32)]
        + [pltpu.VMEM(tab_shape, jnp.int32), pltpu.SMEM(tab_shape, jnp.int32)]
        + [pltpu.SMEM((128,), jnp.int32)]
        + [pltpu.SemaphoreType.DMA((n,)) for n in (13, 12, 12, 12)],
        compiler_params=pltpu.CompilerParams(
            collective_id=0, has_side_effects=True, vmem_limit_bytes=VMEM_ALL
        ),
        name="exchange_and_rotate",
    )(owner, g, m, v, left_basis.reshape(flat_q), left_gram.reshape(flat_q))
    bias_out = jax.ShapeDtypeStruct(bias_gradient.shape, F32)
    outs = pl.pallas_call(
        unpack_kernel,
        out_shape=(flat_out,) * 3 + (strip_out,) * 2 + (bias_out,) * 3,
        in_specs=[hbm] * 11,
        out_specs=(hbm,) * 8,
        scratch_shapes=[pltpu.SMEM((128,), jnp.int32), wide]
        + [rows] * 3
        + [strips] * 2
        + [pltpu.VMEM((7, 1) + bias_gradient.shape, F32)]
        + [pltpu.SemaphoreType.DMA((11,)), pltpu.SemaphoreType.DMA((8,))],
        compiler_params=pltpu.CompilerParams(vmem_limit_bytes=VMEM_ALL),
        name="unpack",
    )(
        places,
        back_d,
        w,
        second,
        first,
        basis,
        gram,
        bias_gradient,
        bias_weight,
        bias_first,
        bias_second,
    )
    weight_new, first_new, second_new, basis_new, gram_new = outs[:5]
    return (
        weight_new.reshape(weight.shape),
        first_new.reshape(weight.shape),
        second_new.reshape(weight.shape),
        basis_new.transpose(0, 2, 1)[None],
        gram_new.transpose(0, 2, 1)[None],
        *outs[5:],
    )


def solution(mesh):
    rows = P("shard", "tensor", None)
    flat = P(("shard", "tensor"))
    owned = P("shard", None, None, "tensor")
    return jax.shard_map(
        body,
        mesh=mesh,
        in_specs=(rows,) * 6 + (P(),) + (flat,) * 4,
        out_specs=(rows,) * 3 + (owned,) * 2 + (flat,) * 3,
        check_vma=False,
    )
```

```python
import functools

import jax
import jax.numpy as jnp
from jax import lax
from jax.experimental import pallas as pl
from jax.experimental.pallas import tpu as pltpu
from jax.sharding import PartitionSpec as P

MESH = pl.DeviceIdType.MESH
STEP = 10
NS_STEPS = 5
N_SHARD = 32
N_TENSOR = 4
D = 384
ROWS = 12
PAIRS = 6
TYPE_TILES = (3, 1, 4, 4, 6)
TYPE_START = (0, 3, 4, 8, 12)
TYPE_CHUNKS = (3, 1, 3, 3, 5)
CHUNK_START = (0, 3, 4, 7, 10)
CAP = 6
MSG = ROWS * CAP
QMSG = ROWS * 3
LINE = 162
QLINE = 45
ZERO_CHUNK = 180
ZERO_MAT = 60
CORR_ONE = 1.0 - 0.9**STEP
CORR_TWO = 1.0 - 0.95**STEP
NO_CODE = (ZERO_MAT << 16) + (ZERO_CHUNK << 8)
HEAD = 48
TAIL = 24
VMEM_ALL = 67043328
F32 = jnp.float32


def send_order():
    rings = (
        ((2, 2),),
        ((1, 2), (2, 1), (3, 2), (2, 3)),
        ((1, 1), (3, 3), (1, 3), (3, 1)),
        ((2, 0), (0, 2)),
        ((1, 0), (0, 1), (3, 0), (0, 3)),
    )
    order = [(dy, dz, dc) for ring in rings for dc in range(2) for dy, dz in ring]
    return order + [(0, 0, 1)]


ORDER = send_order()
BF16 = jnp.bfloat16


def table_of(owners):
    group = lax.broadcasted_iota(jnp.int32, (N_SHARD, 12), 0)
    layer = lax.broadcasted_iota(jnp.int32, (N_SHARD, 12), 1)
    low = jnp.full((N_SHARD, 12), NO_CODE, jnp.int32)
    high = jnp.full((N_SHARD, 12), -1, jnp.int32)
    for kind in range(5):
        code = ((5 * layer + kind) << 16) + ((15 * layer + CHUNK_START[kind]) << 8)
        code = code + TYPE_CHUNKS[kind]
        hit = owners[kind : kind + 1, :] == group
        low = jnp.minimum(low, jnp.where(hit, code, NO_CODE))
        high = jnp.maximum(high, jnp.where(hit, code, -1))
    first = jnp.min(low, axis=1, keepdims=True)
    second = jnp.max(high, axis=1, keepdims=True)
    second = jnp.where((second < 0) | (second == first), NO_CODE, second)
    c0, c1 = first & 255, second & 255
    at0, at1 = (first >> 8) & 255, (second >> 8) & 255
    k = lax.broadcasted_iota(jnp.int32, (N_SHARD, 128), 1)
    rest = jnp.where(k - c0 < c1, at1 + k - c0, ZERO_CHUNK)
    table = jnp.where(k < c0, at0 + k, rest)
    table = jnp.where(k == 8, first >> 16, table)
    table = jnp.where(k == 9, second >> 16, table)
    return jnp.where(k == 10, c0, table)


def place_of(owner, tab, pair, mat):
    group = owner[mat % 5, 2 * pair + mat // 5]
    base = jnp.where(tab[group, 8] == 10 * pair + mat, 0, tab[group, 10])
    return MSG * group + base


def align_rows(src, dst):
    lane = lax.broadcasted_iota(jnp.int32, (ROWS, 128), 1)

    @pl.loop(0, PAIRS)
    def _(pair):
        for half in range(2):
            for kind in range(5):
                for j in range(TYPE_CHUNKS[kind]):
                    col = 1728 * half + 96 * TYPE_START[kind] + 128 * j
                    at, shift = divmod(col, 128)
                    valid = min(128, 96 * TYPE_TILES[kind] - 128 * j)
                    val = src[pl.ds(27 * pair + at, ROWS, stride=LINE), :]
                    if shift:
                        val = pltpu.roll(val, 128 - shift, 1)
                        if valid > 128 - shift:
                            nxt = src[pl.ds(27 * pair + at + 1, ROWS, stride=LINE), :]
                            nxt = pltpu.roll(nxt, 128 - shift, 1)
                            val = jnp.where(lane < 128 - shift, val, nxt)
                    if valid < 128:
                        val = jnp.where(lane < valid, val, 0.0)
                    dst[30 * pair + 15 * half + CHUNK_START[kind] + j] = val


def align_mats(src, dst):
    lane = lax.broadcasted_iota(jnp.int32, (ROWS, 128), 1)

    @pl.loop(0, 3)
    def _(step):
        for part in range(20):
            at, shift = divmod(96 * part, 128)
            val = src[pl.ds(15 * step + at, ROWS, stride=QLINE), :]
            if shift:
                val = pltpu.roll(val, 128 - shift, 1)
                if 96 > 128 - shift:
                    nxt = src[pl.ds(15 * step + at + 1, ROWS, stride=QLINE), :]
                    nxt = pltpu.roll(nxt, 128 - shift, 1)
                    val = jnp.where(lane < 128 - shift, val, nxt)
            dst[20 * step + part] = jnp.where(lane < 96, val, 0.0)


def split(x):
    high = x.astype(BF16)
    return high, (x - high.astype(F32)).astype(BF16)


NN = ((1,), (0,))
NT = ((1,), (1,))


def dot(a, b, dims):
    return lax.dot_general(a, b, (dims, ((), ())), preferred_element_type=F32)


def dot3(a, b):
    ah, al = a
    bh, bl = b
    wide = bh.shape[1]
    both = dot(ah, jnp.concatenate([bh, bl], axis=1), NN)
    return both[:, :wide] + (both[:, wide:] + dot(al, bh, NN))


def outer3(pieces):
    high, low = pieces
    wide = high.shape[0]
    both = dot(high, jnp.concatenate([high, low], axis=0), NT)
    mixed = both[:, wide:]
    return both[:, :wide] + (mixed + mixed.T)


def out_pieces():
    owner_of = []
    for half in range(2):
        for kind in range(5):
            start = 1728 * half + 96 * TYPE_START[kind]
            for c in range(96 * TYPE_TILES[kind]):
                owner_of.append((5 * half + kind, start))
    table = []
    for chunk in range(27):
        pieces = []
        for lane in range(128):
            col = 128 * chunk + lane
            mat, start = owner_of[col]
            j, src = divmod(col - start, 128)
            key = (mat, j, (lane - src) % 128)
            if pieces and pieces[-1][0] == key:
                pieces[-1][2] = lane + 1
            else:
                pieces.append([key, lane, lane + 1])
        table.append(pieces)
    return table


def unpack(back, place, write, first=0, last=PAIRS):
    lane = lax.broadcasted_iota(jnp.int32, (ROWS, 128), 1)
    table = out_pieces()

    @pl.loop(first, last)
    def _(pair):
        for chunk in range(27):
            out = None
            for (mat, j, turn), _lo, hi in reversed(table[chunk]):
                val = back[pl.ds(place[10 * pair + mat] + j, ROWS, stride=CAP), :]
                if turn:
                    val = pltpu.roll(val, turn, 1)
                out = val if out is None else jnp.where(lane < hi, val, out)
            write(pl.ds(27 * pair + chunk, ROWS, stride=LINE), out)


def main_kernel(
    owner_hbm,
    g_hbm,
    m_hbm,
    v_hbm,
    q_hbm,
    s_hbm,
    back_d,
    second_out,
    first_out,
    basis_out,
    gram_out,
    places_out,
    g2,
    m2,
    v2,
    q2,
    s2,
    lined,
    lined_q,
    lined_s,
    send_g,
    send_m,
    send_v,
    send_qs,
    recv_g,
    recv_m,
    recv_v,
    recv_qs,
    nat,
    qx,
    ret_d,
    ret_n,
    gram,
    xg,
    power,
    q_hi,
    q_lo,
    qt_hi,
    qt_lo,
    g_hat,
    m_hat,
    gram_strip,
    basis_strip,
    back_n,
    second2,
    owner,
    owners,
    tab_vec,
    tab,
    places,
    in_sem,
    send_sem,
    recv_sem,
    own_sem,
):
    me = lax.axis_index("shard")
    rank = lax.axis_index("tensor")
    my_y, my_z, my_c = me // 8, (me // 2) % 4, me % 2

    def peer(offset):
        dy, dz, dc = offset
        return ((my_y + dy) % 4) * 8 + ((my_z + dz) % 4) * 2 + (my_c + dc) % 2

    def local(src, dst, n):
        made = pltpu.make_async_copy(src, dst, in_sem.at[n])
        made.start()
        return made

    load_owner = local(owner_hbm, owner, 11)
    load_owners = local(owner_hbm, owners, 12)
    load_q = local(q_hbm.at[:, 0, :], q2, 0)
    load_s = local(s_hbm.at[:, 0, :], s2, 2)
    barrier = pltpu.get_barrier_semaphore()

    for offset in ORDER:
        pl.semaphore_signal(
            barrier, inc=1, device_id=(peer(offset), rank), device_id_type=MESH
        )

    for dx in range(1, N_TENSOR):
        pl.semaphore_signal(
            barrier, inc=1, device_id=(me, (rank + dx) % N_TENSOR), device_id_type=MESH
        )

    load_g = local(g_hbm, g2, 1)
    load_m = local(m_hbm, m2, 3)
    load_v = local(v_hbm, v2, 4)
    lined[ZERO_CHUNK] = jnp.zeros((ROWS, 128), F32)
    lined_q[ZERO_MAT] = jnp.zeros((ROWS, 128), F32)
    lined_s[ZERO_MAT] = jnp.zeros((ROWS, 128), F32)
    load_q.wait()
    align_mats(q2, lined_q)
    load_owner.wait()
    load_owners.wait()
    tab_vec[...] = table_of(owners[...])
    load_tab = local(tab_vec, tab, 5)

    def own_copy(send, recv, unit, off, rows, n):
        own = pl.ds(pl.multiple_of(me * unit + off, 8), rows)
        return pltpu.make_async_copy(send.at[own], recv.at[own], own_sem.at[n])

    def exchange(send, recv, unit, n, off=0, rows=None):
        rows = unit if rows is None else rows
        for offset in ORDER:
            dst = peer(offset)
            pltpu.make_async_remote_copy(
                src_ref=send.at[pl.ds(pl.multiple_of(dst * unit + off, 8), rows)],
                dst_ref=recv.at[pl.ds(pl.multiple_of(me * unit + off, 8), rows)],
                send_sem=send_sem.at[n],
                recv_sem=recv_sem.at[n],
                device_id=(dst, rank),
                device_id_type=MESH,
            ).start()
        own_copy(send, recv, unit, off, rows, n).start()

    def share(send, recv, rows, count, n):
        whole = pl.ds(0, count * rows)
        return pltpu.make_async_remote_copy(
            src_ref=send.at[whole],
            dst_ref=recv.at[whole],
            send_sem=send_sem.at[n],
            recv_sem=recv_sem.at[n],
            device_id=((me + 1) % N_SHARD, rank),
            device_id_type=MESH,
        )

    def exchange_done(send, recv, unit, n, off=0, rows=None):
        rows = unit if rows is None else rows
        own_copy(send, recv, unit, off, rows, n).wait()
        every = share(send, recv, rows, N_SHARD - 1, n)
        every.wait_send()
        every.wait_recv()

    def pack(lines, send):
        @pl.loop(0, N_SHARD)
        def _(d):
            for k in range(CAP):
                send[pl.ds(MSG * d + k, ROWS, stride=CAP), :] = lines[tab[d, k]]

    def mats_copy():
        return pltpu.make_async_copy(send_qs.at[me], recv_qs.at[me], own_sem.at[0])

    def pack_mats():
        lane = lax.broadcasted_iota(jnp.int32, (ROWS, 128), 1)

        @pl.loop(0, N_SHARD // 8)
        def _(step):
            held = []
            for n in range(8):
                one, two = tab[8 * step + n, 8], tab[8 * step + n, 9]
                held.append((lined_q[one], lined_q[two], lined_s[one], lined_s[two]))
            for n, (q_one, q_two, s_one, s_two) in enumerate(held):
                d = 8 * step + n
                q_two = pltpu.roll(q_two, 96, 1)
                s_one = pltpu.roll(s_one, 64, 1)
                s_two = pltpu.roll(s_two, 32, 1)
                send_qs[d, pl.ds(0, ROWS, stride=3), :] = jnp.where(lane < 96, q_one, q_two)
                send_qs[d, pl.ds(1, ROWS, stride=3), :] = jnp.where(lane < 64, q_two, s_one)
                send_qs[d, pl.ds(2, ROWS, stride=3), :] = jnp.where(lane < 32, s_one, s_two)

    load_s.wait()
    align_mats(s2, lined_s)
    load_tab.wait()
    pack_mats()
    pl.semaphore_wait(barrier, N_SHARD - 1 + N_TENSOR - 1)
    for offset in ORDER:
        dst = peer(offset)
        pltpu.make_async_remote_copy(
            src_ref=send_qs.at[dst],
            dst_ref=recv_qs.at[me],
            send_sem=send_sem.at[0],
            recv_sem=recv_sem.at[0],
            device_id=(dst, rank),
            device_id_type=MESH,
        ).start()
    mats_copy().start()

    load_g.wait()
    align_rows(g2, lined)
    pack(lined, send_g)
    exchange(send_g, recv_g, MSG, 1)

    load_m.wait()
    m2[...] = 0.9 * m2[...] + 0.1 * g2[...]
    save_first = local(m2, first_out, 7)
    align_rows(m2, lined)
    pack(lined, send_m)
    exchange(send_m, recv_m, MSG, 3)

    load_v.wait()
    align_rows(v2, lined)
    pack(lined, send_v)
    exchange(send_v, recv_v, MSG, 4, 0, HEAD)
    exchange(send_v, recv_v, MSG, 10, HEAD, TAIL)

    @pl.loop(0, PAIRS)
    def _(pair):
        for mat in range(10):
            places[10 * pair + mat] = place_of(owner, tab, pair, mat)

    save_places = local(places, places_out, 6)

    def spread(src_of, dst_of, n):
        for dx in range(1, N_TENSOR):
            other = (rank + dx) % N_TENSOR
            pltpu.make_async_remote_copy(
                src_ref=src_of(other),
                dst_ref=dst_of(rank),
                send_sem=send_sem.at[n],
                recv_sem=recv_sem.at[n],
                device_id=(me, other),
                device_id_type=MESH,
            ).start()

    def spread_done(three, n):
        every = pltpu.make_async_remote_copy(
            src_ref=three,
            dst_ref=three,
            send_sem=send_sem.at[n],
            recv_sem=recv_sem.at[n],
            device_id=(me, (rank + 1) % N_TENSOR),
            device_id_type=MESH,
        )
        every.wait_send()
        every.wait_recv()

    most = pl.ds(0, N_SHARD - 1)
    every_mat = pltpu.make_async_remote_copy(
        src_ref=send_qs.at[most],
        dst_ref=recv_qs.at[most],
        send_sem=send_sem.at[0],
        recv_sem=recv_sem.at[0],
        device_id=((me + 1) % N_SHARD, rank),
        device_id_type=MESH,
    )
    mats_copy().wait()
    every_mat.wait_send()
    every_mat.wait_recv()
    lane = lax.broadcasted_iota(jnp.int32, (D, 128), 1)
    lane_half = lax.broadcasted_iota(jnp.int32, (D // 2, 128), 1)
    for k in range(3):
        for s in range(0, N_SHARD, 2):
            pair = [recv_qs[s + n, pl.ds(k, ROWS, stride=3), :] for n in range(2)]
            into = jnp.concatenate(pair, axis=0)
            if k == 0:
                qx[rank, pl.ds(ROWS * s, 2 * ROWS), :] = into
            else:
                nat[k - 1, pl.ds(ROWS * s, 2 * ROWS), :] = into
    qx[rank, pl.ds(D, D // 2), :] = jnp.where(
        lane_half < 64, nat[0, : D // 2], pltpu.roll(nat[0, D // 2 :], 64, 1)
    )
    q_part = (lambda other: qx.at[rank]), (lambda other: qx.at[other])
    spread(*q_part, 5)

    exchange_done(send_g, recv_g, MSG, 1)
    c0 = tab[me, 10]
    for j in range(2):
        chunks = []
        for k in range(CAP):
            mine = (k < c0) if j == 0 else (k >= c0)
            chunks.append(split(jnp.where(mine, recv_g[pl.ds(k, D, stride=CAP), :], 0.0)))
        gram[j] = outer3(tuple(jnp.concatenate(half, axis=1) for half in zip(*chunks)))

    def strip(x):
        return pl.ds(pl.multiple_of(96 * x, 8), 96)

    g_part = (lambda other: gram.at[:, strip(other), :]), (lambda other: xg.at[other])
    spread(*g_part, 6)

    spread_done(qx.at[pl.ds(0, 3)], 5)
    for j in range(2):
        parts = [qx[x, :D] for x in range(4)]
        if j == 1:
            rests = [qx[x, D:] for x in range(4)]
            rests = [jnp.concatenate([r, pltpu.roll(r, 64, 1)], axis=0) for r in rests]
            parts = [
                pltpu.roll(jnp.where(lane >= 96, part, rest), 32, 1)
                for part, rest in zip(parts, rests)
            ]
        full = jnp.concatenate(
            [
                jnp.where(lane < 96, parts[0], pltpu.roll(parts[1], 96, 1)),
                jnp.where(lane < 64, pltpu.roll(parts[1], 96, 1), pltpu.roll(parts[2], 64, 1)),
                jnp.where(lane < 32, pltpu.roll(parts[2], 64, 1), pltpu.roll(parts[3], 32, 1)),
            ],
            axis=1,
        )
        q_hi[j], q_lo[j] = split(full)
        qt_hi[j], qt_lo[j] = split(full.T)

    exchange_done(send_m, recv_m, MSG, 3)

    @pl.loop(0, CAP)
    def _(k):
        sel = jnp.where(k >= c0, 1, 0)
        both = jnp.concatenate(
            [recv_g[pl.ds(k, D, stride=CAP), :], recv_m[pl.ds(k, D, stride=CAP), :]], axis=1
        )
        hat = dot3((qt_hi[sel], qt_lo[sel]), split(both))
        g_hat[pl.ds(k, D, stride=CAP), :] = hat[:, :128]
        m_hat[pl.ds(k, D, stride=CAP), :] = hat[:, 128:]

    spread_done(xg.at[pl.ds(0, 3)], 6)
    gram_parts = (
        pltpu.roll(jnp.where(lane >= 64, nat[0], nat[1]), 64, 1),
        pltpu.roll(nat[1], 96, 1),
    )
    for j in range(2):
        total = gram[j, strip(rank), :]
        for dx in range(1, N_TENSOR):
            total = total + xg[(rank + dx) % N_TENSOR, j]
        held = gram_parts[j].T[:96]
        fresh = 0.95 * held + 0.05 * total
        gram_strip[j] = fresh
        power[j, strip(rank), :] = dot3(split(fresh), (q_hi[j], q_lo[j]))
    p_part = (
        (lambda other: power.at[:, strip(rank), :]),
        (lambda other: power.at[:, strip(other), :]),
    )
    spread(*p_part, 7)

    for n, off, rows in ((4, 0, HEAD), (10, HEAD, TAIL)):
        exchange_done(send_v, recv_v, MSG, n, off, rows)

        @pl.loop(0, N_SHARD)
        def _(s):
            here = pl.ds(pl.multiple_of(MSG * s + off, 8), rows)
            rot = g_hat[here, :]
            ret_n[here, :] = 0.95 * recv_v[here, :] + 0.05 * rot * rot

        exchange(ret_n, back_n, MSG, 8 if off == 0 else 11, off, rows)

    @pl.loop(0, N_SHARD)
    def _(s):
        here = pl.ds(pl.multiple_of(MSG * s, 8), MSG)
        m_hat[here, :] = m_hat[here, :] / CORR_ONE / (jnp.sqrt(ret_n[here, :] / CORR_TWO) + 1e-08)

    @pl.loop(0, CAP)
    def _(k):
        sel = jnp.where(k >= c0, 1, 0)
        ret_d[pl.ds(k, D, stride=CAP), :] = dot3((q_hi[sel], q_lo[sel]), split(m_hat[pl.ds(k, D, stride=CAP), :]))

    exchange(ret_d, back_d, MSG, 9)

    spread_done(power.at[:, pl.ds(0, 288), :], 7)
    for j in range(2):
        full = power[j]
        norm = jnp.sqrt(jnp.sum(full * full, keepdims=True) + 1e-06)
        power[j] = full / norm

    @pl.loop(0, NS_STEPS - 1)
    def _(sweep):
        for j in range(2):
            frame = power[j]
            pieces = split(frame)
            power[j] = 1.5 * frame - 0.5 * dot3(split(outer3(pieces)), pieces)

    for j in range(2):
        gram[j] = power[j].T
        square = split(outer3(split(power[j])))
        mine = gram[j, strip(rank), :]
        basis_strip[j] = 1.5 * mine - 0.5 * dot3(split(mine), square)

    save_basis = local(basis_strip, basis_out, 8)
    save_gram = local(gram_strip, gram_out, 9)
    exchange_done(ret_n, back_n, MSG, 8, 0, HEAD)
    exchange_done(ret_n, back_n, MSG, 11, HEAD, TAIL)

    def write_second(here, val):
        second2[here, :] = val

    unpack(back_n, places, write_second)
    save_second = local(second2, second_out, 10)
    for save in (save_places, save_first, save_basis, save_gram, save_second):
        save.wait()
    exchange_done(ret_d, back_d, MSG, 9)


def unpack_kernel(
    places,
    back_d,
    w_hbm,
    second,
    first,
    basis,
    gram,
    bias_g,
    bias_w,
    bias_m,
    bias_v,
    weight_out,
    first_out,
    second_out,
    basis_out,
    gram_out,
    bias_w_out,
    bias_m_out,
    bias_v_out,
    place,
    dv,
    w2,
    n2,
    f2,
    b2,
    s2,
    bias,
    sem,
    sem_out,
):
    def copy(src, dst, n, sems=sem):
        made = pltpu.make_async_copy(src, dst, sems.at[n])
        made.start()
        return made

    load_p = copy(places, place, 0)
    load_d = copy(back_d, dv, 1)
    load_w = copy(w_hbm, w2, 2)
    loads = [
        copy(src, bias.at[n, 0], 3 + n) for n, src in enumerate((bias_g, bias_w, bias_m, bias_v))
    ]
    passed = []
    for n, (src, held, dst) in enumerate(
        (
            (second, n2, second_out),
            (first, f2, first_out),
            (basis, b2, basis_out),
            (gram, s2, gram_out),
        )
    ):
        passed.append((copy(src, held, 7 + n), held, dst))

    def write_weight(here, val):
        w = w2[here, :]
        w2[here, :] = w - 0.01 * (val + 0.1 * w)

    load_p.wait()
    load_d.wait()
    load_w.wait()
    unpack(dv, place, write_weight, 0, 1)
    saves = []
    for n, (load, held, dst) in enumerate(passed):
        load.wait()
        saves.append(copy(held, dst, 3 + n, sem_out))
    unpack(dv, place, write_weight, 1, PAIRS)
    saves.append(copy(w2, weight_out, 7, sem_out))
    for load in loads:
        load.wait()
    moment = 0.9 * bias[2] + 0.1 * bias[0]
    moment_two = 0.95 * bias[3] + 0.05 * bias[0] * bias[0]
    bias[5] = moment
    bias[6] = moment_two
    bias[4] = bias[1] - 0.01 * (moment / CORR_ONE / (jnp.sqrt(moment_two / CORR_TWO) + 1e-08))
    saves += [
        copy(bias.at[4 + n, 0], dst, n, sem_out)
        for n, dst in enumerate((bias_w_out, bias_m_out, bias_v_out))
    ]
    for save in saves:
        save.wait()


def body(
    gradient,
    weight,
    first_moment,
    second_moment,
    left_basis,
    left_gram,
    owner_table,
    bias_gradient,
    bias_weight,
    bias_first,
    bias_second,
):
    hbm = pl.BlockSpec(memory_space=pltpu.HBM)
    flat = (ROWS * LINE, 128)
    g, w, m, v = (a.reshape(flat) for a in (gradient, weight, first_moment, second_moment))
    wide = pltpu.VMEM((N_SHARD * MSG, 128), F32)
    mats = pltpu.VMEM((N_SHARD, QMSG, 128), F32)
    lines_q = pltpu.VMEM((ZERO_MAT + 1, ROWS, 128), F32)
    full = pltpu.VMEM((2, D, D), F32)
    half = pltpu.VMEM((2, D, D), BF16)
    strips = pltpu.VMEM((2, 96, D), F32)
    rows = pltpu.VMEM(flat, F32)
    rows_q = pltpu.VMEM((ROWS * QLINE, 128), F32)
    wide_out = jax.ShapeDtypeStruct((N_SHARD * MSG, 128), F32)
    flat_out = jax.ShapeDtypeStruct(flat, F32)
    strip_out = jax.ShapeDtypeStruct((2, 96, D), F32)
    tab_shape = (N_SHARD, 128)
    flat_q = (ROWS * QLINE, 1, 128)
    owner = owner_table.T
    back_d, second, first, basis, gram, places = pl.pallas_call(
        main_kernel,
        out_shape=(
            wide_out,
            flat_out,
            flat_out,
            strip_out,
            strip_out,
            jax.ShapeDtypeStruct((128,), jnp.int32),
        ),
        in_specs=[hbm] * 6,
        out_specs=(hbm,) * 6,
        scratch_shapes=[rows] * 3
        + [rows_q] * 2
        + [pltpu.VMEM((ZERO_CHUNK + 1, ROWS, 128), F32), lines_q, lines_q]
        + [wide] * 3
        + [mats]
        + [wide] * 3
        + [mats, pltpu.VMEM((2, D, 128), F32)]
        + [pltpu.VMEM((N_TENSOR, D + D // 2, 128), F32)]
        + [wide] * 2
        + [full, pltpu.VMEM((N_TENSOR, 2, 96, D), F32), full]
        + [half] * 4
        + [wide] * 2
        + [strips] * 2
        + [wide, rows]
        + [pltpu.SMEM(owner.shape, jnp.int32), pltpu.VMEM(owner.shape, jnp.int32)]
        + [pltpu.VMEM(tab_shape, jnp.int32), pltpu.SMEM(tab_shape, jnp.int32)]
        + [pltpu.SMEM((128,), jnp.int32)]
        + [pltpu.SemaphoreType.DMA((n,)) for n in (13, 12, 12, 12)],
        compiler_params=pltpu.CompilerParams(
            collective_id=0, has_side_effects=True, vmem_limit_bytes=VMEM_ALL
        ),
        name="exchange_and_rotate",
    )(owner, g, m, v, left_basis.reshape(flat_q), left_gram.reshape(flat_q))
    bias_out = jax.ShapeDtypeStruct(bias_gradient.shape, F32)
    outs = pl.pallas_call(
        unpack_kernel,
        out_shape=(flat_out,) * 3 + (strip_out,) * 2 + (bias_out,) * 3,
        in_specs=[hbm] * 11,
        out_specs=(hbm,) * 8,
        scratch_shapes=[pltpu.SMEM((128,), jnp.int32), wide]
        + [rows] * 3
        + [strips] * 2
        + [pltpu.VMEM((7, 1) + bias_gradient.shape, F32)]
        + [pltpu.SemaphoreType.DMA((11,)), pltpu.SemaphoreType.DMA((8,))],
        compiler_params=pltpu.CompilerParams(vmem_limit_bytes=VMEM_ALL),
        name="unpack",
    )(
        places,
        back_d,
        w,
        second,
        first,
        basis,
        gram,
        bias_gradient,
        bias_weight,
        bias_first,
        bias_second,
    )
    weight_new, first_new, second_new, basis_new, gram_new = outs[:5]
    return (
        weight_new.reshape(weight.shape),
        first_new.reshape(weight.shape),
        second_new.reshape(weight.shape),
        basis_new.transpose(0, 2, 1)[None],
        gram_new.transpose(0, 2, 1)[None],
        *outs[5:],
    )


def solution(mesh):
    rows = P("shard", "tensor", None)
    flat = P(("shard", "tensor"))
    owned = P("shard", None, None, "tensor")
    return jax.shard_map(
        body,
        mesh=mesh,
        in_specs=(rows,) * 6 + (P(),) + (flat,) * 4,
        out_specs=(rows,) * 3 + (owned,) * 2 + (flat,) * 3,
        check_vma=False,
    )
```

```python
import functools

import jax
import jax.numpy as jnp
from jax import lax
from jax.experimental import pallas as pl
from jax.experimental.pallas import tpu as pltpu
from jax.sharding import PartitionSpec as P

MESH = pl.DeviceIdType.MESH
STEP = 10
NS_STEPS = 5
N_SHARD = 32
N_TENSOR = 4
D = 384
ROWS = 12
PAIRS = 6
TYPE_TILES = (3, 1, 4, 4, 6)
TYPE_START = (0, 3, 4, 8, 12)
TYPE_CHUNKS = (3, 1, 3, 3, 5)
CHUNK_START = (0, 3, 4, 7, 10)
CAP = 6
MSG = ROWS * CAP
QMSG = ROWS * 3
LINE = 162
QLINE = 45
ZERO_CHUNK = 180
ZERO_MAT = 60
CORR_ONE = 1.0 - 0.9**STEP
CORR_TWO = 1.0 - 0.95**STEP
NO_CODE = (ZERO_MAT << 16) + (ZERO_CHUNK << 8)
HEAD = 48
TAIL = 24
VMEM_ALL = 67043328
F32 = jnp.float32


def send_order():
    rings = (
        ((2, 2),),
        ((1, 2), (2, 1), (3, 2), (2, 3)),
        ((1, 1), (3, 3), (1, 3), (3, 1)),
        ((2, 0), (0, 2)),
        ((1, 0), (0, 1), (3, 0), (0, 3)),
    )
    order = [(dy, dz, dc) for ring in rings for dc in range(2) for dy, dz in ring]
    return order + [(0, 0, 1)]


ORDER = send_order()
BF16 = jnp.bfloat16


def table_of(owners):
    group = lax.broadcasted_iota(jnp.int32, (N_SHARD, 12), 0)
    layer = lax.broadcasted_iota(jnp.int32, (N_SHARD, 12), 1)
    low = jnp.full((N_SHARD, 12), NO_CODE, jnp.int32)
    high = jnp.full((N_SHARD, 12), -1, jnp.int32)
    for kind in range(5):
        code = ((5 * layer + kind) << 16) + ((15 * layer + CHUNK_START[kind]) << 8)
        code = code + TYPE_CHUNKS[kind]
        hit = owners[kind : kind + 1, :] == group
        low = jnp.minimum(low, jnp.where(hit, code, NO_CODE))
        high = jnp.maximum(high, jnp.where(hit, code, -1))
    first = jnp.min(low, axis=1, keepdims=True)
    second = jnp.max(high, axis=1, keepdims=True)
    second = jnp.where((second < 0) | (second == first), NO_CODE, second)
    c0, c1 = first & 255, second & 255
    at0, at1 = (first >> 8) & 255, (second >> 8) & 255
    k = lax.broadcasted_iota(jnp.int32, (N_SHARD, 128), 1)
    rest = jnp.where(k - c0 < c1, at1 + k - c0, ZERO_CHUNK)
    table = jnp.where(k < c0, at0 + k, rest)
    table = jnp.where(k == 8, first >> 16, table)
    table = jnp.where(k == 9, second >> 16, table)
    return jnp.where(k == 10, c0, table)


def place_of(owner, tab, pair, mat):
    group = owner[mat % 5, 2 * pair + mat // 5]
    base = jnp.where(tab[group, 8] == 10 * pair + mat, 0, tab[group, 10])
    return MSG * group + base


def align_rows(src, dst):
    lane = lax.broadcasted_iota(jnp.int32, (ROWS, 128), 1)

    @pl.loop(0, PAIRS)
    def _(pair):
        for half in range(2):
            for kind in range(5):
                for j in range(TYPE_CHUNKS[kind]):
                    col = 1728 * half + 96 * TYPE_START[kind] + 128 * j
                    at, shift = divmod(col, 128)
                    valid = min(128, 96 * TYPE_TILES[kind] - 128 * j)
                    val = src[pl.ds(27 * pair + at, ROWS, stride=LINE), :]
                    if shift:
                        val = pltpu.roll(val, 128 - shift, 1)
                        if valid > 128 - shift:
                            nxt = src[pl.ds(27 * pair + at + 1, ROWS, stride=LINE), :]
                            nxt = pltpu.roll(nxt, 128 - shift, 1)
                            val = jnp.where(lane < 128 - shift, val, nxt)
                    if valid < 128:
                        val = jnp.where(lane < valid, val, 0.0)
                    dst[30 * pair + 15 * half + CHUNK_START[kind] + j] = val


def align_mats(src, dst):
    lane = lax.broadcasted_iota(jnp.int32, (ROWS, 128), 1)

    @pl.loop(0, 3)
    def _(step):
        for part in range(20):
            at, shift = divmod(96 * part, 128)
            val = src[pl.ds(15 * step + at, ROWS, stride=QLINE), :]
            if shift:
                val = pltpu.roll(val, 128 - shift, 1)
                if 96 > 128 - shift:
                    nxt = src[pl.ds(15 * step + at + 1, ROWS, stride=QLINE), :]
                    nxt = pltpu.roll(nxt, 128 - shift, 1)
                    val = jnp.where(lane < 128 - shift, val, nxt)
            dst[20 * step + part] = jnp.where(lane < 96, val, 0.0)


def split(x):
    high = x.astype(BF16)
    return high, (x - high.astype(F32)).astype(BF16)


def dot3(a, b, dims):
    ah, al = a
    bh, bl = b
    dot = functools.partial(
        lax.dot_general, dimension_numbers=(dims, ((), ())), preferred_element_type=F32
    )
    return dot(ah, bh) + (dot(ah, bl) + dot(al, bh))


NN = ((1,), (0,))
NT = ((1,), (1,))


def outer3(pieces):
    high, low = pieces
    dot = functools.partial(
        lax.dot_general, dimension_numbers=(NT, ((), ())), preferred_element_type=F32
    )
    mixed = dot(high, low)
    return dot(high, high) + (mixed + mixed.T)


def out_pieces():
    owner_of = []
    for half in range(2):
        for kind in range(5):
            start = 1728 * half + 96 * TYPE_START[kind]
            for c in range(96 * TYPE_TILES[kind]):
                owner_of.append((5 * half + kind, start))
    table = []
    for chunk in range(27):
        pieces = []
        for lane in range(128):
            col = 128 * chunk + lane
            mat, start = owner_of[col]
            j, src = divmod(col - start, 128)
            key = (mat, j, (lane - src) % 128)
            if pieces and pieces[-1][0] == key:
                pieces[-1][2] = lane + 1
            else:
                pieces.append([key, lane, lane + 1])
        table.append(pieces)
    return table


def unpack(back, place, write, first=0, last=PAIRS):
    lane = lax.broadcasted_iota(jnp.int32, (ROWS, 128), 1)
    table = out_pieces()

    @pl.loop(first, last)
    def _(pair):
        for chunk in range(27):
            out = None
            for (mat, j, turn), _lo, hi in reversed(table[chunk]):
                val = back[pl.ds(place[10 * pair + mat] + j, ROWS, stride=CAP), :]
                if turn:
                    val = pltpu.roll(val, turn, 1)
                out = val if out is None else jnp.where(lane < hi, val, out)
            write(pl.ds(27 * pair + chunk, ROWS, stride=LINE), out)


def main_kernel(
    owner_hbm,
    g_hbm,
    m_hbm,
    v_hbm,
    q_hbm,
    s_hbm,
    back_d,
    second_out,
    first_out,
    basis_out,
    gram_out,
    places_out,
    g2,
    m2,
    v2,
    q2,
    s2,
    lined,
    lined_q,
    lined_s,
    send_g,
    send_m,
    send_v,
    send_qs,
    recv_g,
    recv_m,
    recv_v,
    recv_qs,
    nat,
    qx,
    ret_d,
    ret_n,
    gram,
    xg,
    power,
    q_hi,
    q_lo,
    qt_hi,
    qt_lo,
    g_hat,
    m_hat,
    gram_strip,
    basis_strip,
    back_n,
    second2,
    owner,
    owners,
    tab_vec,
    tab,
    places,
    in_sem,
    send_sem,
    recv_sem,
    own_sem,
):
    me = lax.axis_index("shard")
    rank = lax.axis_index("tensor")
    my_y, my_z, my_c = me // 8, (me // 2) % 4, me % 2

    def peer(offset):
        dy, dz, dc = offset
        return ((my_y + dy) % 4) * 8 + ((my_z + dz) % 4) * 2 + (my_c + dc) % 2

    def local(src, dst, n):
        made = pltpu.make_async_copy(src, dst, in_sem.at[n])
        made.start()
        return made

    load_owner = local(owner_hbm, owner, 11)
    load_owners = local(owner_hbm, owners, 12)
    load_q = local(q_hbm.at[:, 0, :], q2, 0)
    load_s = local(s_hbm.at[:, 0, :], s2, 2)
    barrier = pltpu.get_barrier_semaphore()

    for offset in ORDER:
        pl.semaphore_signal(
            barrier, inc=1, device_id=(peer(offset), rank), device_id_type=MESH
        )

    for dx in range(1, N_TENSOR):
        pl.semaphore_signal(
            barrier, inc=1, device_id=(me, (rank + dx) % N_TENSOR), device_id_type=MESH
        )

    load_g = local(g_hbm, g2, 1)
    load_m = local(m_hbm, m2, 3)
    load_v = local(v_hbm, v2, 4)
    load_owner.wait()
    load_owners.wait()
    tab_vec[...] = table_of(owners[...])
    load_tab = local(tab_vec, tab, 5)

    lined[ZERO_CHUNK] = jnp.zeros((ROWS, 128), F32)
    lined_q[ZERO_MAT] = jnp.zeros((ROWS, 128), F32)
    lined_s[ZERO_MAT] = jnp.zeros((ROWS, 128), F32)

    def own_copy(send, recv, unit, off, rows, n):
        own = pl.ds(pl.multiple_of(me * unit + off, 8), rows)
        return pltpu.make_async_copy(send.at[own], recv.at[own], own_sem.at[n])

    def exchange(send, recv, unit, n, off=0, rows=None):
        rows = unit if rows is None else rows
        for offset in ORDER:
            dst = peer(offset)
            pltpu.make_async_remote_copy(
                src_ref=send.at[pl.ds(pl.multiple_of(dst * unit + off, 8), rows)],
                dst_ref=recv.at[pl.ds(pl.multiple_of(me * unit + off, 8), rows)],
                send_sem=send_sem.at[n],
                recv_sem=recv_sem.at[n],
                device_id=(dst, rank),
                device_id_type=MESH,
            ).start()
        own_copy(send, recv, unit, off, rows, n).start()

    def share(send, recv, rows, count, n):
        whole = pl.ds(0, count * rows)
        return pltpu.make_async_remote_copy(
            src_ref=send.at[whole],
            dst_ref=recv.at[whole],
            send_sem=send_sem.at[n],
            recv_sem=recv_sem.at[n],
            device_id=((me + 1) % N_SHARD, rank),
            device_id_type=MESH,
        )

    def exchange_done(send, recv, unit, n, off=0, rows=None):
        rows = unit if rows is None else rows
        own_copy(send, recv, unit, off, rows, n).wait()
        every = share(send, recv, rows, N_SHARD - 1, n)
        every.wait_send()
        every.wait_recv()

    def pack(lines, send):
        @pl.loop(0, N_SHARD)
        def _(d):
            for k in range(CAP):
                send[pl.ds(MSG * d + k, ROWS, stride=CAP), :] = lines[tab[d, k]]

    def mats_copy():
        return pltpu.make_async_copy(send_qs.at[me], recv_qs.at[me], own_sem.at[0])

    def pack_mats():
        lane = lax.broadcasted_iota(jnp.int32, (ROWS, 128), 1)

        @pl.loop(0, N_SHARD // 8)
        def _(step):
            held = []
            for n in range(8):
                one, two = tab[8 * step + n, 8], tab[8 * step + n, 9]
                held.append((lined_q[one], lined_q[two], lined_s[one], lined_s[two]))
            for n, (q_one, q_two, s_one, s_two) in enumerate(held):
                d = 8 * step + n
                q_two = pltpu.roll(q_two, 96, 1)
                s_one = pltpu.roll(s_one, 64, 1)
                s_two = pltpu.roll(s_two, 32, 1)
                send_qs[d, pl.ds(0, ROWS, stride=3), :] = jnp.where(lane < 96, q_one, q_two)
                send_qs[d, pl.ds(1, ROWS, stride=3), :] = jnp.where(lane < 64, q_two, s_one)
                send_qs[d, pl.ds(2, ROWS, stride=3), :] = jnp.where(lane < 32, s_one, s_two)

    load_q.wait()
    align_mats(q2, lined_q)
    load_s.wait()
    align_mats(s2, lined_s)
    load_tab.wait()
    pack_mats()
    pl.semaphore_wait(barrier, N_SHARD - 1 + N_TENSOR - 1)
    for offset in ORDER:
        dst = peer(offset)
        pltpu.make_async_remote_copy(
            src_ref=send_qs.at[dst],
            dst_ref=recv_qs.at[me],
            send_sem=send_sem.at[0],
            recv_sem=recv_sem.at[0],
            device_id=(dst, rank),
            device_id_type=MESH,
        ).start()
    mats_copy().start()

    load_g.wait()
    align_rows(g2, lined)
    pack(lined, send_g)
    exchange(send_g, recv_g, MSG, 1)

    load_m.wait()
    m2[...] = 0.9 * m2[...] + 0.1 * g2[...]
    save_first = local(m2, first_out, 7)
    align_rows(m2, lined)
    pack(lined, send_m)
    exchange(send_m, recv_m, MSG, 3)

    load_v.wait()
    align_rows(v2, lined)
    pack(lined, send_v)
    exchange(send_v, recv_v, MSG, 4, 0, HEAD)
    exchange(send_v, recv_v, MSG, 10, HEAD, TAIL)

    @pl.loop(0, PAIRS)
    def _(pair):
        for mat in range(10):
            places[10 * pair + mat] = place_of(owner, tab, pair, mat)

    save_places = local(places, places_out, 6)

    def spread(src_of, dst_of, n):
        for dx in range(1, N_TENSOR):
            other = (rank + dx) % N_TENSOR
            pltpu.make_async_remote_copy(
                src_ref=src_of(other),
                dst_ref=dst_of(rank),
                send_sem=send_sem.at[n],
                recv_sem=recv_sem.at[n],
                device_id=(me, other),
                device_id_type=MESH,
            ).start()

    def spread_done(three, n):
        every = pltpu.make_async_remote_copy(
            src_ref=three,
            dst_ref=three,
            send_sem=send_sem.at[n],
            recv_sem=recv_sem.at[n],
            device_id=(me, (rank + 1) % N_TENSOR),
            device_id_type=MESH,
        )
        every.wait_send()
        every.wait_recv()

    most = pl.ds(0, N_SHARD - 1)
    every_mat = pltpu.make_async_remote_copy(
        src_ref=send_qs.at[most],
        dst_ref=recv_qs.at[most],
        send_sem=send_sem.at[0],
        recv_sem=recv_sem.at[0],
        device_id=((me + 1) % N_SHARD, rank),
        device_id_type=MESH,
    )
    mats_copy().wait()
    every_mat.wait_send()
    every_mat.wait_recv()
    lane = lax.broadcasted_iota(jnp.int32, (D, 128), 1)
    lane_half = lax.broadcasted_iota(jnp.int32, (D // 2, 128), 1)
    for k in range(3):
        for s in range(0, N_SHARD, 2):
            pair = [recv_qs[s + n, pl.ds(k, ROWS, stride=3), :] for n in range(2)]
            into = jnp.concatenate(pair, axis=0)
            if k == 0:
                qx[rank, pl.ds(ROWS * s, 2 * ROWS), :] = into
            else:
                nat[k - 1, pl.ds(ROWS * s, 2 * ROWS), :] = into
    qx[rank, pl.ds(D, D // 2), :] = jnp.where(
        lane_half < 64, nat[0, : D // 2], pltpu.roll(nat[0, D // 2 :], 64, 1)
    )
    q_part = (lambda other: qx.at[rank]), (lambda other: qx.at[other])
    spread(*q_part, 5)

    exchange_done(send_g, recv_g, MSG, 1)
    c0 = tab[me, 10]
    for j in range(2):
        chunks = []
        for k in range(CAP):
            mine = (k < c0) if j == 0 else (k >= c0)
            chunks.append(split(jnp.where(mine, recv_g[pl.ds(k, D, stride=CAP), :], 0.0)))
        gram[j] = outer3(tuple(jnp.concatenate(half, axis=1) for half in zip(*chunks)))

    def strip(x):
        return pl.ds(pl.multiple_of(96 * x, 8), 96)

    g_part = (lambda other: gram.at[:, strip(other), :]), (lambda other: xg.at[other])
    spread(*g_part, 6)

    spread_done(qx.at[pl.ds(0, 3)], 5)
    for j in range(2):
        parts = [qx[x, :D] for x in range(4)]
        if j == 1:
            rests = [qx[x, D:] for x in range(4)]
            rests = [jnp.concatenate([r, pltpu.roll(r, 64, 1)], axis=0) for r in rests]
            parts = [
                pltpu.roll(jnp.where(lane >= 96, part, rest), 32, 1)
                for part, rest in zip(parts, rests)
            ]
        full = jnp.concatenate(
            [
                jnp.where(lane < 96, parts[0], pltpu.roll(parts[1], 96, 1)),
                jnp.where(lane < 64, pltpu.roll(parts[1], 96, 1), pltpu.roll(parts[2], 64, 1)),
                jnp.where(lane < 32, pltpu.roll(parts[2], 64, 1), pltpu.roll(parts[3], 32, 1)),
            ],
            axis=1,
        )
        q_hi[j], q_lo[j] = split(full)
        qt_hi[j], qt_lo[j] = split(full.T)

    exchange_done(send_m, recv_m, MSG, 3)

    @pl.loop(0, CAP)
    def _(k):
        sel = jnp.where(k >= c0, 1, 0)
        both = jnp.concatenate(
            [recv_g[pl.ds(k, D, stride=CAP), :], recv_m[pl.ds(k, D, stride=CAP), :]], axis=1
        )
        hat = dot3((qt_hi[sel], qt_lo[sel]), split(both), NN)
        g_hat[pl.ds(k, D, stride=CAP), :] = hat[:, :128]
        m_hat[pl.ds(k, D, stride=CAP), :] = hat[:, 128:]

    spread_done(xg.at[pl.ds(0, 3)], 6)
    gram_parts = (
        pltpu.roll(jnp.where(lane >= 64, nat[0], nat[1]), 64, 1),
        pltpu.roll(nat[1], 96, 1),
    )
    for j in range(2):
        total = gram[j, strip(rank), :]
        for dx in range(1, N_TENSOR):
            total = total + xg[(rank + dx) % N_TENSOR, j]
        held = gram_parts[j].T[:96]
        fresh = 0.95 * held + 0.05 * total
        gram_strip[j] = fresh
        power[j, strip(rank), :] = dot3(split(fresh), (q_hi[j], q_lo[j]), NN)
    p_part = (
        (lambda other: power.at[:, strip(rank), :]),
        (lambda other: power.at[:, strip(other), :]),
    )
    spread(*p_part, 7)

    for n, off, rows in ((4, 0, HEAD), (10, HEAD, TAIL)):
        exchange_done(send_v, recv_v, MSG, n, off, rows)

        @pl.loop(0, N_SHARD)
        def _(s):
            here = pl.ds(pl.multiple_of(MSG * s + off, 8), rows)
            rot = g_hat[here, :]
            ret_n[here, :] = 0.95 * recv_v[here, :] + 0.05 * rot * rot

        exchange(ret_n, back_n, MSG, 8 if off == 0 else 11, off, rows)

    @pl.loop(0, N_SHARD)
    def _(s):
        here = pl.ds(pl.multiple_of(MSG * s, 8), MSG)
        m_hat[here, :] = m_hat[here, :] / CORR_ONE / (jnp.sqrt(ret_n[here, :] / CORR_TWO) + 1e-08)

    @pl.loop(0, CAP)
    def _(k):
        sel = jnp.where(k >= c0, 1, 0)
        ret_d[pl.ds(k, D, stride=CAP), :] = dot3((q_hi[sel], q_lo[sel]), split(m_hat[pl.ds(k, D, stride=CAP), :]), NN)

    exchange(ret_d, back_d, MSG, 9)

    spread_done(power.at[:, pl.ds(0, 288), :], 7)
    for j in range(2):
        full = power[j]
        norm = jnp.sqrt(jnp.sum(full * full, keepdims=True) + 1e-06)
        power[j] = full / norm

    @pl.loop(0, NS_STEPS - 1)
    def _(sweep):
        for j in range(2):
            frame = power[j]
            pieces = split(frame)
            power[j] = 1.5 * frame - 0.5 * dot3(split(outer3(pieces)), pieces, NN)

    exchange_done(ret_n, back_n, MSG, 8, 0, HEAD)
    exchange_done(ret_n, back_n, MSG, 11, HEAD, TAIL)

    def write_second(here, val):
        second2[here, :] = val

    unpack(back_n, places, write_second)
    save_second = local(second2, second_out, 10)
    for j in range(2):
        gram[j] = power[j].T
        square = split(outer3(split(power[j])))
        mine = gram[j, strip(rank), :]
        basis_strip[j] = 1.5 * mine - 0.5 * dot3(split(mine), square, NN)

    save_basis = local(basis_strip, basis_out, 8)
    save_gram = local(gram_strip, gram_out, 9)
    exchange_done(ret_d, back_d, MSG, 9)
    for save in (save_places, save_first, save_basis, save_gram, save_second):
        save.wait()


def unpack_kernel(
    places,
    back_d,
    w_hbm,
    second,
    first,
    basis,
    gram,
    bias_g,
    bias_w,
    bias_m,
    bias_v,
    weight_out,
    first_out,
    second_out,
    basis_out,
    gram_out,
    bias_w_out,
    bias_m_out,
    bias_v_out,
    place,
    dv,
    w2,
    n2,
    f2,
    b2,
    s2,
    bias,
    sem,
    sem_out,
):
    def copy(src, dst, n, sems=sem):
        made = pltpu.make_async_copy(src, dst, sems.at[n])
        made.start()
        return made

    load_p = copy(places, place, 0)
    load_d = copy(back_d, dv, 1)
    load_w = copy(w_hbm, w2, 2)
    loads = [
        copy(src, bias.at[n, 0], 3 + n) for n, src in enumerate((bias_g, bias_w, bias_m, bias_v))
    ]
    passed = []
    for n, (src, held, dst) in enumerate(
        (
            (second, n2, second_out),
            (first, f2, first_out),
            (basis, b2, basis_out),
            (gram, s2, gram_out),
        )
    ):
        passed.append((copy(src, held, 7 + n), held, dst))

    def write_weight(here, val):
        w = w2[here, :]
        w2[here, :] = w - 0.01 * (val + 0.1 * w)

    load_p.wait()
    load_d.wait()
    load_w.wait()
    unpack(dv, place, write_weight, 0, PAIRS // 2)
    for load in loads:
        load.wait()
    moment = 0.9 * bias[2] + 0.1 * bias[0]
    moment_two = 0.95 * bias[3] + 0.05 * bias[0] * bias[0]
    bias[5] = moment
    bias[6] = moment_two
    bias[4] = bias[1] - 0.01 * (moment / CORR_ONE / (jnp.sqrt(moment_two / CORR_TWO) + 1e-08))
    saves = [
        copy(bias.at[4 + n, 0], dst, n, sem_out)
        for n, dst in enumerate((bias_w_out, bias_m_out, bias_v_out))
    ]
    for n, (load, held, dst) in enumerate(passed):
        load.wait()
        saves.append(copy(held, dst, 3 + n, sem_out))
    unpack(dv, place, write_weight, PAIRS // 2, PAIRS)
    saves.append(copy(w2, weight_out, 7, sem_out))
    for save in saves:
        save.wait()


def body(
    gradient,
    weight,
    first_moment,
    second_moment,
    left_basis,
    left_gram,
    owner_table,
    bias_gradient,
    bias_weight,
    bias_first,
    bias_second,
):
    hbm = pl.BlockSpec(memory_space=pltpu.HBM)
    flat = (ROWS * LINE, 128)
    g, w, m, v = (a.reshape(flat) for a in (gradient, weight, first_moment, second_moment))
    wide = pltpu.VMEM((N_SHARD * MSG, 128), F32)
    mats = pltpu.VMEM((N_SHARD, QMSG, 128), F32)
    lines_q = pltpu.VMEM((ZERO_MAT + 1, ROWS, 128), F32)
    full = pltpu.VMEM((2, D, D), F32)
    half = pltpu.VMEM((2, D, D), BF16)
    strips = pltpu.VMEM((2, 96, D), F32)
    rows = pltpu.VMEM(flat, F32)
    rows_q = pltpu.VMEM((ROWS * QLINE, 128), F32)
    wide_out = jax.ShapeDtypeStruct((N_SHARD * MSG, 128), F32)
    flat_out = jax.ShapeDtypeStruct(flat, F32)
    strip_out = jax.ShapeDtypeStruct((2, 96, D), F32)
    tab_shape = (N_SHARD, 128)
    flat_q = (ROWS * QLINE, 1, 128)
    owner = owner_table.T
    back_d, second, first, basis, gram, places = pl.pallas_call(
        main_kernel,
        out_shape=(
            wide_out,
            flat_out,
            flat_out,
            strip_out,
            strip_out,
            jax.ShapeDtypeStruct((128,), jnp.int32),
        ),
        in_specs=[hbm] * 6,
        out_specs=(hbm,) * 6,
        scratch_shapes=[rows] * 3
        + [rows_q] * 2
        + [pltpu.VMEM((ZERO_CHUNK + 1, ROWS, 128), F32), lines_q, lines_q]
        + [wide] * 3
        + [mats]
        + [wide] * 3
        + [mats, pltpu.VMEM((2, D, 128), F32)]
        + [pltpu.VMEM((N_TENSOR, D + D // 2, 128), F32)]
        + [wide] * 2
        + [full, pltpu.VMEM((N_TENSOR, 2, 96, D), F32), full]
        + [half] * 4
        + [wide] * 2
        + [strips] * 2
        + [wide, rows]
        + [pltpu.SMEM(owner.shape, jnp.int32), pltpu.VMEM(owner.shape, jnp.int32)]
        + [pltpu.VMEM(tab_shape, jnp.int32), pltpu.SMEM(tab_shape, jnp.int32)]
        + [pltpu.SMEM((128,), jnp.int32)]
        + [pltpu.SemaphoreType.DMA((n,)) for n in (13, 12, 12, 12)],
        compiler_params=pltpu.CompilerParams(
            collective_id=0, has_side_effects=True, vmem_limit_bytes=VMEM_ALL
        ),
        name="exchange_and_rotate",
    )(owner, g, m, v, left_basis.reshape(flat_q), left_gram.reshape(flat_q))
    bias_out = jax.ShapeDtypeStruct(bias_gradient.shape, F32)
    outs = pl.pallas_call(
        unpack_kernel,
        out_shape=(flat_out,) * 3 + (strip_out,) * 2 + (bias_out,) * 3,
        in_specs=[hbm] * 11,
        out_specs=(hbm,) * 8,
        scratch_shapes=[pltpu.SMEM((128,), jnp.int32), wide]
        + [rows] * 3
        + [strips] * 2
        + [pltpu.VMEM((7, 1) + bias_gradient.shape, F32)]
        + [pltpu.SemaphoreType.DMA((11,)), pltpu.SemaphoreType.DMA((8,))],
        compiler_params=pltpu.CompilerParams(vmem_limit_bytes=VMEM_ALL),
        name="unpack",
    )(
        places,
        back_d,
        w,
        second,
        first,
        basis,
        gram,
        bias_gradient,
        bias_weight,
        bias_first,
        bias_second,
    )
    weight_new, first_new, second_new, basis_new, gram_new = outs[:5]
    return (
        weight_new.reshape(weight.shape),
        first_new.reshape(weight.shape),
        second_new.reshape(weight.shape),
        basis_new.transpose(0, 2, 1)[None],
        gram_new.transpose(0, 2, 1)[None],
        *outs[5:],
    )


def solution(mesh):
    rows = P("shard", "tensor", None)
    flat = P(("shard", "tensor"))
    owned = P("shard", None, None, "tensor")
    return jax.shard_map(
        body,
        mesh=mesh,
        in_specs=(rows,) * 6 + (P(),) + (flat,) * 4,
        out_specs=(rows,) * 3 + (owned,) * 2 + (flat,) * 3,
        check_vma=False,
    )
```
